512 devices in a mesh: gx: 16 (over z), gy: 4 (over x), gz: 8 (over y, core).
Axes of the slice: x: 4, y: 4, z: 16, core: 2. Of those that a mesh axis runs over, the one named last changes fastest.
Arguments:
- targets: float32 [3, 524288], P(None, ('gx', 'gy', 'gz')), may hold values from -20 to 20
- sources: float32 [65536, 4, 256], P(('gx', 'gy', 'gz')), may hold values from -20 to 20, as said below
- send_ids: int32 [512, 128, 2], P(('gx', 'gy', 'gz')), may hold values from 0 to 127, as said below
- send_count: int32 [512, 128], P(('gx', 'gy', 'gz')), may hold values from 0 to 2
- far_ids: int32 [4096, 64], P(('gx', 'gy', 'gz')), may hold values from 0 to 65535
- near_ids: int32 [4096, 8], P(('gx', 'gy', 'gz')), may hold values from 0 to 383, as said below
- near_count: int32 [4096], P(('gx', 'gy', 'gz')), may hold values from 1 to 8
Outputs:
- potential: float32 [524288], P(('gx', 'gy', 'gz'))
The draws below stay inside these ranges and needn't reach their ends.
Inputs may be any that keep to these rules, and one draw needn't show every extreme that they name: `sources`: coordinates of rows 0 to 2; masses in row 3 lie between 0.0002 and 0.002. send_ids of a domain name its own buckets, counted from 0. `near_ids`: entries may name empty slots; the live entries of every near list include a filled slot received from a peer.
All inputs are finite; a program needn't handle non-finite values.
Results may differ from the reference program's by a relative error of at most 0.0003.
Values sent between devices are 32-bit elements; how exact they have to be, the bound alone decides.
A program may use at most 128 MiB of HBM per device.

```python
import jax
import jax.numpy as jnp
from jax import lax

BS = 256
TBS = 128
TB_DEV = 8
SB_DEV = 128
LIST_C = 64
LIST_P = 8
SLOTS = 2
GROUP = 128
TILES = 384
SBUCKETS = 65536
TBUCKETS = 4096
TPART = 524288
N_GX = 16
N_GY = 4
N_GZ = 8


def geometry(key):
    key_centre, key_spread, key_offset, key_mass = jax.random.split(jax.random.fold_in(key, 7), 4)
    centre = jnp.clip(3.0 * jax.random.normal(key_centre, (SBUCKETS, 3, 1), jnp.float32), -12.0, 12.0)
    spread = jnp.exp(jax.random.uniform(key_spread, (SBUCKETS, 3, 1), jnp.float32, jnp.log(0.2), jnp.log(2.0)))
    return (centre, spread, key_offset, key_mass)


def routing(key):
    streams = jax.random.split(jax.random.fold_in(key, 11), 7)
    domains = N_GX * N_GY * N_GZ
    sent_buckets = jax.random.randint(streams[0], (domains, GROUP, SLOTS), 0, SB_DEV, jnp.int32)
    base_count = jax.random.randint(streams[1], (domains, GROUP), 0, SLOTS + 1, jnp.int32)
    bucket_index = jnp.arange(TBUCKETS, dtype=jnp.int32)
    domain = bucket_index // TB_DEV
    index_x = domain // (N_GY * N_GZ)
    index_y = domain // N_GZ % N_GY
    index_z = domain % N_GZ
    own_rank = index_x * N_GZ + index_z
    anchor_rank = jax.random.randint(streams[2], (TBUCKETS,), 0, GROUP, jnp.int32)
    partner = anchor_rank // N_GZ * (N_GY * N_GZ) + index_y * N_GZ + anchor_rank % N_GZ
    filled_count = base_count.at[partner, own_rank].max(jnp.ones((TBUCKETS,), jnp.int32))
    anchor_filled = filled_count[partner, own_rank]
    anchor_slot = jax.random.randint(streams[3], (TBUCKETS,), 0, anchor_filled, jnp.int32)
    live_count = jax.random.randint(streams[4], (TBUCKETS,), 1, LIST_P + 1, jnp.int32)
    listed = jax.random.randint(streams[5], (TBUCKETS, LIST_P), 0, TILES, jnp.int32)
    anchor_place = jax.random.randint(streams[6], (TBUCKETS,), 0, live_count, jnp.int32)
    anchor_tile = SB_DEV + anchor_rank * SLOTS + anchor_slot
    positions = jnp.arange(LIST_P, dtype=jnp.int32)[None, :]
    near_list = jnp.where(positions == anchor_place[:, None], anchor_tile[:, None], listed)
    anchor_bucket = partner * SB_DEV + sent_buckets[partner, own_rank, anchor_slot]
    return (sent_buckets, filled_count, near_list, live_count, anchor_bucket)


def draw_sources(key, part):
    centre, spread, key_offset, key_mass = geometry(key)
    offset = jnp.clip(jax.random.normal(key_offset, (SBUCKETS, 3, BS), jnp.float32), -4.0, 4.0)
    places = centre + spread * offset
    masses = jnp.exp(jax.random.uniform(key_mass, (SBUCKETS, 1, BS), jnp.float32, jnp.log(0.0002), jnp.log(0.002)))
    return jnp.concatenate([places, masses], 1)


def draw_targets(key, part):
    shapes = geometry(key)
    centre = shapes[0]
    spread = shapes[1]
    anchor_bucket = routing(key)[4]
    key_place = jax.random.fold_in(key, 13)
    offset = jnp.clip(jax.random.normal(key_place, (TBUCKETS, 3, TBS), jnp.float32), -3.0, 3.0)
    places = centre[anchor_bucket] + 0.7 * spread[anchor_bucket] * offset
    return jnp.transpose(places, (1, 0, 2)).reshape(3, TPART)


def draw_send_ids(key, part):
    return routing(key)[0]


def draw_send_count(key, part):
    return routing(key)[1]


def draw_near_ids(key, part):
    return routing(key)[2]


def draw_near_count(key, part):
    return routing(key)[3]


def place_ends(array, rng, low, high):
    index_at = [jax.random.randint(jax.random.fold_in(rng, axis), (), 0, length) for axis, length in enumerate(array.shape)]
    main_axis = array.shape.index(max(array.shape))
    beside = index_at[:main_axis] + [(index_at[main_axis] + 1) % array.shape[main_axis]] + index_at[main_axis + 1:]
    return array.at[tuple(index_at)].set(low).at[tuple(beside)].set(high)


def setup_inputs(seed: int = 0) -> dict:
    key_of = jax.random.split(jax.random.key(seed), 8)
    return {
        "targets": draw_targets(jax.random.fold_in(key_of[7], 71), 0),
        "sources": draw_sources(jax.random.fold_in(key_of[7], 71), 0),
        "send_ids": draw_send_ids(jax.random.fold_in(key_of[7], 71), 0),
        "send_count": draw_send_count(jax.random.fold_in(key_of[7], 71), 0),
        "far_ids": place_ends(jax.random.randint(key_of[4], (TBUCKETS, LIST_C), 0, SBUCKETS), jax.random.fold_in(key_of[4], 1), 0, SBUCKETS - 1).astype(jnp.int32),
        "near_ids": draw_near_ids(jax.random.fold_in(key_of[7], 71), 0),
        "near_count": draw_near_count(jax.random.fold_in(key_of[7], 71), 0),
    }


soften_sq = 0.01

def moments(buckets):
    places = buckets[:, :3, :]
    masses = buckets[:, 3, :]
    weight_sum = lax.optimization_barrier(jnp.sum(masses, axis=-1))
    centre = lax.optimization_barrier(jnp.sum(places * masses[:, None, :], axis=-1)) / weight_sum[:, None]
    offset = places - centre[:, :, None]
    weighted = offset * masses[:, None, :]
    sxx = lax.optimization_barrier(jnp.sum(weighted[:, 0] * offset[:, 0], axis=-1))
    syy = lax.optimization_barrier(jnp.sum(weighted[:, 1] * offset[:, 1], axis=-1))
    szz = lax.optimization_barrier(jnp.sum(weighted[:, 2] * offset[:, 2], axis=-1))
    sxy = lax.optimization_barrier(jnp.sum(weighted[:, 0] * offset[:, 1], axis=-1))
    sxz = lax.optimization_barrier(jnp.sum(weighted[:, 0] * offset[:, 2], axis=-1))
    syz = lax.optimization_barrier(jnp.sum(weighted[:, 1] * offset[:, 2], axis=-1))
    return jnp.stack([weight_sum, centre[:, 0], centre[:, 1], centre[:, 2], sxx, syy, szz, sxy, sxz, syz], 0)

def far_field(chosen_cells, points):
    delta_x = points[0][:, None, :] - chosen_cells[1][:, :, None]
    delta_y = points[1][:, None, :] - chosen_cells[2][:, :, None]
    delta_z = points[2][:, None, :] - chosen_cells[3][:, :, None]
    dist_sq = delta_x * delta_x + delta_y * delta_y + delta_z * delta_z + soften_sq
    inverse = 1.0 / jnp.sqrt(dist_sq)
    second = chosen_cells[4:10][..., None]
    quad_form = second[0] * delta_x * delta_x + second[1] * delta_y * delta_y + second[2] * delta_z * delta_z + 2.0 * (second[3] * delta_x * delta_y + second[4] * delta_x * delta_z + second[5] * delta_y * delta_z)
    trace_sum = second[0] + second[1] + second[2]
    inv_cube = inverse * inverse * inverse
    contrib = chosen_cells[0][..., None] * inverse + 0.5 * (3.0 * quad_form - dist_sq * trace_sum) * inv_cube * inverse * inverse
    return -lax.optimization_barrier(jnp.sum(contrib, axis=1))

def near_field(chosen, counts, points):
    listed = chosen.shape[1]
    active = (jnp.arange(listed, dtype=jnp.int32)[None, :] < counts[:, None]).astype(chosen.dtype)

    def bucket(inputs):
        picked, flags, spots = inputs
        places = jnp.transpose(picked[:, :3, :], (1, 0, 2)).reshape(3, -1)
        masses = (picked[:, 3, :] * flags[:, None]).reshape(-1)
        delta_x = spots[0][:, None] - places[0][None, :]
        delta_y = spots[1][:, None] - places[1][None, :]
        delta_z = spots[2][:, None] - places[2][None, :]
        inverse = 1.0 / jnp.sqrt(delta_x * delta_x + delta_y * delta_y + delta_z * delta_z + soften_sq)
        return -jnp.dot(inverse, masses, precision=lax.Precision.HIGHEST)
    return lax.map(bucket, (chosen, active, jnp.transpose(points, (1, 0, 2))))

def reference(targets, sources, send_ids, send_count, far_ids, near_ids, near_count):
    multipoles = moments(sources)
    group_size = N_GX * N_GZ
    per_device = TB_DEV * TBS

    def domain(device):
        index_x = device // (N_GY * N_GZ)
        index_y = device // N_GZ % N_GY
        index_z = device % N_GZ
        ranks = jnp.arange(group_size, dtype=jnp.int32)
        partner = ranks // N_GZ * (N_GY * N_GZ) + index_y * N_GZ + ranks % N_GZ
        own_slot = index_x * N_GZ + index_z
        bucket_ids = send_ids[partner, own_slot]
        counts = send_count[partner, own_slot]
        filled = (jnp.arange(SLOTS, dtype=jnp.int32)[None, :] < counts[:, None]).astype(sources.dtype)
        remote = sources[partner[:, None] * SB_DEV + bucket_ids] * filled[:, :, None, None]
        own_tiles = lax.dynamic_slice_in_dim(sources, (device * SB_DEV).astype(jnp.int32), SB_DEV, 0)
        source_tiles = jnp.concatenate([own_tiles, remote.reshape((group_size * SLOTS, 4, BS))], 0)
        points = lax.dynamic_slice_in_dim(targets, (device * per_device).astype(jnp.int32), per_device, 1).reshape(3, TB_DEV, TBS)
        far_rows = lax.dynamic_slice_in_dim(far_ids, (device * TB_DEV).astype(jnp.int32), TB_DEV, 0)
        near_rows = lax.dynamic_slice_in_dim(near_ids, (device * TB_DEV).astype(jnp.int32), TB_DEV, 0)
        live_rows = lax.dynamic_slice_in_dim(near_count, (device * TB_DEV).astype(jnp.int32), TB_DEV, 0)
        far_part = far_field(multipoles[:, far_rows], points)
        near_part = near_field(source_tiles[near_rows], live_rows, points)
        return (far_part + near_part).reshape(-1)
    result = lax.map(domain, jnp.arange(N_GX * N_GY * N_GZ, dtype=jnp.int32))
    return result.reshape(-1)
```

```python
import functools

import jax
import jax.numpy as jnp
from jax import lax
from jax.experimental import pallas as pl
from jax.experimental.pallas import tpu as pltpu
from jax.sharding import PartitionSpec as P

ALL = ("gx", "gy", "gz")
MESH = pl.DeviceIdType.MESH
SOFT = 0.01
FAR = 64
NEAR = 8
LISTED = FAR + NEAR
PARAMS = 16
VMEM = pltpu.VMEM
SMEM = pltpu.SMEM


def iota(shape, dim):
    return lax.broadcasted_iota(jnp.int32, shape, dim)


def sorted_lists(nx, nz, cells_per_x, own, ids, counts):
    lane = iota((8, 128), 1)
    is_far = lane < FAR
    remote = ids - own
    rank = remote >> 1
    live = (lane - FAR < counts) & (remote >= 0)
    key = jnp.where(is_far, ids // cells_per_x, jnp.where(live, rank // nz, nx))
    code = jnp.where(is_far, ids % cells_per_x, (rank % nz) * 2 + (remote & 1))
    far_base = LISTED
    near_base = LISTED + nx + 1
    place = jnp.zeros((8, 128), jnp.int32)
    starts = jnp.zeros((8, 128), jnp.int32)
    for e in range(LISTED):
        other = jnp.broadcast_to(key[:, e : e + 1], (8, 128))
        before = (other < key) | ((other == key) & (lane > e))
        same = is_far if e < FAR else ~is_far
        place += jnp.where(before & same, 1, 0)
        base = far_base if e < FAR else near_base
        starts += jnp.where((lane >= base) & (lane <= base + nx) & (other < lane - base), 1, 0)
    place = jnp.where(is_far, place, place + FAR)
    both = place * 8192 + code
    out = starts
    for e in range(LISTED):
        entry = jnp.broadcast_to(both[:, e : e + 1], (8, 128))
        out += jnp.where((entry >> 13) == lane, entry & 8191, 0)
    return out


def cell_row(x, y, z, m):
    lane = iota((8, 128), 1)
    sub = iota((8, 128), 0)

    def total(v):
        return jnp.sum(v, axis=1, keepdims=True)

    mass = total(m)
    cx, cy, cz = total(x * m) / mass, total(y * m) / mass, total(z * m) / mass
    dx, dy, dz = x - cx, y - cy, z - cz
    wx, wy, wz = dx * m, dy * m, dz * m
    sxx, syy, szz = total(wx * dx), total(wy * dy), total(wz * dz)
    sxy, sxz, syz = total(wx * dy), total(wx * dz), total(wy * dz)
    values = (
        mass, cx, cy, cz, 1.5 * sxx, 1.5 * syy, 1.5 * szz,
        3.0 * sxy, 3.0 * sxz, 3.0 * syz, 0.5 * (sxx + syy + szz),
    )
    spread = jnp.zeros((8, 128), jnp.float32)
    for p, value in enumerate(values):
        spread = jnp.where(lane == sub * PARAMS + p, value, spread)
    return jnp.sum(spread, axis=0, keepdims=True)


def gather_kernel(
    sizes, send_ids, send_count, near_count, far, near, tgt, src,
    t_all, meta_all, tiles_all, cells_all,
    ids_buf, tbuf, mbuf, obuf, cbuf,
    t_send, t_recv, m_send, m_recv, o_send, o_recv, c_send, c_recv, own_sem,
):
    nx, ny, nz = sizes
    gx, gy, gz = (lax.axis_index(n) for n in ALL)
    own = src.shape[0]
    plane = [(dy, dz) for dy in range(ny) for dz in range(nz) if dy or dz]
    barrier = pltpu.get_barrier_semaphore()

    def along_x(d):
        return (lax.rem(gx + d, nx), gy, gz)

    def in_plane(dy, dz):
        return (gx, lax.rem(gy + dy, ny), lax.rem(gz + dz, nz))

    for d in range(1, nx):
        pl.semaphore_signal(barrier, inc=1, device_id=along_x(d), device_id_type=MESH)
    for dy, dz in plane:
        pl.semaphore_signal(barrier, inc=1, device_id=in_plane(dy, dz), device_id_type=MESH)

    for t in range(8):
        for c in range(3):
            tbuf[c, t : t + 1, :] = tgt[t, c : c + 1, :]
    ids_buf[...] = jnp.zeros((8, 128), jnp.int32)
    ids_buf[:, 0:FAR] = far[...]
    ids_buf[:, FAR:LISTED] = near[...]
    sub = iota((8, 128), 0)
    counts = jnp.zeros((8, 128), jnp.int32)
    for t in range(8):
        counts = jnp.where(sub == t, near_count[t], counts)
    mbuf[...] = sorted_lists(nx, nz, ny * nz * own, own, ids_buf[...], counts)

    def gather_for(r, carry):
        i, k = r // nz, lax.rem(r, nz)
        filled = send_count[0, r]
        for s in range(2):
            bucket = src[send_ids[s, r]]
            obuf[k, i * 2 + s] = jnp.where(filled > s, bucket, 0.0)
        return carry

    lax.fori_loop(0, nx * nz, gather_for, 0, unroll=4)

    pl.semaphore_wait(barrier, nx - 1 + len(plane))

    waits = []
    order = sorted(range(1, nx), key=lambda d: -min(d, nx - d))
    for d in order:
        for source, dest, s_sem, r_sem in (
            (tbuf, t_all, t_send, t_recv), (mbuf, meta_all, m_send, m_recv)
        ):
            copy = pltpu.make_async_remote_copy(
                src_ref=source, dst_ref=dest.at[gx], send_sem=s_sem.at[d], recv_sem=r_sem.at[d],
                device_id=along_x(d), device_id_type=MESH,
            )
            copy.start()
            waits.append(copy)
    for dz in range(1, nz):
        to = lax.rem(gz + dz, nz)
        copy = pltpu.make_async_remote_copy(
            src_ref=obuf.at[to], dst_ref=tiles_all.at[gz],
            send_sem=o_send.at[dz], recv_sem=o_recv.at[dz],
            device_id=in_plane(0, dz), device_id_type=MESH,
        )
        copy.start()
        waits.append(copy)
    mine = pltpu.make_async_copy(obuf.at[gz], tiles_all.at[gz], own_sem)
    mine.start()
    t_all[gx] = tbuf[...]
    meta_all[gx] = mbuf[...]

    def moments(g, carry):
        group = src[pl.ds(g * 8, 8)]
        x, y, z, m = (group[:, r, :] for r in range(4))
        cbuf[pl.ds(g, 1), :] = cell_row(x, y, z, m)
        return carry

    lax.fori_loop(0, own // 8, moments, 0)
    me = gy * nz + gz
    for n, (dy, dz) in enumerate(plane):
        copy = pltpu.make_async_remote_copy(
            src_ref=cbuf, dst_ref=cells_all.at[me], send_sem=c_send.at[n], recv_sem=c_recv.at[n],
            device_id=in_plane(dy, dz), device_id_type=MESH,
        )
        copy.start()
        waits.append(copy)
    cells_all[me] = cbuf[...]
    for copy in waits:
        copy.wait()
    mine.wait()


def near_sums(tx, ty, tz, rows_of, tiles, acc, first):
    for rb in range(0, 128, 32):
        cx = jnp.broadcast_to(tx[rb : rb + 32], (32, 128))
        cy = jnp.broadcast_to(ty[rb : rb + 32], (32, 128))
        cz = jnp.broadcast_to(tz[rb : rb + 32], (32, 128))
        total = jnp.zeros((32, 128), jnp.float32) if first else acc[rb : rb + 32, :]
        for n in range(tiles):
            for h in range(2):
                sx, sy, sz, m = rows_of(n, h)
                dx, dy, dz = cx - sx, cy - sy, cz - sz
                total += lax.rsqrt(dx * dx + dy * dy + dz * dz + SOFT) * m
        acc[rb : rb + 32, :] = total


def lane_sums(acc):
    value = acc[...]
    high = value.astype(jnp.bfloat16)
    low = (value - high.astype(jnp.float32)).astype(jnp.bfloat16)
    ones = jnp.ones((8, 128), jnp.bfloat16)

    def summed(v):
        return lax.dot_general(
            ones, v, (((1,), (1,)), ((), ())), preferred_element_type=jnp.float32
        )

    return (summed(high) + summed(low))[0:1]


def columns(x, y, z):
    rows = jnp.concatenate([x, y, z, jnp.zeros((5, 128), jnp.float32)], axis=0)
    cols = rows.T
    return cols[:, 0:1], cols[:, 1:2], cols[:, 2:3]


def far_chunk(v, live, tx, ty, tz):
    def p(n):
        return jnp.broadcast_to(v[:, n : n + 1], (8, 128))

    dx, dy, dz = tx - p(1), ty - p(2), tz - p(3)
    r2 = dx * dx + dy * dy + dz * dz + SOFT
    inv = lax.rsqrt(r2)
    inv2 = inv * inv
    quad = dx * (p(4) * dx + p(7) * dy + p(8) * dz) + dy * (p(5) * dy + p(9) * dz) + p(6) * dz * dz
    value = inv * (p(0) + (quad - r2 * p(10)) * (inv2 * inv2))
    return jnp.sum(jnp.where(iota((8, 128), 0) < live, value, 0.0), axis=0, keepdims=True)


def walk_kernel(sizes, meta, t_all, tiles, cells, out, rows, acc, todo):
    nx, ny, nz = sizes
    a = lax.axis_index("gx")
    far_at = LISTED + a
    near_at = LISTED + nx + 1 + a

    def fetch(i, t, start, u):
        cell = meta[i, t, jnp.minimum(start + u, FAR - 1)]
        row = cells[pl.ds(cell >> 3, 1), :]
        shift = (128 - (cell & 7) * PARAMS) & 127
        return pltpu.roll(jnp.broadcast_to(row, (8, 128)), shift, 1)[0:1]

    def domain(i, found):
        bounds = []
        for t in range(8):
            bounds.append((meta[i, t, far_at], meta[i, t, far_at + 1]))
        for t in range(8):
            for u in range(8):
                rows[t * 8 + u : t * 8 + u + 1, :] = fetch(i, t, bounds[t][0], u)
        most = jnp.int32(0)
        for t in range(8):
            f0, f1 = bounds[t]
            most = jnp.maximum(most, f1 - f0)
            tx, ty, tz = (t_all[i, c, t : t + 1, :] for c in range(3))
            out[i, t : t + 1, :] = -far_chunk(rows[t * 8 : t * 8 + 8, :], f1 - f0, tx, ty, tz)

        @pl.when(most > 8)
        def _():
            def bucket(t, carry):
                f0 = meta[i, t, far_at]
                f1 = meta[i, t, far_at + 1]
                tx, ty, tz = (t_all[i, c, pl.ds(t, 1), :] for c in range(3))

                def chunk(n, carry):
                    start = f0 + n * 8
                    for u in range(8):
                        rows[u : u + 1, :] = fetch(i, t, start, u)
                    out[i, pl.ds(t, 1), :] -= far_chunk(rows[0:8, :], f1 - start, tx, ty, tz)
                    return carry

                return lax.fori_loop(1, (f1 - f0 + 7) // 8, chunk, carry)

            lax.fori_loop(0, 8, bucket, 0)

        def listed(t, found):
            n0 = meta[i, t, near_at]
            n1 = meta[i, t, near_at + 1]

            def entry(e, found):
                code = meta[i, t, FAR + e]
                todo[found] = (i * 8 + t) * 1024 + (code >> 1) * (nx * 2) + i * 2 + (code & 1)
                return found + 1

            return lax.fori_loop(n0, n1, entry, found)

        return lax.fori_loop(0, 8, listed, found)

    found = lax.fori_loop(0, nx, domain, jnp.int32(0))

    def near(n, carry):
        item = todo[n]
        tile = item & 1023
        i = item >> 13
        t = (item >> 10) & 7

        def rows_of(_, h):
            return [tiles[tile, r : r + 1, h * 128 : (h + 1) * 128] for r in range(4)]

        near_sums(*columns(*(t_all[i, c, pl.ds(t, 1), :] for c in range(3))), rows_of, 1, acc, True)
        out[i, pl.ds(t, 1), :] -= lane_sums(acc)
        return carry

    lax.fori_loop(0, found, near, 0)


def return_kernel(
    sizes, near_ids, near_count, part, tgt, src, out, landed, acc, total, send, recv,
):
    nx, ny, nz = sizes
    gx, gy, gz = (lax.axis_index(n) for n in ALL)
    own = src.shape[0]
    barrier = pltpu.get_barrier_semaphore()

    def along_x(d):
        return (lax.rem(gx + d, nx), gy, gz)

    for d in range(1, nx):
        pl.semaphore_signal(barrier, inc=1, device_id=along_x(d), device_id_type=MESH)
    pl.semaphore_wait(barrier, nx - 1)
    copies = []
    for d in sorted(range(1, nx), key=lambda d: -min(d, nx - d)):
        copy = pltpu.make_async_remote_copy(
            src_ref=part.at[lax.rem(gx + d, nx)], dst_ref=landed.at[d - 1],
            send_sem=send.at[d], recv_sem=recv.at[d],
            device_id=along_x(d), device_id_type=MESH,
        )
        copy.start()
        copies.append(copy)

    def bucket(t, carry):
        cols = columns(*(tgt[t, c : c + 1, :] for c in range(3)))
        count = near_count[t]
        ids = [near_ids[t, e] for e in range(NEAR)]

        def rows_of(e, h):
            tile = jnp.minimum(ids[e], own - 1)
            live = (ids[e] < own) & (count > e)
            x, y, z, m = (src[tile, r : r + 1, h * 128 : (h + 1) * 128] for r in range(4))
            return x, y, z, jnp.where(live, m, 0.0)

        near_sums(*cols, rows_of, NEAR, acc, True)
        total[pl.ds(t, 1), :] = lane_sums(acc)
        return carry

    lax.fori_loop(0, 8, bucket, 0)
    summed = part[gx] - total[...]
    for copy in copies:
        copy.wait()
    for d in range(nx - 1):
        summed += landed[d]
    out[...] = summed


def body(sizes, targets, sources, send_ids, send_count, far_ids, near_ids, near_count):
    nx, ny, nz = sizes
    f32, i32 = jnp.float32, jnp.int32
    own = sources.shape[0]
    shape = jax.ShapeDtypeStruct
    vmem = pl.BlockSpec(memory_space=VMEM)
    smem = pl.BlockSpec(memory_space=SMEM)
    dma = pltpu.SemaphoreType.DMA
    tgt = jnp.transpose(targets.reshape(3, 8, 128), (1, 0, 2))
    t_all, meta_all, tiles_all, cells_all = pl.pallas_call(
        functools.partial(gather_kernel, sizes),
        out_shape=(
            shape((nx, 3, 8, 128), f32), shape((nx, 8, 128), i32),
            shape((nz, nx * 2, 4, 256), f32), shape((ny * nz, own // 8, 128), f32),
        ),
        in_specs=[smem, smem, smem, vmem, vmem, vmem, vmem],
        out_specs=(vmem,) * 4,
        scratch_shapes=[
            VMEM((8, 128), i32), VMEM((3, 8, 128), f32), VMEM((8, 128), i32),
            VMEM((nz, nx * 2, 4, 256), f32), VMEM((own // 8, 128), f32),
            dma((nx,)), dma((nx,)), dma((nx,)), dma((nx,)), dma((nz,)), dma((nz,)),
            dma((ny * nz,)), dma((ny * nz,)), dma,
        ],
        compiler_params=pltpu.CompilerParams(collective_id=0, has_side_effects=True),
        name="gather",
    )(send_ids[0].T, send_count, near_count, far_ids, near_ids, tgt, sources)

    part = pl.pallas_call(
        functools.partial(walk_kernel, sizes),
        out_shape=shape((nx, 8, 128), f32),
        in_specs=[smem, vmem, vmem, vmem],
        out_specs=vmem,
        scratch_shapes=[VMEM((64, 128), f32), VMEM((128, 128), f32), SMEM((nx * 64,), i32)],
        name="walk",
    )(
        meta_all, t_all, tiles_all.reshape(nz * nx * 2, 4, 256),
        cells_all.reshape(ny * nz * own // 8, 128),
    )

    out = pl.pallas_call(
        functools.partial(return_kernel, sizes),
        out_shape=shape((8, 128), f32),
        in_specs=[smem, smem, vmem, vmem, vmem],
        out_specs=vmem,
        scratch_shapes=[
            VMEM((nx - 1, 8, 128), f32), VMEM((128, 128), f32), VMEM((8, 128), f32),
            dma((nx,)), dma((nx,)),
        ],
        compiler_params=pltpu.CompilerParams(collective_id=1, has_side_effects=True),
        name="bring_back",
    )(near_ids, near_count, part, tgt, sources)
    return out.reshape(-1)


def solution(mesh):
    sizes = tuple(mesh.shape[n] for n in ALL)
    in_specs = (
        P(None, ALL), P(ALL, None, None), P(ALL, None, None), P(ALL, None),
        P(ALL, None), P(ALL, None), P(ALL),
    )
    return jax.shard_map(
        functools.partial(body, sizes), mesh=mesh, in_specs=in_specs, out_specs=P(ALL),
        check_vma=False,
    )
```

```python
import functools

import jax
import jax.numpy as jnp
from jax import lax
from jax.experimental import pallas as pl
from jax.experimental.pallas import tpu as pltpu
from jax.sharding import PartitionSpec as P

ALL = ("gx", "gy", "gz")
MESH = pl.DeviceIdType.MESH
SOFT = 0.01
FAR = 64
NEAR = 8
LISTED = FAR + NEAR
PARAMS = 16
LIMIT = 16 * 1024 * 1024
VMEM = pltpu.VMEM
SMEM = pltpu.SMEM


def iota(shape, dim):
    return lax.broadcasted_iota(jnp.int32, shape, dim)


def sorted_lists(nx, nz, cells_per_x, own, ids, counts):
    lane = iota((8, 128), 1)
    sub = iota((8, 128), 0)
    is_far = lane < FAR
    is_near = (lane >= FAR) & (lane < LISTED)
    remote = ids - own
    rank = remote >> 1
    live = (lane - FAR < counts) & (remote >= 0)
    near_code = sub * (2 * nz) + (rank % nz) * 2 + (remote & 1)
    cell = ids % cells_per_x
    cell = cell - (cell & 63) + ((cell & 7) << 3) + ((cell >> 3) & 7)
    order = jnp.where(is_far, lane, sub * NEAR + lane - FAR)
    key = jnp.where(is_far, ids // cells_per_x, jnp.where(live, rank // nz, nx)) * 64 + order
    far_base, near_base, most_base = LISTED, LISTED + nx + 1, LISTED + 2 * nx + 2
    far_limit = jnp.where((lane >= far_base) & (lane < near_base), (lane - far_base) * 64, 0)
    near_limit = jnp.where((lane >= near_base) & (lane < most_base), (lane - near_base) * 64, 0)
    zero = jnp.zeros((8, 128), jnp.int32)
    far_place, near_place, far_start, near_start = zero, zero, zero, zero
    for e in range(FAR):
        other = jnp.broadcast_to(key[:, e : e + 1], (8, 128))
        far_place += jnp.where(other < key, 1, 0)
        far_start += jnp.where(other < far_limit, 1, 0)
    for e in range(NEAR):
        other = jnp.broadcast_to(key[:, FAR + e : FAR + e + 1], (8, 128))
        near_start += jnp.where(other < near_limit, 1, 0)
        for r in range(8):
            moved = pltpu.roll(other, r, 0) if r else other
            near_place += jnp.where(moved < key, 1, 0)
    both = jnp.where(is_far, far_place * 8192 + cell, near_place * 8192 + near_code)
    far_list, near_list = zero, zero
    for e in range(LISTED):
        entry = jnp.broadcast_to(both[:, e : e + 1], (8, 128))
        term = jnp.where((entry >> 13) == lane, entry & 8191, 0)
        if e < FAR:
            far_list += term
        else:
            near_list += term
    near_list = jnp.broadcast_to(jnp.sum(near_list, axis=0, keepdims=True), (8, 128))
    near_start = jnp.broadcast_to(jnp.sum(near_start, axis=0, keepdims=True), (8, 128))
    near_rows = zero
    for t in range(8):
        near_rows = jnp.where(sub == t, pltpu.roll(near_list, (FAR - 8 * t) % 128, 1), near_rows)
    most = pltpu.roll(far_start, 127, 1) - far_start
    most = jnp.broadcast_to(jnp.max(most, axis=0, keepdims=True), (8, 128))
    most = pltpu.roll(most, most_base - far_base, 1)
    out = jnp.where(is_far, far_list, jnp.where(is_near, near_rows, far_start + near_start))
    return jnp.where(lane >= most_base, most, out)


def cell_row(x, y, z, m):
    lane = iota((8, 128), 1)
    sub = iota((8, 128), 0)

    def total(*v):
        return jnp.sum(sum(p * q for p, q in zip(*v)) if len(v) == 2 else sum(v[0]), axis=1, keepdims=True)

    mass = total(m)
    cx, cy, cz = (total(v, m) / mass for v in (x, y, z))
    dx, dy, dz = ([h - c for h in v] for v, c in ((x, cx), (y, cy), (z, cz)))
    wx, wy, wz = ([h * w for h, w in zip(v, m)] for v in (dx, dy, dz))
    sxx, syy, szz = total(wx, dx), total(wy, dy), total(wz, dz)
    sxy, sxz, syz = total(wx, dy), total(wx, dz), total(wy, dz)
    values = (
        mass, cx, cy, cz, 1.5 * sxx, 1.5 * syy, 1.5 * szz,
        3.0 * sxy, 3.0 * sxz, 3.0 * syz, 0.5 * (sxx + syy + szz),
    )
    spread = jnp.zeros((8, 128), jnp.float32)
    for p, value in enumerate(values):
        spread = jnp.where(lane == sub * PARAMS + p, value, spread)
    return jnp.sum(spread, axis=0, keepdims=True)


def wrap(value, size):
    return value & (size - 1) if size & (size - 1) == 0 else lax.rem(value, size)


def gather_kernel(
    sizes, send_ids, send_count, near_ids, near_count, far, near, tgt, src_hbm,
    t_all, meta_all, tiles_all, table, local,
    src, ids_buf, tbuf, mbuf, obuf, cbuf, cells_all, acc,
    t_send, t_recv, m_send, m_recv, o_send, o_recv, c_send, c_recv, own_sem, src_sem,
):
    nx, ny, nz = sizes
    gx, gy, gz = (lax.axis_index(n) for n in ALL)
    own = src.shape[0]
    plane = [(dy, dz) for dy in range(ny) for dz in range(nz) if dy or dz]
    barrier = pltpu.get_barrier_semaphore()
    load = pltpu.make_async_copy(src_hbm, src, src_sem)
    load.start()
    xs = [wrap(gx + d, nx) for d in range(nx)]
    ys = [wrap(gy + d, ny) for d in range(ny)]
    zs = [wrap(gz + d, nz) for d in range(nz)]

    def along_x(d):
        return (xs[d], gy, gz)

    def in_plane(dy, dz):
        return (gx, ys[dy], zs[dz])

    far_first = sorted(range(1, nx), key=lambda d: -min(d, nx - d))
    for d in far_first:
        pl.semaphore_signal(barrier, inc=1, device_id=along_x(d), device_id_type=MESH)
    for dy, dz in plane:
        pl.semaphore_signal(barrier, inc=1, device_id=in_plane(dy, dz), device_id_type=MESH)

    for t in range(8):
        for c in range(3):
            tbuf[c, t : t + 1, :] = tgt[t, c : c + 1, :]
    ids_buf[...] = jnp.zeros((8, 128), jnp.int32)
    ids_buf[:, 0:FAR] = far[...]
    ids_buf[:, FAR:LISTED] = near[...]
    sub = iota((8, 128), 0)
    counts = jnp.zeros((8, 128), jnp.int32)
    for t in range(8):
        counts = jnp.where(sub == t, near_count[t], counts)
    mbuf[...] = sorted_lists(nx, nz, ny * nz * own, own, ids_buf[...], counts)
    load.wait()

    for dz in range(nz):
        k = zs[dz]

        def gather_for(i, carry):
            r = i * nz + k
            filled = send_count[0, r]
            for s in range(2):
                obuf[k, i * 2 + s] = jnp.where(filled > s, src[send_ids[s, r]], 0.0)
            return carry

        lax.fori_loop(0, nx, gather_for, 0, unroll=min(nx, 8))

    pl.semaphore_wait(barrier, nx - 1 + len(plane))

    t_waits, o_waits, c_waits = [], [], []
    for d in far_first:
        for source, dest, s_sem, r_sem in (
            (tbuf, t_all, t_send, t_recv), (mbuf, meta_all, m_send, m_recv)
        ):
            copy = pltpu.make_async_remote_copy(
                src_ref=source, dst_ref=dest.at[gx], send_sem=s_sem.at[d], recv_sem=r_sem.at[d],
                device_id=along_x(d), device_id_type=MESH,
            )
            copy.start()
            t_waits.append(copy)
    for dz in range(1, nz):
        copy = pltpu.make_async_remote_copy(
            src_ref=obuf.at[zs[dz]], dst_ref=tiles_all.at[gz],
            send_sem=o_send.at[dz], recv_sem=o_recv.at[dz],
            device_id=in_plane(0, dz), device_id_type=MESH,
        )
        copy.start()
        o_waits.append(copy)
    mine = pltpu.make_async_copy(obuf.at[gz], tiles_all.at[gz], own_sem)
    mine.start()
    t_all[gx] = tbuf[...]
    meta_all[gx] = mbuf[...]

    def moments(g, carry):
        group = src[pl.ds(g * 8, 8)]
        x, y, z, m = ([group[:, h * 4 + r, :] for h in range(2)] for r in range(4))
        cbuf[pl.ds(g, 1), :] = cell_row(x, y, z, m)
        return carry

    lax.fori_loop(0, own // 8, moments, 0)
    me = gy * nz + gz
    for n, (dy, dz) in enumerate(plane):
        copy = pltpu.make_async_remote_copy(
            src_ref=cbuf, dst_ref=cells_all.at[me], send_sem=c_send.at[n], recv_sem=c_recv.at[n],
            device_id=in_plane(dy, dz), device_id_type=MESH,
        )
        copy.start()
        c_waits.append(copy)
    cells_all[me] = cbuf[...]

    def bucket(t, carry):
        cols = columns(*(tgt[t, c : c + 1, :] for c in range(3)))
        count = near_count[t]
        ids = [near_ids[t, e] for e in range(NEAR)]

        def rows_of(e, h):
            tile = jnp.minimum(ids[e], own - 1)
            live = (ids[e] < own) & (count > e)
            x, y, z, m = (src[tile, h * 4 + r : h * 4 + r + 1, :] for r in range(4))
            return x, y, z, jnp.where(live, m, 0.0)

        near_sums(*cols, rows_of, NEAR, acc)
        local[pl.ds(t, 1), :] = -lane_sums(acc)
        return carry

    lax.fori_loop(0, 8, bucket, 0)
    for copy in c_waits:
        copy.wait()
    blocks = own // 64

    def expand(n, carry):
        for b in range(blocks):
            cells = cells_all[n, b * 8 : b * 8 + 8, :]
            for j in range(8):
                moved = pltpu.roll(cells, 128 - PARAMS * j, 1) if j else cells
                table[pl.ds((n * blocks + b) * 64 + j * 8, 8), :] = moved
        return carry

    lax.fori_loop(0, ny * nz, expand, 0)
    for copy in t_waits + o_waits:
        copy.wait()
    mine.wait()


def near_sums(tx, ty, tz, rows_of, tiles, acc):
    for rb in range(0, 128, 32):
        cx = jnp.broadcast_to(tx[rb : rb + 32], (32, 128))
        cy = jnp.broadcast_to(ty[rb : rb + 32], (32, 128))
        cz = jnp.broadcast_to(tz[rb : rb + 32], (32, 128))
        total = jnp.zeros((32, 128), jnp.float32)
        for n in range(tiles):
            for h in range(2):
                sx, sy, sz, m = rows_of(n, h)
                dx, dy, dz = cx - sx, cy - sy, cz - sz
                total += lax.rsqrt(dx * dx + dy * dy + dz * dz + SOFT) * m
        acc[rb : rb + 32, :] = total


def lane_sums(acc):
    value = acc[...]
    high = value.astype(jnp.bfloat16)
    low = (value - high.astype(jnp.float32)).astype(jnp.bfloat16)
    ones = jnp.ones((8, 128), jnp.bfloat16)

    def summed(v):
        return lax.dot_general(
            ones, v, (((1,), (1,)), ((), ())), preferred_element_type=jnp.float32
        )

    return (summed(high) + summed(low))[0:1]


def columns(x, y, z):
    rows = jnp.concatenate([x, y, z, jnp.zeros((5, 128), jnp.float32)], axis=0)
    cols = rows.T
    return cols[:, 0:1], cols[:, 1:2], cols[:, 2:3]


def far_chunk(v, live, tx, ty, tz):
    def p(n):
        return jnp.broadcast_to(v[:, n : n + 1], (8, 128))

    dx, dy, dz = tx - p(1), ty - p(2), tz - p(3)
    r2 = dx * dx + dy * dy + dz * dz + SOFT
    inv = lax.rsqrt(r2)
    inv2 = inv * inv
    quad = dx * (p(4) * dx + p(7) * dy + p(8) * dz) + dy * (p(5) * dy + p(9) * dz) + p(6) * dz * dz
    value = inv * (p(0) + (quad - r2 * p(10)) * (inv2 * inv2))
    return jnp.sum(jnp.where(iota((8, 128), 0) < live, value, 0.0), axis=0, keepdims=True)


def walk_kernel(sizes, meta, t_all, tiles, table, out, rows, acc0, acc1, todo):
    nx, ny, nz = sizes
    a = lax.axis_index("gx")
    out[...] = jnp.zeros_like(out)

    def domain(i, found):
        base = i * 1024
        near_at = base + LISTED + nx + 1 + a
        n0 = meta[near_at]
        n1 = meta[near_at + 1]

        @pl.when(meta[base + LISTED + 2 * nx + 2 + a] > 8)
        def _():
            def bucket(t, carry):
                at = base + t * 128
                f0 = meta[at + LISTED + a]
                f1 = meta[at + LISTED + a + 1]
                tx, ty, tz = (t_all[i, c, pl.ds(t, 1), :] for c in range(3))

                def chunk(n, carry):
                    start = f0 + n * 8
                    for u in range(8):
                        rows[u : u + 1, :] = table[pl.ds(meta[at + start + u], 1), :]
                    out[i, pl.ds(t, 1), :] -= far_chunk(rows[...], f1 - start, tx, ty, tz)
                    return carry

                return lax.fori_loop(1, (f1 - f0 + 7) >> 3, chunk, carry)

            lax.fori_loop(0, 8, bucket, 0)

        def entry(e, found):
            code = meta[base + ((e >> 3) << 7) + FAR + (e & 7)]
            t = code // (2 * nz)
            tile = ((code % (2 * nz)) >> 1) * (nx * 2) + i * 2 + (code & 1)
            todo[found] = (i * 8 + t) * 1024 + tile
            return found + 1

        return lax.fori_loop(n0, n1, entry, found)

    found = lax.fori_loop(0, nx, domain, jnp.int32(0))

    def near(n, carry):
        results = []
        for slot, acc in enumerate((acc0, acc1)):
            at = n * 2 + slot
            live = at < found
            item = todo[jnp.minimum(at, found - 1)]
            tile = item & 1023
            i = item >> 13
            t = (item >> 10) & 7

            def rows_of(_, h):
                x, y, z, m = (tiles[tile, h * 4 + r : h * 4 + r + 1, :] for r in range(4))
                return x, y, z, jnp.where(live, m, 0.0) if slot else m

            near_sums(*columns(*(t_all[i, c, pl.ds(t, 1), :] for c in range(3))), rows_of, 1, acc)
            results.append((i, t, lane_sums(acc)))
        for i, t, value in results:
            out[i, pl.ds(t, 1), :] -= value
        return carry

    lax.fori_loop(0, (found + 1) >> 1, near, 0)


def return_kernel(
    sizes, meta, t_all, table, part, local, out, landed, rows, mine, send, recv,
):
    nx, ny, nz = sizes
    gx, gy, gz = (lax.axis_index(n) for n in ALL)
    barrier = pltpu.get_barrier_semaphore()
    xs = [wrap(gx + d, nx) for d in range(nx)]
    far_first = sorted(range(1, nx), key=lambda d: -min(d, nx - d))
    for d in far_first:
        pl.semaphore_signal(barrier, inc=1, device_id=(xs[d], gy, gz), device_id_type=MESH)

    def domain(i, carry):
        bounds = []
        for t in range(8):
            at = i * 1024 + t * 128
            f0 = meta[at + LISTED + gx]
            bounds.append(meta[at + LISTED + gx + 1] - f0)
            for u in range(8):
                rows[t * 8 + u : t * 8 + u + 1, :] = table[pl.ds(meta[at + f0 + u], 1), :]
        for t in range(8):
            tx, ty, tz = (t_all[i, c, t : t + 1, :] for c in range(3))
            value = far_chunk(rows[t * 8 : t * 8 + 8, :], bounds[t], tx, ty, tz)
            mine[i, t : t + 1, :] = part[i, t : t + 1, :] - value
        return carry

    lax.fori_loop(0, nx, domain, 0)
    pl.semaphore_wait(barrier, nx - 1)
    copies = []
    for d in far_first:
        copy = pltpu.make_async_remote_copy(
            src_ref=mine.at[xs[d]], dst_ref=landed.at[d - 1],
            send_sem=send.at[d], recv_sem=recv.at[d],
            device_id=(xs[d], gy, gz), device_id_type=MESH,
        )
        copy.start()
        copies.append(copy)
    summed = mine[gx] + local[...]
    for copy in copies:
        copy.wait()
    for d in range(nx - 1):
        summed += landed[d]
    out[...] = summed


def body(sizes, targets, sources, send_ids, send_count, far_ids, near_ids, near_count):
    nx, ny, nz = sizes
    f32, i32 = jnp.float32, jnp.int32
    own = sources.shape[0]
    shape = jax.ShapeDtypeStruct
    vmem = pl.BlockSpec(memory_space=VMEM)
    smem = pl.BlockSpec(memory_space=SMEM)
    hbm = pl.BlockSpec(memory_space=pltpu.HBM)
    dma = pltpu.SemaphoreType.DMA
    tgt = jnp.transpose(targets.reshape(3, 8, 128), (1, 0, 2))
    src = jnp.transpose(sources.reshape(own, 4, 2, 128), (0, 2, 1, 3)).reshape(own, 8, 128)
    t_all, meta_all, tiles_all, table, local = pl.pallas_call(
        functools.partial(gather_kernel, sizes),
        out_shape=(
            shape((nx, 3, 8, 128), f32), shape((nx, 8, 128), i32),
            shape((nz, nx * 2, 8, 128), f32), shape((ny * nz * own, 128), f32),
            shape((8, 128), f32),
        ),
        in_specs=[smem, smem, smem, smem, vmem, vmem, vmem, hbm],
        out_specs=(vmem,) * 5,
        scratch_shapes=[
            VMEM((own, 8, 128), f32),
            VMEM((8, 128), i32), VMEM((3, 8, 128), f32), VMEM((8, 128), i32),
            VMEM((nz, nx * 2, 8, 128), f32), VMEM((own // 8, 128), f32),
            VMEM((ny * nz, own // 8, 128), f32), VMEM((128, 128), f32),
            dma((nx,)), dma((nx,)), dma((nx,)), dma((nx,)), dma((nz,)), dma((nz,)),
            dma((ny * nz,)), dma((ny * nz,)), dma, dma,
        ],
        compiler_params=pltpu.CompilerParams(
            collective_id=0, has_side_effects=True, vmem_limit_bytes=LIMIT
        ),
        name="gather",
    )(send_ids[0].T, send_count, near_ids, near_count, far_ids, near_ids, tgt, src)

    meta = meta_all.reshape(-1)
    part = pl.pallas_call(
        functools.partial(walk_kernel, sizes),
        out_shape=shape((nx, 8, 128), f32),
        in_specs=[smem, vmem, vmem, vmem],
        out_specs=vmem,
        scratch_shapes=[
            VMEM((8, 128), f32), VMEM((128, 128), f32), VMEM((128, 128), f32),
            SMEM((nx * 64,), i32),
        ],
        compiler_params=pltpu.CompilerParams(vmem_limit_bytes=LIMIT),
        name="walk",
    )(meta, t_all, tiles_all.reshape(nz * nx * 2, 8, 128), table)

    out = pl.pallas_call(
        functools.partial(return_kernel, sizes),
        out_shape=shape((8, 128), f32),
        in_specs=[smem, vmem, vmem, vmem, vmem],
        out_specs=vmem,
        scratch_shapes=[
            VMEM((nx - 1, 8, 128), f32), VMEM((64, 128), f32), VMEM((nx, 8, 128), f32),
            dma((nx,)), dma((nx,)),
        ],
        compiler_params=pltpu.CompilerParams(
            collective_id=1, has_side_effects=True, vmem_limit_bytes=LIMIT
        ),
        name="bring_back",
    )(meta, t_all, table, part, local)
    return out.reshape(-1)


def solution(mesh):
    sizes = tuple(mesh.shape[n] for n in ALL)
    in_specs = (
        P(None, ALL), P(ALL, None, None), P(ALL, None, None), P(ALL, None),
        P(ALL, None), P(ALL, None), P(ALL),
    )
    return jax.shard_map(
        functools.partial(body, sizes), mesh=mesh, in_specs=in_specs, out_specs=P(ALL),
        check_vma=False,
    )
```

```python
import functools

import jax
import jax.numpy as jnp
from jax import lax
from jax.experimental import pallas as pl
from jax.experimental.pallas import tpu as pltpu
from jax.sharding import PartitionSpec as P

ALL = ("gx", "gy", "gz")
MESH = pl.DeviceIdType.MESH
SOFT = 0.01
FAR = 64
NEAR = 8
LISTED = FAR + NEAR
PARAMS = 16
LIMIT = 16 * 1024 * 1024
OWN = 16
AWAY = 32
VMEM = pltpu.VMEM
SMEM = pltpu.SMEM


def iota(shape, dim):
    return lax.broadcasted_iota(jnp.int32, shape, dim)


def sorted_lists(nx, nz, cells_per_x, own, ids, counts):
    lane = iota((8, 128), 1)
    sub = iota((8, 128), 0)
    is_far = lane < FAR
    is_near = (lane >= FAR) & (lane < LISTED)
    remote = ids - own
    rank = remote >> 1
    live = lane - FAR < counts
    near_code = sub * 128 + jnp.where(remote >= 0, (rank % nz) * 2 + (remote & 1), ids)
    holder = jnp.where(remote >= 0, rank // nz, nx)
    cell = ids % cells_per_x
    cell = cell - (cell & 63) + ((cell & 7) << 3) + ((cell >> 3) & 7)
    order = jnp.where(is_far, lane, sub * NEAR + lane - FAR)
    key = jnp.where(is_far, ids // cells_per_x, jnp.where(live, holder, nx + 1)) * 64 + order
    far_base, near_base, most_base = LISTED, LISTED + nx + 1, LISTED + 2 * nx + 3
    far_limit = jnp.where((lane >= far_base) & (lane < near_base), (lane - far_base) * 64, 0)
    near_limit = jnp.where((lane >= near_base) & (lane < most_base), (lane - near_base) * 64, 0)
    zero = jnp.zeros((8, 128), jnp.int32)
    far_place, near_place, far_start, near_start = zero, zero, zero, zero
    for e in range(FAR):
        other = jnp.broadcast_to(key[:, e : e + 1], (8, 128))
        far_place += jnp.where(other < key, 1, 0)
        far_start += jnp.where(other < far_limit, 1, 0)
    for e in range(NEAR):
        other = jnp.broadcast_to(key[:, FAR + e : FAR + e + 1], (8, 128))
        near_start += jnp.where(other < near_limit, 1, 0)
        for r in range(8):
            moved = pltpu.roll(other, r, 0) if r else other
            near_place += jnp.where(moved < key, 1, 0)
    both = jnp.where(is_far, far_place * 8192 + cell, near_place * 8192 + near_code)
    far_list, near_list = zero, zero
    for e in range(LISTED):
        entry = jnp.broadcast_to(both[:, e : e + 1], (8, 128))
        term = jnp.where((entry >> 13) == lane, entry & 8191, 0)
        if e < FAR:
            far_list += term
        else:
            near_list += term
    near_list = jnp.broadcast_to(jnp.sum(near_list, axis=0, keepdims=True), (8, 128))
    near_start = jnp.broadcast_to(jnp.sum(near_start, axis=0, keepdims=True), (8, 128))
    near_rows = zero
    for t in range(8):
        near_rows = jnp.where(sub == t, pltpu.roll(near_list, (FAR - 8 * t) % 128, 1), near_rows)
    most = pltpu.roll(far_start, 127, 1) - far_start
    most = jnp.broadcast_to(jnp.max(most, axis=0, keepdims=True), (8, 128))
    most = pltpu.roll(most, most_base - far_base, 1)
    out = jnp.where(is_far, far_list, jnp.where(is_near, near_rows, far_start + near_start))
    return jnp.where(lane >= most_base, most, out)


def cell_row(x, y, z, m):
    lane = iota((8, 128), 1)
    sub = iota((8, 128), 0)

    def total(*v):
        return jnp.sum(sum(p * q for p, q in zip(*v)) if len(v) == 2 else sum(v[0]), axis=1, keepdims=True)

    mass = total(m)
    cx, cy, cz = (total(v, m) / mass for v in (x, y, z))
    dx, dy, dz = ([h - c for h in v] for v, c in ((x, cx), (y, cy), (z, cz)))
    wx, wy, wz = ([h * w for h, w in zip(v, m)] for v in (dx, dy, dz))
    sxx, syy, szz = total(wx, dx), total(wy, dy), total(wz, dz)
    sxy, sxz, syz = total(wx, dy), total(wx, dz), total(wy, dz)
    values = (
        mass, cx, cy, cz, 1.5 * sxx, 1.5 * syy, 1.5 * szz,
        3.0 * sxy, 3.0 * sxz, 3.0 * syz, 0.5 * (sxx + syy + szz),
    )
    spread = jnp.zeros((8, 128), jnp.float32)
    for p, value in enumerate(values):
        spread = jnp.where(lane == sub * PARAMS + p, value, spread)
    return jnp.sum(spread, axis=0, keepdims=True)


def wrap(value, size):
    return value & (size - 1) if size & (size - 1) == 0 else lax.rem(value, size)


def gather_kernel(
    sizes, send_ids_hbm, send_count_hbm, near_count_hbm, far_hbm, near_hbm, tgt_hbm, src_hbm,
    t_all, meta_all, tiles_all, table, local,
    send_ids, send_count, near_count, far, near, tgt,
    src, ids_buf, tbuf, mbuf, obuf, cbuf, cells_all, lists,
    t_send, t_recv, m_send, m_recv, o_send, o_recv, c_send, c_recv, own_sem, list_sem, in_sems,
):
    nx, ny, nz = sizes
    gx, gy, gz = (lax.axis_index(n) for n in ALL)
    own = src.shape[0]
    plane = [(dy, dz) for dy in range(ny) for dz in range(nz) if dy or dz]
    barrier = pltpu.get_barrier_semaphore()
    loads = [
        pltpu.make_async_copy(source, dest, in_sems.at[n])
        for n, (source, dest) in enumerate((
            (send_ids_hbm, send_ids), (send_count_hbm, send_count), (near_count_hbm, near_count),
            (far_hbm, far), (near_hbm, near), (tgt_hbm, tgt), (src_hbm, src),
        ))
    ]
    for load in loads:
        load.start()
    xs = [wrap(gx + d, nx) for d in range(nx)]
    ys = [wrap(gy + d, ny) for d in range(ny)]
    zs = [wrap(gz + d, nz) for d in range(nz)]

    def along_x(d):
        return (xs[d], gy, gz)

    def in_plane(dy, dz):
        return (gx, ys[dy], zs[dz])

    far_first = sorted(range(1, nx), key=lambda d: -min(d, nx - d))
    for d in far_first:
        pl.semaphore_signal(barrier, inc=1, device_id=along_x(d), device_id_type=MESH)
    for dy, dz in plane:
        pl.semaphore_signal(barrier, inc=1, device_id=in_plane(dy, dz), device_id_type=MESH)

    for load in loads[:-1]:
        load.wait()
    for t in range(8):
        for c in range(3):
            tbuf[c, t : t + 1, :] = tgt[t, c : c + 1, :]
    ids_buf[...] = jnp.zeros((8, 128), jnp.int32)
    ids_buf[:, 0:FAR] = far[...]
    ids_buf[:, FAR:LISTED] = near[...]
    sub = iota((8, 128), 0)
    counts = jnp.zeros((8, 128), jnp.int32)
    for t in range(8):
        counts = jnp.where(sub == t, near_count[t], counts)
    mbuf[...] = sorted_lists(nx, nz, ny * nz * own, own, ids_buf[...], counts)
    own_list = pltpu.make_async_copy(mbuf, lists, list_sem)
    own_list.start()
    loads[-1].wait()

    for dz in range(nz):
        k = zs[dz]

        def gather_for(i, carry):
            r = i * nz + k
            filled = send_count[0, r]
            for s in range(2):
                obuf[k, i * 2 + s] = jnp.where(filled > s, src[send_ids[s, r]], 0.0)
            return carry

        lax.fori_loop(0, nx, gather_for, 0, unroll=min(nx, 8))

    pl.semaphore_wait(barrier, nx - 1 + len(plane))

    t_waits, o_waits, c_waits = [], [], []
    for d in far_first:
        for source, dest, s_sem, r_sem in (
            (tbuf, t_all, t_send, t_recv), (mbuf, meta_all, m_send, m_recv)
        ):
            copy = pltpu.make_async_remote_copy(
                src_ref=source, dst_ref=dest.at[gx], send_sem=s_sem.at[d], recv_sem=r_sem.at[d],
                device_id=along_x(d), device_id_type=MESH,
            )
            copy.start()
            t_waits.append(copy)
    for dz in range(1, nz):
        copy = pltpu.make_async_remote_copy(
            src_ref=obuf.at[zs[dz]], dst_ref=tiles_all.at[gz],
            send_sem=o_send.at[dz], recv_sem=o_recv.at[dz],
            device_id=in_plane(0, dz), device_id_type=MESH,
        )
        copy.start()
        o_waits.append(copy)
    mine = pltpu.make_async_copy(obuf.at[gz], tiles_all.at[gz], own_sem)
    mine.start()
    t_all[gx] = tbuf[...]
    meta_all[gx] = mbuf[...]

    def moments(g, carry):
        group = src[pl.ds(g * 8, 8)]
        x, y, z, m = ([group[:, h * 4 + r, :] for h in range(2)] for r in range(4))
        cbuf[pl.ds(g, 1), :] = cell_row(x, y, z, m)
        return carry

    lax.fori_loop(0, own // 8, moments, 0)
    me = gy * nz + gz
    for n, (dy, dz) in enumerate(plane):
        copy = pltpu.make_async_remote_copy(
            src_ref=cbuf, dst_ref=cells_all.at[me], send_sem=c_send.at[n], recv_sem=c_recv.at[n],
            device_id=in_plane(dy, dz), device_id_type=MESH,
        )
        copy.start()
        c_waits.append(copy)
    cells_all[me] = cbuf[...]

    own_list.wait()
    at = LISTED + nx + 1 + nx
    n0, n1 = lists[0, at], lists[0, at + 1]

    def own_item(j, total):
        e = n0 + j
        p = jnp.minimum(e, 8 * NEAR - 1)
        code = lists[p >> 3, FAR + (p & 7)]
        t = code >> 7
        tile = src[jnp.minimum(code & 127, own - 1)]
        row = near_row(tile, *(tbuf[c, pl.ds(t, 1), :] for c in range(3)))
        return total - jnp.where((sub == t) & (e < n1), row, 0.0)

    local[...] = lax.fori_loop(0, OWN, own_item, jnp.zeros((8, 128), jnp.float32), unroll=4)
    for copy in c_waits:
        copy.wait()
    blocks = own // 64

    def expand(n, carry):
        for b in range(blocks):
            cells = cells_all[n, b * 8 : b * 8 + 8, :]
            for j in range(8):
                moved = pltpu.roll(cells, 128 - PARAMS * j, 1) if j else cells
                table[pl.ds((n * blocks + b) * 64 + j * 8, 8), :] = moved
        return carry

    lax.fori_loop(0, ny * nz, expand, 0)
    for copy in t_waits + o_waits:
        copy.wait()
    mine.wait()


def parts(v):
    high = v.astype(jnp.bfloat16).astype(jnp.float32)
    rest = v - high
    mid = rest.astype(jnp.bfloat16).astype(jnp.float32)
    return high, mid, rest - mid


def near_row(tile, x, y, z):
    sub = iota((8, 128), 0)
    left = jnp.concatenate([*parts(tile), jnp.where(sub < 3, 1.0, tile)], axis=0).T
    picks = []
    for c, row in enumerate((x, y, z)):
        high, mid, low = parts(jnp.broadcast_to(-row, (8, 128)))
        target = jnp.where(sub == 0, high, jnp.where(sub == 1, mid, jnp.where(sub == 2, low, 0.0)))
        for h in range(2):
            one = jnp.where(sub == h * 4 + c, 1.0, 0.0)
            picks.append(jnp.concatenate([one, one, one, target], axis=0))
    right = jnp.concatenate(picks, axis=1).astype(jnp.bfloat16)
    d = jnp.dot(left.astype(jnp.bfloat16), right, preferred_element_type=jnp.float32)
    total = jnp.zeros((8, 128), jnp.float32)
    for h in range(2):
        for s in range(0, 128, 8):
            dx, dy, dz = (
                d[s : s + 8, (2 * c + h) * 128 : (2 * c + h + 1) * 128] for c in range(3)
            )
            inv = lax.rsqrt(dx * dx + dy * dy + dz * dz + SOFT)
            total += inv * jnp.broadcast_to(left[s : s + 8, 27 + 4 * h : 28 + 4 * h], (8, 128))
    return jnp.sum(total, axis=0, keepdims=True)


def far_value(p, live, tx, ty, tz):
    dx, dy, dz = tx - p(1), ty - p(2), tz - p(3)
    r2 = dx * dx + dy * dy + dz * dz + SOFT
    inv = lax.rsqrt(r2)
    inv2 = inv * inv
    quad = dx * (p(4) * dx + p(7) * dy + p(8) * dz) + dy * (p(5) * dy + p(9) * dz) + p(6) * dz * dz
    value = inv * (p(0) + (quad - r2 * p(10)) * (inv2 * inv2))
    return jnp.sum(jnp.where(iota((8, 128), 0) < live, value, 0.0), axis=0, keepdims=True)


def walk_kernel(sizes, meta, t_all, tiles, table, src, out, rows, tile_buf, sem):
    nx, ny, nz = sizes
    a = lax.axis_index("gx")
    out[...] = jnp.zeros_like(out)
    near_base = LISTED + nx + 1

    def domain(i, found):
        base = i * 1024
        n0 = meta[base + near_base + a]
        n1 = meta[base + near_base + a + 1]

        @pl.when(meta[base + LISTED + 2 * nx + 3 + a] > 8)
        def _():
            def bucket(t, carry):
                at = base + t * 128
                f0 = meta[at + LISTED + a]
                f1 = meta[at + LISTED + a + 1]
                tx, ty, tz = (t_all[i, c, pl.ds(t, 1), :] for c in range(3))

                def chunk(n, carry):
                    start = f0 + n * 8
                    for u in range(8):
                        rows[u : u + 1, :] = table[pl.ds(meta[at + start + u], 1), :]
                    v = rows[...]
                    p = lambda n: jnp.broadcast_to(v[:, n : n + 1], (8, 128))
                    out[i, pl.ds(t, 1), :] -= far_value(p, f1 - start, tx, ty, tz)
                    return carry

                return lax.fori_loop(1, (f1 - f0 + 7) >> 3, chunk, carry)

            lax.fori_loop(0, 8, bucket, 0)

        def entry(e, carry):
            code = meta[base + ((e >> 3) << 7) + FAR + (e & 7)]
            t = code >> 7
            tile = tiles[((code & 127) >> 1) * (nx * 2) + i * 2 + (code & 1)]
            out[i, pl.ds(t, 1), :] -= near_row(tile, *(t_all[i, c, pl.ds(t, 1), :] for c in range(3)))
            return carry

        lax.fori_loop(jnp.maximum(n0, n0 + AWAY - found), n1, entry, 0)
        return found + n1 - n0

    lax.fori_loop(0, nx, domain, jnp.int32(0))
    base = a * 1024

    def own_entry(e, carry):
        code = meta[base + ((e >> 3) << 7) + FAR + (e & 7)]
        t = code >> 7
        copy = pltpu.make_async_copy(src.at[code & 127], tile_buf, sem)
        copy.start()
        copy.wait()
        row = near_row(tile_buf[...], *(t_all[a, c, pl.ds(t, 1), :] for c in range(3)))
        out[a, pl.ds(t, 1), :] -= row
        return carry

    lax.fori_loop(meta[base + near_base + nx] + OWN, meta[base + near_base + nx + 1], own_entry, 0)


def return_kernel(
    sizes, meta, t_all, tiles, table, part, local,
    out, landed, rows, near_rows, mine, first, last, follow, send, recv,
):
    nx, ny, nz = sizes
    gx, gy, gz = (lax.axis_index(n) for n in ALL)
    barrier = pltpu.get_barrier_semaphore()
    xs = [wrap(gx + d, nx) for d in range(nx)]
    far_first = sorted(range(1, nx), key=lambda d: -min(d, nx - d))
    for d in far_first:
        pl.semaphore_signal(barrier, inc=1, device_id=(xs[d], gy, gz), device_id_type=MESH)
    lane = iota((8, 128), 1)
    sub = iota((8, 128), 0)
    k = iota((128, 128), 0)
    spread = jnp.concatenate(
        [jnp.where(((k & 15) == p) & (k < 48), 1.0, 0.0) for p in range(11)], axis=1
    ).astype(jnp.bfloat16)

    at = LISTED + nx + 1 + gx
    following = jnp.int32(nx)
    for i in reversed(range(nx)):
        n0, n1 = meta[i * 1024 + at], meta[i * 1024 + at + 1]
        first[i] = n0
        last[i] = n1
        follow[i + 1] = following
        following = jnp.where(n1 > n0, i, following)
    first[nx] = 0
    last[nx] = 0
    follow[0] = following

    def near(j, carry):
        i, e, ids = carry
        live = i < nx
        domain = jnp.minimum(i, nx - 1)
        code = meta[domain * 1024 + ((e >> 3) << 7) + FAR + (e & 7)]
        t = (code >> 7) & 7
        tile = tiles[(wrap(code, 2 * nz) >> 1) * (nx * 2) + domain * 2 + (code & 1)]
        near_rows[pl.ds(j, 1), :] = near_row(tile, *(t_all[domain, c, pl.ds(t, 1), :] for c in range(3)))
        ids = jnp.where(lane == j, jnp.where(live, domain * 8 + t, -1), ids)
        more = live & (e + 1 < last[domain])
        next_i = jnp.where(more, i, follow[jnp.minimum(i, nx - 1) + 1])
        next_i = jnp.where(live, next_i, nx)
        return next_i, jnp.where(more, e + 1, first[next_i]), ids

    near_rows[...] = jnp.zeros_like(near_rows)
    start = (follow[0], first[follow[0]], jnp.full((8, 128), -1, jnp.int32))
    _, _, ids = lax.fori_loop(0, AWAY, near, start, unroll=4)
    pick = jnp.where(iota((nx * 8, 128), 0) == jnp.broadcast_to(ids[0:1], (nx * 8, 128)), 1.0, 0.0)
    placed = sum(
        jnp.dot(pick.astype(jnp.bfloat16), v.astype(jnp.bfloat16), preferred_element_type=jnp.float32)
        for v in parts(near_rows[...])
    )
    mine[...] = part[...] - placed.reshape(nx, 8, 128)

    def domain(i, carry):
        bounds = []
        slot = rows.at[i & 1]
        for t in range(8):
            at = i * 1024 + t * 128
            f0 = meta[at + LISTED + gx]
            bounds.append(meta[at + LISTED + gx + 1] - f0)
            for u in range(8):
                slot[t * 8 + u : t * 8 + u + 1, :] = table[pl.ds(meta[at + f0 + u], 1), :]
        high, mid, low = parts(slot[...])
        lane = iota((64, 128), 1)
        packed = jnp.where(
            lane < 16, high, jnp.where(lane < 32, pltpu.roll(mid, 16, 1), pltpu.roll(low, 32, 1))
        )
        wide = jnp.dot(packed.astype(jnp.bfloat16), spread, preferred_element_type=jnp.float32)
        values = []
        for t in range(8):
            tx, ty, tz = (t_all[i, c, t : t + 1, :] for c in range(3))
            p = lambda n: wide[t * 8 : t * 8 + 8, n * 128 : n * 128 + 128]
            values.append(far_value(p, bounds[t], tx, ty, tz))
        mine[i] -= jnp.concatenate(values, axis=0)
        return carry

    lax.fori_loop(0, nx, domain, 0, unroll=2)
    pl.semaphore_wait(barrier, nx - 1)
    copies = []
    for d in far_first:
        copy = pltpu.make_async_remote_copy(
            src_ref=mine.at[xs[d]], dst_ref=landed.at[d - 1],
            send_sem=send.at[d], recv_sem=recv.at[d],
            device_id=(xs[d], gy, gz), device_id_type=MESH,
        )
        copy.start()
        copies.append(copy)
    summed = mine[gx] + local[...]
    for copy in copies:
        copy.wait()
    for d in range(nx - 1):
        summed += landed[d]
    out[...] = summed


def body(sizes, targets, sources, send_ids, send_count, far_ids, near_ids, near_count):
    nx, ny, nz = sizes
    f32, i32 = jnp.float32, jnp.int32
    own = sources.shape[0]
    shape = jax.ShapeDtypeStruct
    vmem = pl.BlockSpec(memory_space=VMEM)
    smem = pl.BlockSpec(memory_space=SMEM)
    hbm = pl.BlockSpec(memory_space=pltpu.HBM)
    dma = pltpu.SemaphoreType.DMA
    in_hbm = functools.partial(pltpu.with_memory_space_constraint, memory_space=pltpu.HBM)
    tgt = jnp.transpose(targets.reshape(3, 8, 128), (1, 0, 2))
    src = jnp.transpose(sources.reshape(own, 4, 2, 128), (0, 2, 1, 3)).reshape(own, 8, 128)
    t_all, meta_all, tiles_all, table, local = pl.pallas_call(
        functools.partial(gather_kernel, sizes),
        out_shape=(
            shape((nx, 3, 8, 128), f32), shape((nx, 8, 128), i32),
            shape((nz, nx * 2, 8, 128), f32), shape((ny * nz * own, 128), f32),
            shape((8, 128), f32),
        ),
        in_specs=[hbm] * 7,
        out_specs=(vmem,) * 5,
        scratch_shapes=[
            SMEM((2, nx * nz), i32), SMEM((1, nx * nz), i32), SMEM((8,), i32),
            VMEM((8, FAR), i32), VMEM((8, NEAR), i32), VMEM((8, 3, 128), f32),
            VMEM((own, 8, 128), f32),
            VMEM((8, 128), i32), VMEM((3, 8, 128), f32), VMEM((8, 128), i32),
            VMEM((nz, nx * 2, 8, 128), f32), VMEM((own // 8, 128), f32),
            VMEM((ny * nz, own // 8, 128), f32), SMEM((8, 128), i32),
            dma((nx,)), dma((nx,)), dma((nx,)), dma((nx,)), dma((nz,)), dma((nz,)),
            dma((ny * nz,)), dma((ny * nz,)), dma, dma, dma((7,)),
        ],
        compiler_params=pltpu.CompilerParams(
            collective_id=0, has_side_effects=True, vmem_limit_bytes=LIMIT
        ),
        name="gather",
    )(*map(in_hbm, (send_ids[0].T, send_count, near_count, far_ids, near_ids, tgt, src)))

    meta = meta_all.reshape(-1)
    tiles = tiles_all.reshape(nz * nx * 2, 8, 128)
    part = pl.pallas_call(
        functools.partial(walk_kernel, sizes),
        out_shape=shape((nx, 8, 128), f32),
        in_specs=[smem, vmem, vmem, vmem, hbm],
        out_specs=vmem,
        scratch_shapes=[VMEM((8, 128), f32), VMEM((8, 128), f32), dma],
        compiler_params=pltpu.CompilerParams(vmem_limit_bytes=LIMIT),
        name="walk",
    )(meta, t_all, tiles, table, in_hbm(src))

    out = pl.pallas_call(
        functools.partial(return_kernel, sizes),
        out_shape=shape((8, 128), f32),
        in_specs=[smem, vmem, vmem, vmem, vmem, vmem],
        out_specs=vmem,
        scratch_shapes=[
            VMEM((nx - 1, 8, 128), f32), VMEM((2, 64, 128), f32), VMEM((128, 128), f32),
            VMEM((nx, 8, 128), f32), SMEM((nx + 1,), i32), SMEM((nx + 1,), i32),
            SMEM((nx + 1,), i32), dma((nx,)), dma((nx,)),
        ],
        compiler_params=pltpu.CompilerParams(
            collective_id=1, has_side_effects=True, vmem_limit_bytes=LIMIT
        ),
        name="bring_back",
    )(meta, t_all, tiles, table, part, local)
    return out.reshape(-1)


def solution(mesh):
    sizes = tuple(mesh.shape[n] for n in ALL)
    in_specs = (
        P(None, ALL), P(ALL, None, None), P(ALL, None, None), P(ALL, None),
        P(ALL, None), P(ALL, None), P(ALL),
    )
    return jax.shard_map(
        functools.partial(body, sizes), mesh=mesh, in_specs=in_specs, out_specs=P(ALL),
        check_vma=False,
    )
```

```python
import functools

import jax
import jax.numpy as jnp
from jax import lax
from jax.experimental import pallas as pl
from jax.experimental.pallas import tpu as pltpu
from jax.sharding import PartitionSpec as P

ALL = ("gx", "gy", "gz")
MESH = pl.DeviceIdType.MESH
SOFT = 0.01
FAR = 64
NEAR = 8
LISTED = FAR + NEAR
PARAMS = 16
LIMIT = 16 * 1024 * 1024
OWN = 16
AWAY = 32
VMEM = pltpu.VMEM
SMEM = pltpu.SMEM


def iota(shape, dim):
    return lax.broadcasted_iota(jnp.int32, shape, dim)


def sorted_lists(nx, nz, cells_per_x, own, ids, counts):
    lane = iota((8, 128), 1)
    sub = iota((8, 128), 0)
    is_far = lane < FAR
    is_near = (lane >= FAR) & (lane < LISTED)
    remote = ids - own
    rank = remote >> 1
    live = lane - FAR < counts
    near_code = sub * 128 + jnp.where(remote >= 0, (rank % nz) * 2 + (remote & 1), ids)
    holder = jnp.where(remote >= 0, rank // nz, nx)
    cell = ids % cells_per_x
    cell = cell - (cell & 63) + ((cell & 7) << 3) + ((cell >> 3) & 7)
    order = jnp.where(is_far, lane, sub * NEAR + lane - FAR)
    key = jnp.where(is_far, ids // cells_per_x, jnp.where(live, holder, nx + 1)) * 64 + order
    far_base, near_base, most_base = LISTED, LISTED + nx + 1, LISTED + 2 * nx + 3
    far_limit = jnp.where((lane >= far_base) & (lane < near_base), (lane - far_base) * 64, 0)
    near_limit = jnp.where((lane >= near_base) & (lane < most_base), (lane - near_base) * 64, 0)
    zero = jnp.zeros((8, 128), jnp.int32)
    far_place, near_place, far_start, near_start = zero, zero, zero, zero
    for e in range(FAR):
        other = jnp.broadcast_to(key[:, e : e + 1], (8, 128))
        far_place += jnp.where(other < key, 1, 0)
        far_start += jnp.where(other < far_limit, 1, 0)
    for e in range(NEAR):
        other = jnp.broadcast_to(key[:, FAR + e : FAR + e + 1], (8, 128))
        near_start += jnp.where(other < near_limit, 1, 0)
        for r in range(8):
            moved = pltpu.roll(other, r, 0) if r else other
            near_place += jnp.where(moved < key, 1, 0)
    both = jnp.where(is_far, far_place * 8192 + cell, near_place * 8192 + near_code)
    far_list, near_list = zero, zero
    for e in range(LISTED):
        entry = jnp.broadcast_to(both[:, e : e + 1], (8, 128))
        term = jnp.where((entry >> 13) == lane, entry & 8191, 0)
        if e < FAR:
            far_list += term
        else:
            near_list += term
    near_list = jnp.broadcast_to(jnp.sum(near_list, axis=0, keepdims=True), (8, 128))
    near_start = jnp.broadcast_to(jnp.sum(near_start, axis=0, keepdims=True), (8, 128))
    near_rows = zero
    for t in range(8):
        near_rows = jnp.where(sub == t, pltpu.roll(near_list, (FAR - 8 * t) % 128, 1), near_rows)
    most = pltpu.roll(far_start, 127, 1) - far_start
    most = jnp.broadcast_to(jnp.max(most, axis=0, keepdims=True), (8, 128))
    most = pltpu.roll(most, most_base - far_base, 1)
    out = jnp.where(is_far, far_list, jnp.where(is_near, near_rows, far_start + near_start))
    return jnp.where(lane >= most_base, most, out)


def cell_row(x, y, z, m):
    lane = iota((8, 128), 1)
    sub = iota((8, 128), 0)

    def total(*v):
        return jnp.sum(sum(p * q for p, q in zip(*v)) if len(v) == 2 else sum(v[0]), axis=1, keepdims=True)

    mass = total(m)
    cx, cy, cz = (total(v, m) / mass for v in (x, y, z))
    dx, dy, dz = ([h - c for h in v] for v, c in ((x, cx), (y, cy), (z, cz)))
    wx, wy, wz = ([h * w for h, w in zip(v, m)] for v in (dx, dy, dz))
    sxx, syy, szz = total(wx, dx), total(wy, dy), total(wz, dz)
    sxy, sxz, syz = total(wx, dy), total(wx, dz), total(wy, dz)
    values = (
        mass, cx, cy, cz, 1.5 * sxx, 1.5 * syy, 1.5 * szz,
        3.0 * sxy, 3.0 * sxz, 3.0 * syz, 0.5 * (sxx + syy + szz),
    )
    spread = jnp.zeros((8, 128), jnp.float32)
    for p, value in enumerate(values):
        spread = jnp.where(lane == sub * PARAMS + p, value, spread)
    return jnp.sum(spread, axis=0, keepdims=True)


def wrap(value, size):
    return value & (size - 1) if size & (size - 1) == 0 else lax.rem(value, size)


def gather_kernel(
    sizes, send_ids_hbm, send_count_hbm, near_count_hbm, far_hbm, near_hbm, tgt_hbm, src_hbm,
    t_all, meta_all, tiles_all, table, local, far_out,
    send_ids, send_count, near_count, far, near, tgt,
    src, ids_buf, tbuf, mbuf, obuf, cbuf, cells_all, rows, meta, own_meta,
    t_send, t_recv, m_send, m_recv, o_send, o_recv, c_send, c_recv, x_send, x_recv,
    own_sem, list_sems, own_list_sem, in_sems,
):
    nx, ny, nz = sizes
    gx, gy, gz = (lax.axis_index(n) for n in ALL)
    own = src.shape[0]
    jump = max(1, nx // 4)
    barrier = pltpu.get_barrier_semaphore()
    loads = [
        pltpu.make_async_copy(source, dest, in_sems.at[n])
        for n, (source, dest) in enumerate((
            (send_ids_hbm, send_ids), (send_count_hbm, send_count), (near_count_hbm, near_count),
            (far_hbm, far), (near_hbm, near), (tgt_hbm, tgt), (src_hbm, src),
        ))
    ]
    for load in loads:
        load.start()
    xs = [wrap(gx + d, nx) for d in range(nx)]
    ys = [wrap(gy + d, ny) for d in range(ny)]
    zs = [wrap(gz + d, nz) for d in range(nz)]
    first = sorted((d for d in range(1, nx) if min(d, nx - d) <= jump), key=lambda d: -min(d, nx - d))
    greeted = [(xs[d], gy, gz) for d in first]
    greeted += [(gx, gy, zs[d]) for d in range(1, nz)]
    greeted += [(gx, ys[d], gz) for d in range(1, ny)]
    for device in greeted:
        pl.semaphore_signal(barrier, inc=1, device_id=device, device_id_type=MESH)

    def sent(source, dest, s_sem, r_sem, device):
        copy = pltpu.make_async_remote_copy(
            src_ref=source, dst_ref=dest, send_sem=s_sem, recv_sem=r_sem,
            device_id=device, device_id_type=MESH,
        )
        copy.start()
        return copy

    def meta_of(ref, i):
        return ref.at[pl.ds(pl.multiple_of(i * 1024, 1024), 1024)]

    for load in loads[:-1]:
        load.wait()
    for t in range(8):
        for c in range(3):
            tbuf[c, t : t + 1, :] = tgt[t, c : c + 1, :]
    ids_buf[...] = jnp.zeros((8, 128), jnp.int32)
    ids_buf[:, 0:FAR] = far[...]
    ids_buf[:, FAR:LISTED] = near[...]
    sub = iota((8, 128), 0)
    counts = jnp.zeros((8, 128), jnp.int32)
    for t in range(8):
        counts = jnp.where(sub == t, near_count[t], counts)
    lists = sorted_lists(nx, nz, ny * nz * own, own, ids_buf[...], counts)
    for t in range(8):
        mbuf[pl.ds(t * 128, 128)] = lists[t]
    to_smem = [pltpu.make_async_copy(mbuf, meta_of(meta, gx), list_sems.at[0])]
    to_smem[0].start()
    own_list = pltpu.make_async_copy(mbuf, own_meta, own_list_sem)
    own_list.start()
    loads[-1].wait()

    for dz in range(nz):
        k = zs[dz]

        def gather_for(i, carry):
            r = i * nz + k
            filled = send_count[0, r]
            for s in range(2):
                obuf[k, i * 2 + s] = jnp.where(filled > s, src[send_ids[s, r]], 0.0)
            return carry

        lax.fori_loop(0, nx, gather_for, 0, unroll=min(nx, 8))

    pl.semaphore_wait(barrier, len(greeted))

    t_copy, m_copy = {}, {}
    for d in first:
        device = (xs[d], gy, gz)
        m_copy[d] = sent(mbuf, meta_of(meta_all, gx), m_send.at[d], m_recv.at[d], device)
        t_copy[d] = sent(tbuf, t_all.at[gx], t_send.at[d], t_recv.at[d], device)
    o_copies = [
        sent(obuf.at[zs[d]], tiles_all.at[gz], o_send.at[d], o_recv.at[d], (gx, gy, zs[d]))
        for d in range(1, nz)
    ]
    mine = pltpu.make_async_copy(obuf.at[gz], tiles_all.at[gz], own_sem)
    mine.start()
    t_all[gx] = tbuf[...]
    meta_all[pl.ds(pl.multiple_of(gx * 1024, 1024), 1024)] = mbuf[...]

    def moments(g, carry):
        group = src[pl.ds(g * 8, 8)]
        x, y, z, m = ([group[:, h * 4 + r, :] for h in range(2)] for r in range(4))
        cbuf[pl.ds(g, 1), :] = cell_row(x, y, z, m)
        return carry

    lax.fori_loop(0, own // 8, moments, 0)
    cells_all[gy, gz] = cbuf[...]
    c_copies = [
        sent(cbuf, cells_all.at[gy, gz], c_send.at[d], c_recv.at[d], (gx, gy, zs[d]))
        for d in range(1, nz)
    ]

    half = nx // 2
    for e in range(1, half - jump + 1):
        up, down = jump + e, nx - jump - e
        for copies, ref, of, s_sems, r_sems in (
            (m_copy, meta_all, meta_of, m_send, m_recv),
            (t_copy, t_all, lambda ref, i: ref.at[i], t_send, t_recv),
        ):
            if e == 1:
                copies[jump].wait_recv()
                copies[nx - jump].wait_recv()
            if e < half - jump or copies is t_copy:
                behind = of(ref, xs[nx - jump])
                copies[up] = sent(behind, behind, s_sems.at[up], r_sems.at[up], (xs[e], gy, gz))
            if e < half - jump or copies is m_copy:
                ahead = of(ref, xs[jump])
                copies[down] = sent(ahead, ahead, s_sems.at[down], r_sems.at[down], (xs[nx - e], gy, gz))

    def listed(d):
        from_d = xs[nx - d]
        copy = pltpu.make_async_copy(meta_of(meta_all, from_d), meta_of(meta, from_d), list_sems.at[d])
        copy.start()
        to_smem.append(copy)

    waited = {jump, nx - jump} if half > jump else set()
    for d in first:
        if d not in waited:
            m_copy[d].wait_recv()
            t_copy[d].wait_recv()
        listed(d)
    for copy in c_copies:
        copy.wait_recv()
    x_copies = [
        sent(cells_all.at[gy], cells_all.at[gy], x_send.at[d], x_recv.at[d], (gx, ys[d], gz))
        for d in range(1, ny)
    ]

    own_list.wait()
    n0 = own_meta[LISTED + nx + 1 + nx]
    n1 = own_meta[LISTED + nx + 1 + nx + 1]

    def own_item(j, total):
        e = n0 + j
        p = jnp.minimum(e, 8 * NEAR - 1)
        code = own_meta[((p >> 3) << 7) + FAR + (p & 7)]
        t = code >> 7
        tile = src[jnp.minimum(code & 127, own - 1)]
        row = near_row(tile, *(tbuf[c, pl.ds(t, 1), :] for c in range(3)))
        return total - jnp.where((sub == t) & (e < n1), row, 0.0)

    local[...] = lax.fori_loop(0, OWN, own_item, jnp.zeros((8, 128), jnp.float32), unroll=4)
    for copy in x_copies:
        copy.wait_recv()
    blocks = own // 64

    def expand(n, carry):
        for b in range(blocks):
            cells = cells_all[n // nz, n % nz, b * 8 : b * 8 + 8, :]
            for j in range(8):
                moved = pltpu.roll(cells, 128 - PARAMS * j, 1) if j else cells
                table[pl.ds((n * blocks + b) * 64 + j * 8, 8), :] = moved
        return carry

    lax.fori_loop(0, ny * nz, expand, 0)

    k = iota((128, 128), 0)
    spread = jnp.concatenate(
        [jnp.where(((k & 15) == p) & (k < 48), 1.0, 0.0) for p in range(11)], axis=1
    ).astype(jnp.bfloat16)

    def far_domain(n, carry):
        i = wrap(gx + n, nx)
        bounds = []
        slot = rows.at[n & 1]
        for t in range(8):
            at = i * 1024 + t * 128
            f0 = meta[at + LISTED + gx]
            bounds.append(meta[at + LISTED + gx + 1] - f0)
            for u in range(8):
                slot[t * 8 + u : t * 8 + u + 1, :] = table[pl.ds(meta[at + f0 + u], 1), :]
        high, mid, low = parts(slot[...])
        lane = iota((64, 128), 1)
        packed = jnp.where(
            lane < 16, high, jnp.where(lane < 32, pltpu.roll(mid, 16, 1), pltpu.roll(low, 32, 1))
        )
        wide = jnp.dot(packed.astype(jnp.bfloat16), spread, preferred_element_type=jnp.float32)
        values = []
        for t in range(8):
            tx, ty, tz = (t_all[i, c, t : t + 1, :] for c in range(3))
            p = lambda n: wide[t * 8 : t * 8 + 8, n * 128 : n * 128 + 128]
            values.append(far_value(p, bounds[t], tx, ty, tz))
        far_out[i] = -jnp.concatenate(values, axis=0)
        return carry

    for copy in to_smem:
        copy.wait()
    to_smem.clear()
    low_end = nx - jump
    near_end = low_end + len(first) + 1
    lax.fori_loop(low_end, near_end, far_domain, 0, unroll=2 if nx > 4 else 1)
    if near_end < low_end + nx:
        for d in range(1, nx):
            if d not in first:
                m_copy[d].wait_recv()
                t_copy[d].wait_recv()
                listed(d)
        for copy in to_smem:
            copy.wait()
        lax.fori_loop(near_end, low_end + nx, far_domain, 0, unroll=2 if nx > 4 else 1)
    for copy in o_copies:
        copy.wait()
    for copy in [*t_copy.values(), *m_copy.values(), *c_copies, *x_copies]:
        copy.wait_send()
    mine.wait()


def parts(v):
    high = v.astype(jnp.bfloat16).astype(jnp.float32)
    rest = v - high
    mid = rest.astype(jnp.bfloat16).astype(jnp.float32)
    return high, mid, rest - mid


def near_row(tile, x, y, z):
    sub = iota((8, 128), 0)
    left = jnp.concatenate([*parts(tile), jnp.where(sub < 3, 1.0, tile)], axis=0).T
    picks = []
    for c, row in enumerate((x, y, z)):
        high, mid, low = parts(jnp.broadcast_to(-row, (8, 128)))
        target = jnp.where(sub == 0, high, jnp.where(sub == 1, mid, jnp.where(sub == 2, low, 0.0)))
        for h in range(2):
            one = jnp.where(sub == h * 4 + c, 1.0, 0.0)
            picks.append(jnp.concatenate([one, one, one, target], axis=0))
    right = jnp.concatenate(picks, axis=1).astype(jnp.bfloat16)
    d = jnp.dot(left.astype(jnp.bfloat16), right, preferred_element_type=jnp.float32)
    total = jnp.zeros((8, 128), jnp.float32)
    for h in range(2):
        for s in range(0, 128, 8):
            dx, dy, dz = (
                d[s : s + 8, (2 * c + h) * 128 : (2 * c + h + 1) * 128] for c in range(3)
            )
            inv = lax.rsqrt(dx * dx + dy * dy + dz * dz + SOFT)
            total += inv * jnp.broadcast_to(left[s : s + 8, 27 + 4 * h : 28 + 4 * h], (8, 128))
    return jnp.sum(total, axis=0, keepdims=True)


def far_value(p, live, tx, ty, tz):
    dx, dy, dz = tx - p(1), ty - p(2), tz - p(3)
    r2 = dx * dx + dy * dy + dz * dz + SOFT
    inv = lax.rsqrt(r2)
    inv2 = inv * inv
    quad = dx * (p(4) * dx + p(7) * dy + p(8) * dz) + dy * (p(5) * dy + p(9) * dz) + p(6) * dz * dz
    value = inv * (p(0) + (quad - r2 * p(10)) * (inv2 * inv2))
    return jnp.sum(jnp.where(iota((8, 128), 0) < live, value, 0.0), axis=0, keepdims=True)


def walk_kernel(sizes, meta, t_all, tiles, table, src, out, rows, tile_buf, sem):
    nx, ny, nz = sizes
    a = lax.axis_index("gx")
    out[...] = jnp.zeros_like(out)
    near_base = LISTED + nx + 1

    def domain(i, found):
        base = i * 1024
        n0 = meta[base + near_base + a]
        n1 = meta[base + near_base + a + 1]

        @pl.when(meta[base + LISTED + 2 * nx + 3 + a] > 8)
        def _():
            def bucket(t, carry):
                at = base + t * 128
                f0 = meta[at + LISTED + a]
                f1 = meta[at + LISTED + a + 1]
                tx, ty, tz = (t_all[i, c, pl.ds(t, 1), :] for c in range(3))

                def chunk(n, carry):
                    start = f0 + n * 8
                    for u in range(8):
                        rows[u : u + 1, :] = table[pl.ds(meta[at + start + u], 1), :]
                    v = rows[...]
                    p = lambda n: jnp.broadcast_to(v[:, n : n + 1], (8, 128))
                    out[i, pl.ds(t, 1), :] -= far_value(p, f1 - start, tx, ty, tz)
                    return carry

                return lax.fori_loop(1, (f1 - f0 + 7) >> 3, chunk, carry)

            lax.fori_loop(0, 8, bucket, 0)

        def entry(e, carry):
            code = meta[base + ((e >> 3) << 7) + FAR + (e & 7)]
            t = code >> 7
            tile = tiles[((code & 127) >> 1) * (nx * 2) + i * 2 + (code & 1)]
            out[i, pl.ds(t, 1), :] -= near_row(tile, *(t_all[i, c, pl.ds(t, 1), :] for c in range(3)))
            return carry

        lax.fori_loop(jnp.maximum(n0, n0 + AWAY - found), n1, entry, 0)
        return found + n1 - n0

    lax.fori_loop(0, nx, domain, jnp.int32(0))
    base = a * 1024

    def own_entry(e, carry):
        code = meta[base + ((e >> 3) << 7) + FAR + (e & 7)]
        t = code >> 7
        copy = pltpu.make_async_copy(src.at[code & 127], tile_buf, sem)
        copy.start()
        copy.wait()
        row = near_row(tile_buf[...], *(t_all[a, c, pl.ds(t, 1), :] for c in range(3)))
        out[a, pl.ds(t, 1), :] -= row
        return carry

    lax.fori_loop(meta[base + near_base + nx] + OWN, meta[base + near_base + nx + 1], own_entry, 0)


def return_kernel(
    sizes, meta, t_all, tiles, part, far_part, local,
    out, landed, near_rows, mine, first, last, follow, send, recv,
):
    nx, ny, nz = sizes
    gx, gy, gz = (lax.axis_index(n) for n in ALL)
    barrier = pltpu.get_barrier_semaphore()
    xs = [wrap(gx + d, nx) for d in range(nx)]
    far_first = sorted(range(1, nx), key=lambda d: -min(d, nx - d))
    for d in far_first:
        pl.semaphore_signal(barrier, inc=1, device_id=(xs[d], gy, gz), device_id_type=MESH)
    lane = iota((8, 128), 1)
    sub = iota((8, 128), 0)

    at = LISTED + nx + 1 + gx
    following = jnp.int32(nx)
    for i in reversed(range(nx)):
        n0, n1 = meta[i * 1024 + at], meta[i * 1024 + at + 1]
        first[i] = n0
        last[i] = n1
        follow[i + 1] = following
        following = jnp.where(n1 > n0, i, following)
    first[nx] = 0
    last[nx] = 0
    follow[0] = following

    def near(j, carry):
        i, e, ids = carry
        live = i < nx
        domain = jnp.minimum(i, nx - 1)
        code = meta[domain * 1024 + ((e >> 3) << 7) + FAR + (e & 7)]
        t = (code >> 7) & 7
        tile = tiles[(wrap(code, 2 * nz) >> 1) * (nx * 2) + domain * 2 + (code & 1)]
        near_rows[pl.ds(j, 1), :] = near_row(tile, *(t_all[domain, c, pl.ds(t, 1), :] for c in range(3)))
        ids = jnp.where(lane == j, jnp.where(live, domain * 8 + t, -1), ids)
        more = live & (e + 1 < last[domain])
        next_i = jnp.where(more, i, follow[jnp.minimum(i, nx - 1) + 1])
        next_i = jnp.where(live, next_i, nx)
        return next_i, jnp.where(more, e + 1, first[next_i]), ids

    near_rows[...] = jnp.zeros_like(near_rows)
    start = (follow[0], first[follow[0]], jnp.full((8, 128), -1, jnp.int32))
    _, _, ids = lax.fori_loop(0, AWAY, near, start, unroll=4)
    pick = jnp.where(iota((nx * 8, 128), 0) == jnp.broadcast_to(ids[0:1], (nx * 8, 128)), 1.0, 0.0)
    placed = sum(
        jnp.dot(pick.astype(jnp.bfloat16), v.astype(jnp.bfloat16), preferred_element_type=jnp.float32)
        for v in parts(near_rows[...])
    )
    mine[...] = part[...] + far_part[...] - placed.reshape(nx, 8, 128)

    pl.semaphore_wait(barrier, nx - 1)
    copies = []
    for d in far_first:
        copy = pltpu.make_async_remote_copy(
            src_ref=mine.at[xs[d]], dst_ref=landed.at[d - 1],
            send_sem=send.at[d], recv_sem=recv.at[d],
            device_id=(xs[d], gy, gz), device_id_type=MESH,
        )
        copy.start()
        copies.append(copy)
    summed = mine[gx] + local[...]
    for copy in copies:
        copy.wait()
    for d in range(nx - 1):
        summed += landed[d]
    out[...] = summed


def body(sizes, targets, sources, send_ids, send_count, far_ids, near_ids, near_count):
    nx, ny, nz = sizes
    f32, i32 = jnp.float32, jnp.int32
    own = sources.shape[0]
    shape = jax.ShapeDtypeStruct
    vmem = pl.BlockSpec(memory_space=VMEM)
    smem = pl.BlockSpec(memory_space=SMEM)
    hbm = pl.BlockSpec(memory_space=pltpu.HBM)
    dma = pltpu.SemaphoreType.DMA
    in_hbm = functools.partial(pltpu.with_memory_space_constraint, memory_space=pltpu.HBM)
    tgt = jnp.transpose(targets.reshape(3, 8, 128), (1, 0, 2))
    src = jnp.transpose(sources.reshape(own, 4, 2, 128), (0, 2, 1, 3)).reshape(own, 8, 128)
    t_all, meta, tiles_all, table, local, far_part = pl.pallas_call(
        functools.partial(gather_kernel, sizes),
        out_shape=(
            shape((nx, 3, 8, 128), f32), shape((nx * 1024,), i32),
            shape((nz, nx * 2, 8, 128), f32), shape((ny * nz * own, 128), f32),
            shape((8, 128), f32), shape((nx, 8, 128), f32),
        ),
        in_specs=[hbm] * 7,
        out_specs=(vmem,) * 6,
        scratch_shapes=[
            SMEM((2, nx * nz), i32), SMEM((1, nx * nz), i32), SMEM((8,), i32),
            VMEM((8, FAR), i32), VMEM((8, NEAR), i32), VMEM((8, 3, 128), f32),
            VMEM((own, 8, 128), f32),
            VMEM((8, 128), i32), VMEM((3, 8, 128), f32), VMEM((1024,), i32),
            VMEM((nz, nx * 2, 8, 128), f32), VMEM((own // 8, 128), f32),
            VMEM((ny, nz, own // 8, 128), f32), VMEM((2, 64, 128), f32),
            SMEM((nx * 1024,), i32), SMEM((1024,), i32),
            dma((nx,)), dma((nx,)), dma((nx,)), dma((nx,)), dma((nz,)), dma((nz,)),
            dma((nz,)), dma((nz,)), dma((ny,)), dma((ny,)), dma, dma((nx,)), dma, dma((7,)),
        ],
        compiler_params=pltpu.CompilerParams(
            collective_id=0, has_side_effects=True, vmem_limit_bytes=LIMIT
        ),
        name="gather",
    )(*map(in_hbm, (send_ids[0].T, send_count, near_count, far_ids, near_ids, tgt, src)))

    tiles = tiles_all.reshape(nz * nx * 2, 8, 128)
    part = pl.pallas_call(
        functools.partial(walk_kernel, sizes),
        out_shape=shape((nx, 8, 128), f32),
        in_specs=[smem, vmem, vmem, vmem, hbm],
        out_specs=vmem,
        scratch_shapes=[VMEM((8, 128), f32), VMEM((8, 128), f32), dma],
        compiler_params=pltpu.CompilerParams(vmem_limit_bytes=LIMIT),
        name="walk",
    )(meta, t_all, tiles, table, in_hbm(src))

    out = pl.pallas_call(
        functools.partial(return_kernel, sizes),
        out_shape=shape((8, 128), f32),
        in_specs=[smem, vmem, vmem, vmem, vmem, vmem],
        out_specs=vmem,
        scratch_shapes=[
            VMEM((nx - 1, 8, 128), f32), VMEM((128, 128), f32),
            VMEM((nx, 8, 128), f32), SMEM((nx + 1,), i32), SMEM((nx + 1,), i32),
            SMEM((nx + 1,), i32), dma((nx,)), dma((nx,)),
        ],
        compiler_params=pltpu.CompilerParams(
            collective_id=1, has_side_effects=True, vmem_limit_bytes=LIMIT
        ),
        name="bring_back",
    )(meta, t_all, tiles, part, far_part, local)
    return out.reshape(-1)


def solution(mesh):
    sizes = tuple(mesh.shape[n] for n in ALL)
    in_specs = (
        P(None, ALL), P(ALL, None, None), P(ALL, None, None), P(ALL, None),
        P(ALL, None), P(ALL, None), P(ALL),
    )
    return jax.shard_map(
        functools.partial(body, sizes), mesh=mesh, in_specs=in_specs, out_specs=P(ALL),
        check_vma=False,
    )
```

```python
import functools

import jax
import jax.numpy as jnp
from jax import lax
from jax.experimental import pallas as pl
from jax.experimental.pallas import tpu as pltpu
from jax.sharding import PartitionSpec as P

ALL = ("gx", "gy", "gz")
MESH = pl.DeviceIdType.MESH
SOFT = 0.01
FAR = 64
NEAR = 8
LISTED = FAR + NEAR
PARAMS = 16
LIMIT = 16 * 1024 * 1024
OWN = 20
AWAY = 28
VMEM = pltpu.VMEM
SMEM = pltpu.SMEM


def iota(shape, dim):
    return lax.broadcasted_iota(jnp.int32, shape, dim)


def sorted_lists(nx, nz, cells_per_x, own, ids, counts):
    lane = iota((8, 128), 1)
    sub = iota((8, 128), 0)
    is_far = lane < FAR
    is_near = (lane >= FAR) & (lane < LISTED)
    remote = ids - own
    rank = remote >> 1
    live = lane - FAR < counts
    near_code = sub * 128 + jnp.where(remote >= 0, (rank % nz) * 2 + (remote & 1), ids)
    holder = jnp.where(remote >= 0, rank // nz, nx)
    cell = ids % cells_per_x
    cell = cell - (cell & 63) + ((cell & 7) << 3) + ((cell >> 3) & 7)
    order = jnp.where(is_far, lane, sub * NEAR + lane - FAR)
    key = jnp.where(is_far, ids // cells_per_x, jnp.where(live, holder, nx + 1)) * 64 + order
    far_base, near_base, most_base = LISTED, LISTED + nx + 1, LISTED + 2 * nx + 3
    far_limit = jnp.where((lane >= far_base) & (lane < near_base), (lane - far_base) * 64, 0)
    near_limit = jnp.where((lane >= near_base) & (lane < most_base), (lane - near_base) * 64, 0)
    zero = jnp.zeros((8, 128), jnp.int32)
    far_place, near_place, far_start, near_start = zero, zero, zero, zero
    for e in range(FAR):
        other = jnp.broadcast_to(key[:, e : e + 1], (8, 128))
        far_place += jnp.where(other < key, 1, 0)
        far_start += jnp.where(other < far_limit, 1, 0)
    for e in range(NEAR):
        other = jnp.broadcast_to(key[:, FAR + e : FAR + e + 1], (8, 128))
        near_start += jnp.where(other < near_limit, 1, 0)
        for r in range(8):
            moved = pltpu.roll(other, r, 0) if r else other
            near_place += jnp.where(moved < key, 1, 0)
    both = jnp.where(is_far, far_place * 8192 + cell, near_place * 8192 + near_code)
    far_list, near_list = zero, zero
    for e in range(LISTED):
        entry = jnp.broadcast_to(both[:, e : e + 1], (8, 128))
        term = jnp.where((entry >> 13) == lane, entry & 8191, 0)
        if e < FAR:
            far_list += term
        else:
            near_list += term
    near_list = jnp.broadcast_to(jnp.sum(near_list, axis=0, keepdims=True), (8, 128))
    near_start = jnp.broadcast_to(jnp.sum(near_start, axis=0, keepdims=True), (8, 128))
    near_rows = zero
    for t in range(8):
        near_rows = jnp.where(sub == t, pltpu.roll(near_list, (FAR - 8 * t) % 128, 1), near_rows)
    most = pltpu.roll(far_start, 127, 1) - far_start
    most = jnp.broadcast_to(jnp.max(most, axis=0, keepdims=True), (8, 128))
    most = pltpu.roll(most, most_base - far_base, 1)
    out = jnp.where(is_far, far_list, jnp.where(is_near, near_rows, far_start + near_start))
    return jnp.where(lane >= most_base, most, out)


def cell_row(x, y, z, m):
    lane = iota((8, 128), 1)
    sub = iota((8, 128), 0)

    def total(*v):
        return jnp.sum(sum(p * q for p, q in zip(*v)) if len(v) == 2 else sum(v[0]), axis=1, keepdims=True)

    mass = total(m)
    cx, cy, cz = (total(v, m) / mass for v in (x, y, z))
    dx, dy, dz = ([h - c for h in v] for v, c in ((x, cx), (y, cy), (z, cz)))
    wx, wy, wz = ([h * w for h, w in zip(v, m)] for v in (dx, dy, dz))
    sxx, syy, szz = total(wx, dx), total(wy, dy), total(wz, dz)
    sxy, sxz, syz = total(wx, dy), total(wx, dz), total(wy, dz)
    values = (
        mass, cx, cy, cz, 1.5 * sxx, 1.5 * syy, 1.5 * szz,
        3.0 * sxy, 3.0 * sxz, 3.0 * syz, 0.5 * (sxx + syy + szz),
    )
    spread = jnp.zeros((8, 128), jnp.float32)
    for p, value in enumerate(values):
        spread = jnp.where(lane == sub * PARAMS + p, value, spread)
    return jnp.sum(spread, axis=0, keepdims=True)


def wrap(value, size):
    return value & (size - 1) if size & (size - 1) == 0 else lax.rem(value, size)


def gather_kernel(
    sizes, send_ids_hbm, send_count_hbm, near_count_hbm, far_hbm, near_hbm, tgt_hbm, src_hbm,
    t_all, meta_all, tiles_all, cnt_all, table, local, far_out,
    send_ids, send_count, cnt_buf, near_count, far, near, tgt,
    src, ids_buf, tbuf, mbuf, obuf, cbuf, cells_all, rows, meta, own_meta,
    t_send, t_recv, m_send, m_recv, o_send, o_recv, c_send, c_recv, x_send, x_recv, n_send, n_recv,
    own_sem, list_sems, own_list_sem, in_sems,
):
    nx, ny, nz = sizes
    gx, gy, gz = (lax.axis_index(n) for n in ALL)
    own = src.shape[0]
    jump = max(1, nx // 4)
    barrier = pltpu.get_barrier_semaphore()
    loads = [
        pltpu.make_async_copy(source, dest, in_sems.at[n])
        for n, (source, dest) in enumerate((
            (send_ids_hbm, send_ids), (send_count_hbm, send_count),
            (send_count_hbm, cnt_buf), (near_count_hbm, near_count),
            (far_hbm, far), (near_hbm, near), (tgt_hbm, tgt), (src_hbm, src),
        ))
    ]
    for load in loads:
        load.start()
    xs = [wrap(gx + d, nx) for d in range(nx)]
    ys = [wrap(gy + d, ny) for d in range(ny)]
    zs = [wrap(gz + d, nz) for d in range(nz)]
    first = sorted((d for d in range(1, nx) if min(d, nx - d) <= jump), key=lambda d: -min(d, nx - d))
    greeted = [(xs[d], gy, gz) for d in first]
    greeted += [(gx, gy, zs[d]) for d in range(1, nz)]
    greeted += [(gx, ys[d], gz) for d in range(1, ny)]
    for device in greeted:
        pl.semaphore_signal(barrier, inc=1, device_id=device, device_id_type=MESH)

    def sent(source, dest, s_sem, r_sem, device):
        copy = pltpu.make_async_remote_copy(
            src_ref=source, dst_ref=dest, send_sem=s_sem, recv_sem=r_sem,
            device_id=device, device_id_type=MESH,
        )
        copy.start()
        return copy

    def meta_of(ref, i):
        return ref.at[pl.ds(pl.multiple_of(i * 1024, 1024), 1024)]

    for load in loads[:-1]:
        load.wait()
    for t in range(8):
        for c in range(3):
            tbuf[c, t : t + 1, :] = tgt[t, c : c + 1, :]
    ids_buf[...] = jnp.zeros((8, 128), jnp.int32)
    ids_buf[:, 0:FAR] = far[...]
    ids_buf[:, FAR:LISTED] = near[...]
    sub = iota((8, 128), 0)
    counts = jnp.zeros((8, 128), jnp.int32)
    for t in range(8):
        counts = jnp.where(sub == t, near_count[t], counts)
    lists = sorted_lists(nx, nz, ny * nz * own, own, ids_buf[...], counts)
    for t in range(8):
        mbuf[pl.ds(t * 128, 128)] = lists[t]
    to_smem = [pltpu.make_async_copy(mbuf, meta_of(meta, gx), list_sems.at[0])]
    to_smem[0].start()
    own_list = pltpu.make_async_copy(mbuf, own_meta, own_list_sem)
    own_list.start()
    loads[-1].wait()

    def moments(g, carry):
        group = src[pl.ds(g * 8, 8)]
        x, y, z, m = ([group[:, h * 4 + r, :] for h in range(2)] for r in range(4))
        cbuf[pl.ds(g, 1), :] = cell_row(x, y, z, m)
        return carry

    lax.fori_loop(0, own // 8, moments, 0, unroll=2)

    def gather_tiles(dz):
        k = zs[dz]

        def gather_for(i, carry):
            r = i * nz + k
            filled = send_count[0, r]
            for s in range(2):
                obuf[k, i * 2 + s] = jnp.where(filled > s, src[send_ids[s, r]], 0.0)
            return carry

        lax.fori_loop(0, nx, gather_for, 0, unroll=min(nx, 8))

    pl.semaphore_wait(barrier, len(greeted))

    t_copy, m_copy = {}, {}
    for d in first:
        device = (xs[d], gy, gz)
        m_copy[d] = sent(mbuf, meta_of(meta_all, gx), m_send.at[d], m_recv.at[d], device)
        t_copy[d] = sent(tbuf, t_all.at[gx], t_send.at[d], t_recv.at[d], device)
    c_copies = [
        sent(cbuf, cells_all.at[gy, gz], c_send.at[d], c_recv.at[d], (gx, gy, zs[d]))
        for d in range(1, nz)
    ]
    c_copies += [
        sent(cnt_buf, cnt_all.at[gz], n_send.at[d], n_recv.at[d], (gx, gy, zs[d]))
        for d in range(1, nz)
    ]
    cells_all[gy, gz] = cbuf[...]
    o_copies = []
    gather_tiles(1)
    for d in range(1, nz):
        gather_tiles((d + 1) % nz)
        o_copies.append(
            sent(obuf.at[zs[d]], tiles_all.at[gz], o_send.at[d], o_recv.at[d], (gx, gy, zs[d]))
        )
    t_all[gx] = tbuf[...]
    meta_all[pl.ds(pl.multiple_of(gx * 1024, 1024), 1024)] = mbuf[...]
    cnt_all[gz] = cnt_buf[...]
    mine = pltpu.make_async_copy(obuf.at[gz], tiles_all.at[gz], own_sem)
    mine.start()

    own_list.wait()
    n0 = own_meta[LISTED + nx + 1 + nx]
    n1 = own_meta[LISTED + nx + 1 + nx + 1]

    def own_item(j, total):
        e = n0 + j
        p = jnp.minimum(e, 8 * NEAR - 1)
        code = own_meta[((p >> 3) << 7) + FAR + (p & 7)]
        t = code >> 7
        tile = src[jnp.minimum(code & 127, own - 1)]
        row = near_row(tile, *(tbuf[c, pl.ds(t, 1), :] for c in range(3)))
        return total - jnp.where((sub == t) & (e < n1), row, 0.0)

    total = lax.fori_loop(0, OWN // 2, own_item, jnp.zeros((8, 128), jnp.float32), unroll=5)
    for copy in c_copies:
        copy.wait_recv()
    x_copies = [
        sent(cells_all.at[gy], cells_all.at[gy], x_send.at[d], x_recv.at[d], (gx, ys[d], gz))
        for d in range(1, ny)
    ]
    local[...] = lax.fori_loop(OWN // 2, OWN, own_item, total, unroll=5)

    half = nx // 2
    for e in range(1, half - jump + 1):
        up, down = jump + e, nx - jump - e
        for copies, ref, of, s_sems, r_sems in (
            (m_copy, meta_all, meta_of, m_send, m_recv),
            (t_copy, t_all, lambda ref, i: ref.at[i], t_send, t_recv),
        ):
            if e == 1:
                copies[jump].wait_recv()
                copies[nx - jump].wait_recv()
            if e < half - jump or copies is t_copy:
                behind = of(ref, xs[nx - jump])
                copies[up] = sent(behind, behind, s_sems.at[up], r_sems.at[up], (xs[e], gy, gz))
            if e < half - jump or copies is m_copy:
                ahead = of(ref, xs[jump])
                copies[down] = sent(ahead, ahead, s_sems.at[down], r_sems.at[down], (xs[nx - e], gy, gz))

    def listed(d):
        from_d = xs[nx - d]
        copy = pltpu.make_async_copy(meta_of(meta_all, from_d), meta_of(meta, from_d), list_sems.at[d])
        copy.start()
        to_smem.append(copy)

    waited = {jump, nx - jump} if half > jump else set()
    for d in first:
        if d not in waited:
            m_copy[d].wait_recv()
            t_copy[d].wait_recv()
        listed(d)
    for copy in x_copies:
        copy.wait_recv()
    blocks = own // 64

    def expand(n, carry):
        for b in range(blocks):
            cells = cells_all[n // nz, n % nz, b * 8 : b * 8 + 8, :]
            for j in range(8):
                moved = pltpu.roll(cells, 128 - PARAMS * j, 1) if j else cells
                table[pl.ds((n * blocks + b) * 64 + j * 8, 8), :] = moved
        return carry

    lax.fori_loop(0, ny * nz, expand, 0, unroll=4)

    k = iota((128, 128), 0)
    spread = jnp.concatenate(
        [jnp.where(((k & 15) == p) & (k < 48), 1.0, 0.0) for p in range(11)], axis=1
    ).astype(jnp.bfloat16)

    def far_domain(n, carry):
        i = wrap(gx + n, nx)
        bounds = []
        slot = rows.at[n & 1]
        for t in range(8):
            at = i * 1024 + t * 128
            f0 = meta[at + LISTED + gx]
            bounds.append(meta[at + LISTED + gx + 1] - f0)
            for u in range(8):
                slot[t * 8 + u : t * 8 + u + 1, :] = table[pl.ds(meta[at + f0 + u], 1), :]
        high, mid, low = parts(slot[...])
        lane = iota((64, 128), 1)
        packed = jnp.where(
            lane < 16, high, jnp.where(lane < 32, pltpu.roll(mid, 16, 1), pltpu.roll(low, 32, 1))
        )
        wide = jnp.dot(packed.astype(jnp.bfloat16), spread, preferred_element_type=jnp.float32)
        values = []
        for t in range(8):
            tx, ty, tz = (t_all[i, c, t : t + 1, :] for c in range(3))
            p = lambda n: wide[t * 8 : t * 8 + 8, n * 128 : n * 128 + 128]
            values.append(far_value(p, bounds[t], tx, ty, tz))
        far_out[i] = -jnp.concatenate(values, axis=0)
        return carry

    for copy in to_smem:
        copy.wait()
    to_smem.clear()
    low_end = nx - jump
    near_end = low_end + len(first) + 1
    lax.fori_loop(low_end, near_end, far_domain, 0, unroll=2 if nx > 4 else 1)
    if near_end < low_end + nx:
        for d in range(1, nx):
            if d not in first:
                m_copy[d].wait_recv()
                t_copy[d].wait_recv()
                listed(d)
        for copy in to_smem:
            copy.wait()
        lax.fori_loop(near_end, low_end + nx, far_domain, 0, unroll=2 if nx > 4 else 1)
    for copy in o_copies:
        copy.wait()
    for copy in [*t_copy.values(), *m_copy.values(), *c_copies, *x_copies]:
        copy.wait_send()
    mine.wait()


def parts(v):
    high = v.astype(jnp.bfloat16).astype(jnp.float32)
    rest = v - high
    mid = rest.astype(jnp.bfloat16).astype(jnp.float32)
    return high, mid, rest - mid


def near_row(tile, x, y, z):
    sub = iota((8, 128), 0)
    left = jnp.concatenate([*parts(tile), jnp.where(sub < 3, 1.0, tile)], axis=0).T
    picks = []
    for c, row in enumerate((x, y, z)):
        high, mid, low = parts(jnp.broadcast_to(-row, (8, 128)))
        target = jnp.where(sub == 0, high, jnp.where(sub == 1, mid, jnp.where(sub == 2, low, 0.0)))
        for h in range(2):
            one = jnp.where(sub == h * 4 + c, 1.0, 0.0)
            picks.append(jnp.concatenate([one, one, one, target], axis=0))
    right = jnp.concatenate(picks, axis=1).astype(jnp.bfloat16)
    d = jnp.dot(left.astype(jnp.bfloat16), right, preferred_element_type=jnp.float32)
    total = jnp.zeros((8, 128), jnp.float32)
    for h in range(2):
        for s in range(0, 128, 8):
            dx, dy, dz = (
                d[s : s + 8, (2 * c + h) * 128 : (2 * c + h + 1) * 128] for c in range(3)
            )
            inv = lax.rsqrt(dx * dx + dy * dy + dz * dz + SOFT)
            total += inv * jnp.broadcast_to(left[s : s + 8, 27 + 4 * h : 28 + 4 * h], (8, 128))
    return jnp.sum(total, axis=0, keepdims=True)


def far_value(p, live, tx, ty, tz):
    dx, dy, dz = tx - p(1), ty - p(2), tz - p(3)
    r2 = dx * dx + dy * dy + dz * dz + SOFT
    inv = lax.rsqrt(r2)
    inv2 = inv * inv
    quad = dx * (p(4) * dx + p(7) * dy + p(8) * dz) + dy * (p(5) * dy + p(9) * dz) + p(6) * dz * dz
    value = inv * (p(0) + (quad - r2 * p(10)) * (inv2 * inv2))
    return jnp.sum(jnp.where(iota((8, 128), 0) < live, value, 0.0), axis=0, keepdims=True)


def walk_kernel(
    sizes, meta, cnt, t_all, tiles, table, src, out, todo, rows, tile_buf, sem
):
    nx, ny, nz = sizes
    a = lax.axis_index("gx")
    gz = lax.axis_index("gz")
    out[...] = jnp.zeros_like(out)
    near_base = LISTED + nx + 1

    def domain(i, found):
        base = i * 1024
        n0 = meta[base + near_base + a]
        n1 = meta[base + near_base + a + 1]

        @pl.when(meta[base + LISTED + 2 * nx + 3 + a] > 8)
        def _():
            def bucket(t, carry):
                at = base + t * 128
                f0 = meta[at + LISTED + a]
                f1 = meta[at + LISTED + a + 1]
                tx, ty, tz = (t_all[i, c, pl.ds(t, 1), :] for c in range(3))

                def chunk(n, carry):
                    start = f0 + n * 8
                    for u in range(8):
                        rows[u : u + 1, :] = table[pl.ds(meta[at + start + u], 1), :]
                    v = rows[...]
                    p = lambda n: jnp.broadcast_to(v[:, n : n + 1], (8, 128))
                    out[i, pl.ds(t, 1), :] -= far_value(p, f1 - start, tx, ty, tz)
                    return carry

                return lax.fori_loop(1, (f1 - f0 + 7) >> 3, chunk, carry)

            lax.fori_loop(0, 8, bucket, 0)

        def entry(e, found):
            code = meta[base + ((e >> 3) << 7) + FAR + (e & 7)]
            peer, slot = (code & 127) >> 1, code & 1
            todo[found] = (i * 8 + (code >> 7)) * 1024 + peer * (nx * 2) + i * 2 + slot
            return found + jnp.where(cnt[peer * (nx * nz) + i * nz + gz] > slot, 1, 0)

        return lax.fori_loop(n0, n1, entry, found)

    found = lax.fori_loop(0, nx, domain, jnp.int32(0))
    todo[nx * 64 + 1] = found

    def away(n, carry):
        item = todo[n]
        i, t = item >> 13, (item >> 10) & 7
        row = near_row(tiles[item & 1023], *(t_all[i, c, pl.ds(t, 1), :] for c in range(3)))
        out[i, pl.ds(t, 1), :] -= row
        return carry

    lax.fori_loop(AWAY, found, away, 0)
    base = a * 1024

    def own_entry(e, carry):
        code = meta[base + ((e >> 3) << 7) + FAR + (e & 7)]
        t = code >> 7
        copy = pltpu.make_async_copy(src.at[code & 127], tile_buf, sem)
        copy.start()
        copy.wait()
        row = near_row(tile_buf[...], *(t_all[a, c, pl.ds(t, 1), :] for c in range(3)))
        out[a, pl.ds(t, 1), :] -= row
        return carry

    lax.fori_loop(meta[base + near_base + nx] + OWN, meta[base + near_base + nx + 1], own_entry, 0)


def return_kernel(
    sizes, todo, t_all, tiles, part, far_part, local, out, landed, near_rows, mine, send, recv,
):
    nx, ny, nz = sizes
    gx, gy, gz = (lax.axis_index(n) for n in ALL)
    barrier = pltpu.get_barrier_semaphore()
    xs = [wrap(gx + d, nx) for d in range(nx)]
    far_first = sorted(range(1, nx), key=lambda d: -min(d, nx - d))
    for d in far_first:
        pl.semaphore_signal(barrier, inc=1, device_id=(xs[d], gy, gz), device_id_type=MESH)
    lane = iota((8, 128), 1)
    found = todo[nx * 64 + 1]

    def near(j, ids):
        item = jnp.where(j < found, todo[j], 0)
        bucket = item >> 10
        i, t = bucket >> 3, bucket & 7
        row = near_row(tiles[item & 1023], *(t_all[i, c, pl.ds(t, 1), :] for c in range(3)))
        near_rows[pl.ds(j, 1), :] = row
        return jnp.where(lane == j, jnp.where(j < found, bucket, -1), ids)

    near_rows[...] = jnp.zeros_like(near_rows)
    ids = lax.fori_loop(0, AWAY, near, jnp.full((8, 128), -1, jnp.int32), unroll=4)
    pick = jnp.where(iota((nx * 8, 128), 0) == jnp.broadcast_to(ids[0:1], (nx * 8, 128)), 1.0, 0.0)
    placed = sum(
        jnp.dot(pick.astype(jnp.bfloat16), v.astype(jnp.bfloat16), preferred_element_type=jnp.float32)
        for v in parts(near_rows[...])
    )
    mine[...] = part[...] + far_part[...] - placed.reshape(nx, 8, 128)

    pl.semaphore_wait(barrier, nx - 1)
    copies = []
    for d in far_first:
        copy = pltpu.make_async_remote_copy(
            src_ref=mine.at[xs[d]], dst_ref=landed.at[d - 1],
            send_sem=send.at[d], recv_sem=recv.at[d],
            device_id=(xs[d], gy, gz), device_id_type=MESH,
        )
        copy.start()
        copies.append(copy)
    summed = mine[gx] + local[...]
    for copy in copies:
        copy.wait()
    for d in range(nx - 1):
        summed += landed[d]
    out[...] = summed


def body(sizes, targets, sources, send_ids, send_count, far_ids, near_ids, near_count):
    nx, ny, nz = sizes
    f32, i32 = jnp.float32, jnp.int32
    own = sources.shape[0]
    shape = jax.ShapeDtypeStruct
    vmem = pl.BlockSpec(memory_space=VMEM)
    smem = pl.BlockSpec(memory_space=SMEM)
    hbm = pl.BlockSpec(memory_space=pltpu.HBM)
    dma = pltpu.SemaphoreType.DMA
    in_hbm = functools.partial(pltpu.with_memory_space_constraint, memory_space=pltpu.HBM)
    tgt = jnp.transpose(targets.reshape(3, 8, 128), (1, 0, 2))
    src = jnp.transpose(sources.reshape(own, 4, 2, 128), (0, 2, 1, 3)).reshape(own, 8, 128)
    t_all, meta, tiles_all, cnt, table, local, far_part = pl.pallas_call(
        functools.partial(gather_kernel, sizes),
        out_shape=(
            shape((nx, 3, 8, 128), f32), shape((nx * 1024,), i32),
            shape((nz, nx * 2, 8, 128), f32), shape((nz, 1, nx * nz), i32),
            shape((ny * nz * own, 128), f32),
            shape((8, 128), f32), shape((nx, 8, 128), f32),
        ),
        in_specs=[hbm] * 7,
        out_specs=(vmem,) * 7,
        scratch_shapes=[
            SMEM((2, nx * nz), i32), SMEM((1, nx * nz), i32), VMEM((1, nx * nz), i32),
            SMEM((8,), i32),
            VMEM((8, FAR), i32), VMEM((8, NEAR), i32), VMEM((8, 3, 128), f32),
            VMEM((own, 8, 128), f32),
            VMEM((8, 128), i32), VMEM((3, 8, 128), f32), VMEM((1024,), i32),
            VMEM((nz, nx * 2, 8, 128), f32), VMEM((own // 8, 128), f32),
            VMEM((ny, nz, own // 8, 128), f32), VMEM((2, 64, 128), f32),
            SMEM((nx * 1024,), i32), SMEM((1024,), i32),
            dma((nx,)), dma((nx,)), dma((nx,)), dma((nx,)), dma((nz,)), dma((nz,)),
            dma((nz,)), dma((nz,)), dma((ny,)), dma((ny,)), dma((nz,)), dma((nz,)),
            dma, dma((nx,)), dma, dma((8,)),
        ],
        compiler_params=pltpu.CompilerParams(
            collective_id=0, has_side_effects=True, vmem_limit_bytes=LIMIT
        ),
        name="gather",
    )(*map(in_hbm, (send_ids[0].T, send_count, near_count, far_ids, near_ids, tgt, src)))

    tiles = tiles_all.reshape(nz * nx * 2, 8, 128)
    part, todo = pl.pallas_call(
        functools.partial(walk_kernel, sizes),
        out_shape=(shape((nx, 8, 128), f32), shape((nx * 64 + 2,), i32)),
        in_specs=[smem, smem, vmem, vmem, vmem, hbm],
        out_specs=(vmem, smem),
        scratch_shapes=[VMEM((8, 128), f32), VMEM((8, 128), f32), dma],
        compiler_params=pltpu.CompilerParams(vmem_limit_bytes=LIMIT),
        name="walk",
    )(meta, cnt.reshape(-1), t_all, tiles, table, in_hbm(src))

    out = pl.pallas_call(
        functools.partial(return_kernel, sizes),
        out_shape=shape((8, 128), f32),
        in_specs=[smem, vmem, vmem, vmem, vmem, vmem],
        out_specs=vmem,
        scratch_shapes=[
            VMEM((nx - 1, 8, 128), f32), VMEM((128, 128), f32),
            VMEM((nx, 8, 128), f32), dma((nx,)), dma((nx,)),
        ],
        compiler_params=pltpu.CompilerParams(
            collective_id=1, has_side_effects=True, vmem_limit_bytes=LIMIT
        ),
        name="bring_back",
    )(todo, t_all, tiles, part, far_part, local)
    return out.reshape(-1)


def solution(mesh):
    sizes = tuple(mesh.shape[n] for n in ALL)
    in_specs = (
        P(None, ALL), P(ALL, None, None), P(ALL, None, None), P(ALL, None),
        P(ALL, None), P(ALL, None), P(ALL),
    )
    return jax.shard_map(
        functools.partial(body, sizes), mesh=mesh, in_specs=in_specs, out_specs=P(ALL),
        check_vma=False,
    )
```

```python
import functools

import jax
import jax.numpy as jnp
from jax import lax
from jax.experimental import pallas as pl
from jax.experimental.pallas import tpu as pltpu
from jax.sharding import PartitionSpec as P

ALL = ("gx", "gy", "gz")
MESH = pl.DeviceIdType.MESH
SOFT = 0.01
FAR = 64
NEAR = 8
LISTED = FAR + NEAR
PARAMS = 16
LIMIT = 16 * 1024 * 1024
OWN = 24
AWAY = 28
VMEM = pltpu.VMEM
SMEM = pltpu.SMEM


def iota(shape, dim):
    return lax.broadcasted_iota(jnp.int32, shape, dim)


def sorted_lists(nx, nz, cells_per_x, own, ids, counts):
    lane = iota((8, 128), 1)
    sub = iota((8, 128), 0)
    is_far = lane < FAR
    is_near = (lane >= FAR) & (lane < LISTED)
    remote = ids - own
    rank = remote >> 1
    live = lane - FAR < counts
    near_code = sub * 128 + jnp.where(remote >= 0, (rank % nz) * 2 + (remote & 1), ids)
    holder = jnp.where(remote >= 0, rank // nz, nx)
    cell = ids % cells_per_x
    cell = cell - (cell & 63) + ((cell & 7) << 3) + ((cell >> 3) & 7)
    order = jnp.where(is_far, lane, sub * NEAR + lane - FAR)
    key = jnp.where(is_far, ids // cells_per_x, jnp.where(live, holder, nx + 1)) * 64 + order
    far_base, near_base, most_base = LISTED, LISTED + nx + 1, LISTED + 2 * nx + 3
    far_limit = jnp.where((lane >= far_base) & (lane < near_base), (lane - far_base) * 64, 0)
    near_limit = jnp.where((lane >= near_base) & (lane < most_base), (lane - near_base) * 64, 0)
    zero = jnp.zeros((8, 128), jnp.int32)
    far_place, near_place, far_start, near_start = zero, zero, zero, zero
    for e in range(FAR):
        other = jnp.broadcast_to(key[:, e : e + 1], (8, 128))
        far_place += jnp.where(other < key, 1, 0)
        far_start += jnp.where(other < far_limit, 1, 0)
    for e in range(NEAR):
        other = jnp.broadcast_to(key[:, FAR + e : FAR + e + 1], (8, 128))
        near_start += jnp.where(other < near_limit, 1, 0)
        for r in range(8):
            moved = pltpu.roll(other, r, 0) if r else other
            near_place += jnp.where(moved < key, 1, 0)
    both = jnp.where(is_far, far_place * 8192 + cell, near_place * 8192 + near_code)
    far_list, near_list = zero, zero
    for e in range(LISTED):
        entry = jnp.broadcast_to(both[:, e : e + 1], (8, 128))
        term = jnp.where((entry >> 13) == lane, entry & 8191, 0)
        if e < FAR:
            far_list += term
        else:
            near_list += term
    near_list = jnp.broadcast_to(jnp.sum(near_list, axis=0, keepdims=True), (8, 128))
    near_start = jnp.broadcast_to(jnp.sum(near_start, axis=0, keepdims=True), (8, 128))
    near_rows = zero
    for t in range(8):
        near_rows = jnp.where(sub == t, pltpu.roll(near_list, (FAR - 8 * t) % 128, 1), near_rows)
    most = pltpu.roll(far_start, 127, 1) - far_start
    most = jnp.broadcast_to(jnp.max(most, axis=0, keepdims=True), (8, 128))
    most = pltpu.roll(most, most_base - far_base, 1)
    out = jnp.where(is_far, far_list, jnp.where(is_near, near_rows, far_start + near_start))
    return jnp.where(lane >= most_base, most, out)


def cell_row(x, y, z, m):
    lane = iota((8, 128), 1)
    sub = iota((8, 128), 0)

    def total(*v):
        return jnp.sum(sum(p * q for p, q in zip(*v)) if len(v) == 2 else sum(v[0]), axis=1, keepdims=True)

    mass = total(m)
    cx, cy, cz = (total(v, m) / mass for v in (x, y, z))
    dx, dy, dz = ([h - c for h in v] for v, c in ((x, cx), (y, cy), (z, cz)))
    wx, wy, wz = ([h * w for h, w in zip(v, m)] for v in (dx, dy, dz))
    sxx, syy, szz = total(wx, dx), total(wy, dy), total(wz, dz)
    sxy, sxz, syz = total(wx, dy), total(wx, dz), total(wy, dz)
    values = (
        mass, cx, cy, cz, 1.5 * sxx, 1.5 * syy, 1.5 * szz,
        3.0 * sxy, 3.0 * sxz, 3.0 * syz, 0.5 * (sxx + syy + szz),
    )
    spread = jnp.zeros((8, 128), jnp.float32)
    for p, value in enumerate(values):
        spread = jnp.where(lane == sub * PARAMS + p, value, spread)
    return jnp.sum(spread, axis=0, keepdims=True)


def wrap(value, size):
    return value & (size - 1) if size & (size - 1) == 0 else lax.rem(value, size)


def gather_kernel(
    sizes, send_ids_hbm, send_count_hbm, near_count_hbm, far_hbm, near_hbm, tgt_hbm, src_hbm,
    t_all, meta_all, tiles_all, cnt_all, table, far_out, mbuf, src,
    send_ids, send_count, cnt_buf, near_count, far, near, tgt,
    ids_buf, tbuf, obuf, cbuf, cells_all, rows, meta,
    t_send, t_recv, m_send, m_recv, o_send, o_recv, c_send, c_recv, x_send, x_recv, n_send, n_recv,
    own_sem, list_sems, in_sems,
):
    nx, ny, nz = sizes
    gx, gy, gz = (lax.axis_index(n) for n in ALL)
    own = src.shape[0]
    jump = max(1, nx // 4)
    barrier = pltpu.get_barrier_semaphore()
    loads = [
        pltpu.make_async_copy(source, dest, in_sems.at[n])
        for n, (source, dest) in enumerate((
            (send_ids_hbm, send_ids), (send_count_hbm, send_count),
            (send_count_hbm, cnt_buf), (near_count_hbm, near_count),
            (far_hbm, far), (near_hbm, near), (tgt_hbm, tgt), (src_hbm, src),
        ))
    ]
    for load in loads:
        load.start()
    xs = [wrap(gx + d, nx) for d in range(nx)]
    ys = [wrap(gy + d, ny) for d in range(ny)]
    zs = [wrap(gz + d, nz) for d in range(nz)]
    first = sorted((d for d in range(1, nx) if min(d, nx - d) <= jump), key=lambda d: -min(d, nx - d))
    greeted = [(xs[d], gy, gz) for d in first]
    greeted += [(gx, gy, zs[d]) for d in range(1, nz)]
    greeted += [(gx, ys[d], gz) for d in range(1, ny)]
    for device in greeted:
        pl.semaphore_signal(barrier, inc=1, device_id=device, device_id_type=MESH)

    def sent(source, dest, s_sem, r_sem, device):
        copy = pltpu.make_async_remote_copy(
            src_ref=source, dst_ref=dest, send_sem=s_sem, recv_sem=r_sem,
            device_id=device, device_id_type=MESH,
        )
        copy.start()
        return copy

    def meta_of(ref, i):
        return ref.at[pl.ds(pl.multiple_of(i * 1024, 1024), 1024)]

    for load in loads[:-1]:
        load.wait()
    for t in range(8):
        for c in range(3):
            tbuf[c, t : t + 1, :] = tgt[t, c : c + 1, :]
    ids_buf[...] = jnp.zeros((8, 128), jnp.int32)
    ids_buf[:, 0:FAR] = far[...]
    ids_buf[:, FAR:LISTED] = near[...]
    sub = iota((8, 128), 0)
    counts = jnp.zeros((8, 128), jnp.int32)
    for t in range(8):
        counts = jnp.where(sub == t, near_count[t], counts)
    lists = sorted_lists(nx, nz, ny * nz * own, own, ids_buf[...], counts)
    for t in range(8):
        mbuf[pl.ds(t * 128, 128)] = lists[t]
    to_smem = [pltpu.make_async_copy(mbuf, meta_of(meta, gx), list_sems.at[0])]
    to_smem[0].start()
    loads[-1].wait()

    def moments(g, carry):
        group = src[pl.ds(g * 8, 8)]
        x, y, z, m = ([group[:, h * 4 + r, :] for h in range(2)] for r in range(4))
        cbuf[pl.ds(g, 1), :] = cell_row(x, y, z, m)
        return carry

    lax.fori_loop(0, own // 8, moments, 0, unroll=2)

    def gather_tiles(dz):
        k = zs[dz]

        def gather_for(i, carry):
            r = i * nz + k
            filled = send_count[0, r]
            for s in range(2):
                obuf[k, i * 2 + s] = jnp.where(filled > s, src[send_ids[s, r]], 0.0)
            return carry

        lax.fori_loop(0, nx, gather_for, 0, unroll=min(nx, 8))

    pl.semaphore_wait(barrier, len(greeted))

    t_copy, m_copy = {}, {}
    for d in first:
        device = (xs[d], gy, gz)
        m_copy[d] = sent(mbuf, meta_of(meta_all, gx), m_send.at[d], m_recv.at[d], device)
        t_copy[d] = sent(tbuf, t_all.at[gx], t_send.at[d], t_recv.at[d], device)
    c_copies = [
        sent(cbuf, cells_all.at[gy, gz], c_send.at[d], c_recv.at[d], (gx, gy, zs[d]))
        for d in range(1, nz)
    ]
    c_copies += [
        sent(cnt_buf, cnt_all.at[gz], n_send.at[d], n_recv.at[d], (gx, gy, zs[d]))
        for d in range(1, nz)
    ]
    cells_all[gy, gz] = cbuf[...]
    o_copies = []
    gather_tiles(1)
    for d in range(1, nz):
        gather_tiles((d + 1) % nz)
        o_copies.append(
            sent(obuf.at[zs[d]], tiles_all.at[gz], o_send.at[d], o_recv.at[d], (gx, gy, zs[d]))
        )
    t_all[gx] = tbuf[...]
    meta_all[pl.ds(pl.multiple_of(gx * 1024, 1024), 1024)] = mbuf[...]
    cnt_all[gz] = cnt_buf[...]
    mine = pltpu.make_async_copy(obuf.at[gz], tiles_all.at[gz], own_sem)
    mine.start()

    for copy in c_copies:
        copy.wait_recv()
    x_copies = [
        sent(cells_all.at[gy], cells_all.at[gy], x_send.at[d], x_recv.at[d], (gx, ys[d], gz))
        for d in range(1, ny)
    ]

    half = nx // 2
    for e in range(1, half - jump + 1):
        up, down = jump + e, nx - jump - e
        for copies, ref, of, s_sems, r_sems in (
            (m_copy, meta_all, meta_of, m_send, m_recv),
            (t_copy, t_all, lambda ref, i: ref.at[i], t_send, t_recv),
        ):
            if e == 1:
                copies[jump].wait_recv()
                copies[nx - jump].wait_recv()
            if e < half - jump or copies is t_copy:
                behind = of(ref, xs[nx - jump])
                copies[up] = sent(behind, behind, s_sems.at[up], r_sems.at[up], (xs[e], gy, gz))
            if e < half - jump or copies is m_copy:
                ahead = of(ref, xs[jump])
                copies[down] = sent(ahead, ahead, s_sems.at[down], r_sems.at[down], (xs[nx - e], gy, gz))

    def listed(d):
        from_d = xs[nx - d]
        copy = pltpu.make_async_copy(meta_of(meta_all, from_d), meta_of(meta, from_d), list_sems.at[d])
        copy.start()
        to_smem.append(copy)

    waited = {jump, nx - jump} if half > jump else set()
    for d in first:
        if d not in waited:
            m_copy[d].wait_recv()
            t_copy[d].wait_recv()
        listed(d)
    for copy in x_copies:
        copy.wait_recv()
    blocks = own // 64

    def expand(n, carry):
        for b in range(blocks):
            cells = cells_all[n // nz, n % nz, b * 8 : b * 8 + 8, :]
            for j in range(8):
                moved = pltpu.roll(cells, 128 - PARAMS * j, 1) if j else cells
                table[pl.ds((n * blocks + b) * 64 + j * 8, 8), :] = moved
        return carry

    lax.fori_loop(0, ny * nz, expand, 0, unroll=4)

    k = iota((128, 128), 0)
    spread = jnp.concatenate(
        [jnp.where(((k & 15) == p) & (k < 48), 1.0, 0.0) for p in range(11)], axis=1
    ).astype(jnp.bfloat16)

    def far_domain(n, carry):
        i = wrap(gx + n, nx)
        bounds = []
        slot = rows.at[n & 3]
        for t in range(8):
            at = i * 1024 + t * 128
            f0 = meta[at + LISTED + gx]
            bounds.append(meta[at + LISTED + gx + 1] - f0)
            for u in range(8):
                slot[t * 8 + u : t * 8 + u + 1, :] = table[pl.ds(meta[at + f0 + u], 1), :]
        high, mid, low = parts(slot[...])
        lane = iota((64, 128), 1)
        packed = jnp.where(
            lane < 16, high, jnp.where(lane < 32, pltpu.roll(mid, 16, 1), pltpu.roll(low, 32, 1))
        )
        wide = jnp.dot(packed.astype(jnp.bfloat16), spread, preferred_element_type=jnp.float32)
        values = []
        for t in range(8):
            tx, ty, tz = (t_all[i, c, t : t + 1, :] for c in range(3))
            p = lambda n: wide[t * 8 : t * 8 + 8, n * 128 : n * 128 + 128]
            values.append(far_value(p, bounds[t], tx, ty, tz))
        far_out[i] = -jnp.concatenate(values, axis=0)
        return carry

    for copy in to_smem:
        copy.wait()
    to_smem.clear()
    low_end = nx - jump
    near_end = low_end + (len(first) if len(first) % 4 == 0 else len(first) + 1)
    lax.fori_loop(low_end, near_end, far_domain, 0, unroll=4 if len(first) % 4 == 0 else 1)
    for d in range(1, nx):
        if d not in first:
            m_copy[d].wait_recv()
            t_copy[d].wait_recv()
            listed(d)
    for copy in to_smem:
        copy.wait()
    lax.fori_loop(near_end, low_end + nx, far_domain, 0, unroll=4 if len(first) % 4 == 0 else 1)
    for copy in o_copies:
        copy.wait()
    for copy in [*t_copy.values(), *m_copy.values(), *c_copies, *x_copies]:
        copy.wait_send()
    mine.wait()


def parts(v):
    high = v.astype(jnp.bfloat16).astype(jnp.float32)
    rest = v - high
    mid = rest.astype(jnp.bfloat16).astype(jnp.float32)
    return high, mid, rest - mid


def near_row(tile, x, y, z):
    sub = iota((8, 128), 0)
    left = jnp.concatenate([*parts(tile), jnp.where(sub < 3, 1.0, tile)], axis=0).T
    picks = []
    for c, row in enumerate((x, y, z)):
        high, mid, low = parts(jnp.broadcast_to(-row, (8, 128)))
        target = jnp.where(sub == 0, high, jnp.where(sub == 1, mid, jnp.where(sub == 2, low, 0.0)))
        for h in range(2):
            one = jnp.where(sub == h * 4 + c, 1.0, 0.0)
            picks.append(jnp.concatenate([one, one, one, target], axis=0))
    right = jnp.concatenate(picks, axis=1).astype(jnp.bfloat16)
    d = jnp.dot(left.astype(jnp.bfloat16), right, preferred_element_type=jnp.float32)
    total = jnp.zeros((8, 128), jnp.float32)
    for h in range(2):
        for s in range(0, 128, 8):
            dx, dy, dz = (
                d[s : s + 8, (2 * c + h) * 128 : (2 * c + h + 1) * 128] for c in range(3)
            )
            inv = lax.rsqrt(dx * dx + dy * dy + dz * dz + SOFT)
            total += inv * jnp.broadcast_to(left[s : s + 8, 27 + 4 * h : 28 + 4 * h], (8, 128))
    return jnp.sum(total, axis=0, keepdims=True)


def far_value(p, live, tx, ty, tz):
    dx, dy, dz = tx - p(1), ty - p(2), tz - p(3)
    r2 = dx * dx + dy * dy + dz * dz + SOFT
    inv = lax.rsqrt(r2)
    inv2 = inv * inv
    quad = dx * (p(4) * dx + p(7) * dy + p(8) * dz) + dy * (p(5) * dy + p(9) * dz) + p(6) * dz * dz
    value = inv * (p(0) + (quad - r2 * p(10)) * (inv2 * inv2))
    return jnp.sum(jnp.where(iota((8, 128), 0) < live, value, 0.0), axis=0, keepdims=True)


def walk_kernel(
    sizes, meta, cnt, t_all, tiles, table, src, out, todo, rows
):
    nx, ny, nz = sizes
    a = lax.axis_index("gx")
    gz = lax.axis_index("gz")
    out[...] = jnp.zeros_like(out)
    near_base = LISTED + nx + 1

    def domain(i, found):
        base = i * 1024
        n0 = meta[base + near_base + a]
        n1 = meta[base + near_base + a + 1]

        @pl.when(meta[base + LISTED + 2 * nx + 3 + a] > 8)
        def _():
            def bucket(t, carry):
                at = base + t * 128
                f0 = meta[at + LISTED + a]
                f1 = meta[at + LISTED + a + 1]
                tx, ty, tz = (t_all[i, c, pl.ds(t, 1), :] for c in range(3))

                def chunk(n, carry):
                    start = f0 + n * 8
                    for u in range(8):
                        rows[u : u + 1, :] = table[pl.ds(meta[at + start + u], 1), :]
                    v = rows[...]
                    p = lambda n: jnp.broadcast_to(v[:, n : n + 1], (8, 128))
                    out[i, pl.ds(t, 1), :] -= far_value(p, f1 - start, tx, ty, tz)
                    return carry

                return lax.fori_loop(1, (f1 - f0 + 7) >> 3, chunk, carry)

            lax.fori_loop(0, 8, bucket, 0)

        def entry(e, found):
            code = meta[base + ((e >> 3) << 7) + FAR + (e & 7)]
            peer, slot = (code & 127) >> 1, code & 1
            todo[found] = (i * 8 + (code >> 7)) * 1024 + peer * (nx * 2) + i * 2 + slot
            return found + jnp.where(cnt[peer * (nx * nz) + i * nz + gz] > slot, 1, 0)

        return lax.fori_loop(n0, n1, entry, found)

    found = lax.fori_loop(0, nx, domain, jnp.int32(0))
    todo[nx * 64 + 1] = found

    def away(n, carry):
        item = todo[n]
        i, t = item >> 13, (item >> 10) & 7
        row = near_row(tiles[item & 1023], *(t_all[i, c, pl.ds(t, 1), :] for c in range(3)))
        out[i, pl.ds(t, 1), :] -= row
        return carry

    lax.fori_loop(AWAY, found, away, 0)
    base = a * 1024

    def own_entry(e, carry):
        code = meta[base + ((e >> 3) << 7) + FAR + (e & 7)]
        t = code >> 7
        row = near_row(src[code & 127], *(t_all[a, c, pl.ds(t, 1), :] for c in range(3)))
        out[a, pl.ds(t, 1), :] -= row
        return carry

    lax.fori_loop(meta[base + near_base + nx] + OWN, meta[base + near_base + nx + 1], own_entry, 0)


def return_kernel(
    sizes, todo, lists, t_all, tiles, part, far_part, src,
    out, landed, near_rows, mine, send, recv,
):
    nx, ny, nz = sizes
    gx, gy, gz = (lax.axis_index(n) for n in ALL)
    barrier = pltpu.get_barrier_semaphore()
    xs = [wrap(gx + d, nx) for d in range(nx)]
    far_first = sorted(range(1, nx), key=lambda d: -min(d, nx - d))
    for d in far_first:
        pl.semaphore_signal(barrier, inc=1, device_id=(xs[d], gy, gz), device_id_type=MESH)
    lane = iota((8, 128), 1)
    found = todo[nx * 64 + 1]

    def near(j, ids):
        item = jnp.where(j < found, todo[j], 0)
        bucket = item >> 10
        i, t = bucket >> 3, bucket & 7
        row = near_row(tiles[item & 1023], *(t_all[i, c, pl.ds(t, 1), :] for c in range(3)))
        near_rows[pl.ds(j, 1), :] = row
        return jnp.where(lane == j, jnp.where(j < found, bucket, -1), ids)

    near_rows[...] = jnp.zeros_like(near_rows)
    ids = lax.fori_loop(0, AWAY, near, jnp.full((8, 128), -1, jnp.int32), unroll=4)
    pick = jnp.where(iota((nx * 8, 128), 0) == jnp.broadcast_to(ids[0:1], (nx * 8, 128)), 1.0, 0.0)
    placed = sum(
        jnp.dot(pick.astype(jnp.bfloat16), v.astype(jnp.bfloat16), preferred_element_type=jnp.float32)
        for v in parts(near_rows[...])
    )
    mine[...] = part[...] + far_part[...] - placed.reshape(nx, 8, 128)

    pl.semaphore_wait(barrier, nx - 1)
    copies = []
    for d in far_first:
        copy = pltpu.make_async_remote_copy(
            src_ref=mine.at[xs[d]], dst_ref=landed.at[d - 1],
            send_sem=send.at[d], recv_sem=recv.at[d],
            device_id=(xs[d], gy, gz), device_id_type=MESH,
        )
        copy.start()
        copies.append(copy)

    n0 = lists[LISTED + nx + 1 + nx]
    n1 = lists[LISTED + nx + 1 + nx + 1]
    sub = iota((8, 128), 0)

    def own_item(j, total):
        e = n0 + j
        p = jnp.minimum(e, 8 * NEAR - 1)
        code = lists[((p >> 3) << 7) + FAR + (p & 7)]
        t = code >> 7
        tile = src[code & 127]
        row = near_row(tile, *(t_all[gx, c, pl.ds(t, 1), :] for c in range(3)))
        return total - jnp.where((sub == t) & (e < n1), row, 0.0)

    summed = lax.fori_loop(0, OWN, own_item, mine[gx], unroll=4)
    for copy in copies:
        copy.wait()
    for d in range(nx - 1):
        summed += landed[d]
    out[...] = summed


def body(sizes, targets, sources, send_ids, send_count, far_ids, near_ids, near_count):
    nx, ny, nz = sizes
    f32, i32 = jnp.float32, jnp.int32
    own = sources.shape[0]
    shape = jax.ShapeDtypeStruct
    vmem = pl.BlockSpec(memory_space=VMEM)
    smem = pl.BlockSpec(memory_space=SMEM)
    hbm = pl.BlockSpec(memory_space=pltpu.HBM)
    dma = pltpu.SemaphoreType.DMA
    in_hbm = functools.partial(pltpu.with_memory_space_constraint, memory_space=pltpu.HBM)
    tgt = jnp.transpose(targets.reshape(3, 8, 128), (1, 0, 2))
    src = jnp.transpose(sources.reshape(own, 4, 2, 128), (0, 2, 1, 3)).reshape(own, 8, 128)
    t_all, meta, tiles_all, cnt, table, far_part, lists, held = pl.pallas_call(
        functools.partial(gather_kernel, sizes),
        out_shape=(
            shape((nx, 3, 8, 128), f32), shape((nx * 1024,), i32),
            shape((nz, nx * 2, 8, 128), f32), shape((nz, 1, nx * nz), i32),
            shape((ny * nz * own, 128), f32),
            shape((nx, 8, 128), f32), shape((1024,), i32), shape((own, 8, 128), f32),
        ),
        in_specs=[hbm] * 7,
        out_specs=(vmem,) * 8,
        scratch_shapes=[
            SMEM((2, nx * nz), i32), SMEM((1, nx * nz), i32), VMEM((1, nx * nz), i32),
            SMEM((8,), i32),
            VMEM((8, FAR), i32), VMEM((8, NEAR), i32), VMEM((8, 3, 128), f32),
            VMEM((8, 128), i32), VMEM((3, 8, 128), f32),
            VMEM((nz, nx * 2, 8, 128), f32), VMEM((own // 8, 128), f32),
            VMEM((ny, nz, own // 8, 128), f32), VMEM((4, 64, 128), f32),
            SMEM((nx * 1024,), i32),
            dma((nx,)), dma((nx,)), dma((nx,)), dma((nx,)), dma((nz,)), dma((nz,)),
            dma((nz,)), dma((nz,)), dma((ny,)), dma((ny,)), dma((nz,)), dma((nz,)),
            dma, dma((nx,)), dma((8,)),
        ],
        compiler_params=pltpu.CompilerParams(
            collective_id=0, has_side_effects=True, vmem_limit_bytes=LIMIT
        ),
        name="gather",
    )(*map(in_hbm, (send_ids[0].T, send_count, near_count, far_ids, near_ids, tgt, src)))

    tiles = tiles_all.reshape(nz * nx * 2, 8, 128)
    part, todo = pl.pallas_call(
        functools.partial(walk_kernel, sizes),
        out_shape=(shape((nx, 8, 128), f32), shape((nx * 64 + 2,), i32)),
        in_specs=[smem, smem, vmem, vmem, vmem, vmem],
        out_specs=(vmem, smem),
        scratch_shapes=[VMEM((8, 128), f32)],
        compiler_params=pltpu.CompilerParams(vmem_limit_bytes=LIMIT),
        name="walk",
    )(meta, cnt.reshape(-1), t_all, tiles, table, held)

    out = pl.pallas_call(
        functools.partial(return_kernel, sizes),
        out_shape=shape((8, 128), f32),
        in_specs=[smem, smem, vmem, vmem, vmem, vmem, vmem],
        out_specs=vmem,
        scratch_shapes=[
            VMEM((nx - 1, 8, 128), f32), VMEM((128, 128), f32),
            VMEM((nx, 8, 128), f32), dma((nx,)), dma((nx,)),
        ],
        compiler_params=pltpu.CompilerParams(
            collective_id=1, has_side_effects=True, vmem_limit_bytes=LIMIT
        ),
        name="bring_back",
    )(todo, lists, t_all, tiles, part, far_part, held)
    return out.reshape(-1)


def solution(mesh):
    sizes = tuple(mesh.shape[n] for n in ALL)
    in_specs = (
        P(None, ALL), P(ALL, None, None), P(ALL, None, None), P(ALL, None),
        P(ALL, None), P(ALL, None), P(ALL),
    )
    return jax.shard_map(
        functools.partial(body, sizes), mesh=mesh, in_specs=in_specs, out_specs=P(ALL),
        check_vma=False,
    )
```

```python
import functools

import jax
import jax.numpy as jnp
from jax import lax
from jax.experimental import pallas as pl
from jax.experimental.pallas import tpu as pltpu
from jax.sharding import PartitionSpec as P

ALL = ("gx", "gy", "gz")
MESH = pl.DeviceIdType.MESH
SOFT = 0.01
FAR = 64
NEAR = 8
LISTED = FAR + NEAR
PARAMS = 16
LIMIT = 16 * 1024 * 1024
OWN = 24
AWAY = 28
VMEM = pltpu.VMEM
SMEM = pltpu.SMEM


def iota(shape, dim):
    return lax.broadcasted_iota(jnp.int32, shape, dim)


def sorted_lists(nx, nz, cells_per_x, own, ids, counts):
    lane = iota((8, 128), 1)
    sub = iota((8, 128), 0)
    is_far = lane < FAR
    is_near = (lane >= FAR) & (lane < LISTED)
    remote = ids - own
    rank = remote >> 1
    live = lane - FAR < counts
    near_code = sub * 128 + jnp.where(remote >= 0, (rank % nz) * 2 + (remote & 1), ids)
    holder = jnp.where(remote >= 0, rank // nz, nx)
    cell = ids % cells_per_x
    cell = cell - (cell & 63) + ((cell & 7) << 3) + ((cell >> 3) & 7)
    order = jnp.where(is_far, lane, sub * NEAR + lane - FAR)
    key = jnp.where(is_far, ids // cells_per_x, jnp.where(live, holder, nx + 1)) * 64 + order
    far_base, near_base, most_base = LISTED, LISTED + nx + 1, LISTED + 2 * nx + 3
    far_limit = jnp.where((lane >= far_base) & (lane < near_base), (lane - far_base) * 64, 0)
    near_limit = jnp.where((lane >= near_base) & (lane < most_base), (lane - near_base) * 64, 0)
    zero = jnp.zeros((8, 128), jnp.int32)
    far_place, near_place, far_start, near_start = zero, zero, zero, zero
    for e in range(FAR):
        other = jnp.broadcast_to(key[:, e : e + 1], (8, 128))
        far_place += jnp.where(other < key, 1, 0)
        far_start += jnp.where(other < far_limit, 1, 0)
    for e in range(NEAR):
        other = jnp.broadcast_to(key[:, FAR + e : FAR + e + 1], (8, 128))
        near_start += jnp.where(other < near_limit, 1, 0)
        for r in range(8):
            moved = pltpu.roll(other, r, 0) if r else other
            near_place += jnp.where(moved < key, 1, 0)
    both = jnp.where(is_far, far_place * 8192 + cell, near_place * 8192 + near_code)
    far_list, near_list = zero, zero
    for e in range(LISTED):
        entry = jnp.broadcast_to(both[:, e : e + 1], (8, 128))
        term = jnp.where((entry >> 13) == lane, entry & 8191, 0)
        if e < FAR:
            far_list += term
        else:
            near_list += term
    near_list = jnp.broadcast_to(jnp.sum(near_list, axis=0, keepdims=True), (8, 128))
    near_start = jnp.broadcast_to(jnp.sum(near_start, axis=0, keepdims=True), (8, 128))
    near_rows = zero
    for t in range(8):
        near_rows = jnp.where(sub == t, pltpu.roll(near_list, (FAR - 8 * t) % 128, 1), near_rows)
    most = pltpu.roll(far_start, 127, 1) - far_start
    most = jnp.broadcast_to(jnp.max(most, axis=0, keepdims=True), (8, 128))
    most = pltpu.roll(most, most_base - far_base, 1)
    out = jnp.where(is_far, far_list, jnp.where(is_near, near_rows, far_start + near_start))
    return jnp.where(lane >= most_base, most, out)


def cell_row(x, y, z, m):
    lane = iota((8, 128), 1)
    sub = iota((8, 128), 0)

    def total(*v):
        return jnp.sum(sum(p * q for p, q in zip(*v)) if len(v) == 2 else sum(v[0]), axis=1, keepdims=True)

    mass = total(m)
    cx, cy, cz = (total(v, m) / mass for v in (x, y, z))
    dx, dy, dz = ([h - c for h in v] for v, c in ((x, cx), (y, cy), (z, cz)))
    wx, wy, wz = ([h * w for h, w in zip(v, m)] for v in (dx, dy, dz))
    sxx, syy, szz = total(wx, dx), total(wy, dy), total(wz, dz)
    sxy, sxz, syz = total(wx, dy), total(wx, dz), total(wy, dz)
    values = (
        mass, cx, cy, cz, 1.5 * sxx, 1.5 * syy, 1.5 * szz,
        3.0 * sxy, 3.0 * sxz, 3.0 * syz, 0.5 * (sxx + syy + szz),
    )
    spread = jnp.zeros((8, 128), jnp.float32)
    for p, value in enumerate(values):
        spread = jnp.where(lane == sub * PARAMS + p, value, spread)
    return jnp.sum(spread, axis=0, keepdims=True)


def wrap(value, size):
    return value & (size - 1) if size & (size - 1) == 0 else lax.rem(value, size)


def gather_kernel(
    sizes, send_ids_hbm, send_count_hbm, near_count_hbm, far_hbm, near_hbm, tgt_hbm, src_hbm,
    t_all, meta_all, tiles_all, cnt_all, table, far_out, mbuf, src,
    send_ids, send_count, cnt_buf, near_count, far, near, tgt,
    ids_buf, tbuf, obuf, cbuf, cells_all, rows, meta_a, meta_b, meta_c,
    t_send, t_recv, m_send, m_recv, o_send, o_recv, c_send, c_recv, x_send, x_recv, n_send, n_recv,
    own_sem, list_sems, in_sems,
):
    nx, ny, nz = sizes
    gx, gy, gz = (lax.axis_index(n) for n in ALL)
    own = src.shape[0]
    jump = max(1, nx // 4)
    metas = (meta_a, meta_b, meta_c)
    barrier = pltpu.get_barrier_semaphore()
    loads = [
        pltpu.make_async_copy(source, dest, in_sems.at[n])
        for n, (source, dest) in enumerate((
            (send_ids_hbm, send_ids), (send_count_hbm, send_count),
            (send_count_hbm, cnt_buf), (near_count_hbm, near_count),
            (far_hbm, far), (near_hbm, near), (tgt_hbm, tgt), (src_hbm, src),
        ))
    ]
    for load in loads:
        load.start()
    xs = [wrap(gx + d, nx) for d in range(nx)]
    ys = [wrap(gy + d, ny) for d in range(ny)]
    zs = [wrap(gz + d, nz) for d in range(nz)]
    first = sorted((d for d in range(1, nx) if min(d, nx - d) <= jump), key=lambda d: -min(d, nx - d))
    greeted = [(xs[d], gy, gz) for d in first]
    greeted += [(gx, gy, zs[d]) for d in range(1, nz)]
    greeted += [(gx, ys[d], gz) for d in range(1, ny)]
    for device in greeted:
        pl.semaphore_signal(barrier, inc=1, device_id=device, device_id_type=MESH)

    def sent(source, dest, s_sem, r_sem, device):
        copy = pltpu.make_async_remote_copy(
            src_ref=source, dst_ref=dest, send_sem=s_sem, recv_sem=r_sem,
            device_id=device, device_id_type=MESH,
        )
        copy.start()
        return copy

    def meta_of(ref, i):
        return ref.at[pl.ds(pl.multiple_of(i * 1024, 1024), 1024)]

    for load in loads[:-1]:
        load.wait()
    for t in range(8):
        for c in range(3):
            tbuf[c, t : t + 1, :] = tgt[t, c : c + 1, :]
    ids_buf[...] = jnp.zeros((8, 128), jnp.int32)
    ids_buf[:, 0:FAR] = far[...]
    ids_buf[:, FAR:LISTED] = near[...]
    sub = iota((8, 128), 0)
    counts = jnp.zeros((8, 128), jnp.int32)
    for t in range(8):
        counts = jnp.where(sub == t, near_count[t], counts)
    lists = sorted_lists(nx, nz, ny * nz * own, own, ids_buf[...], counts)
    for t in range(8):
        mbuf[pl.ds(t * 128, 128)] = lists[t]
    own_copy = pltpu.make_async_copy(mbuf, meta_of(metas[0], gx), list_sems.at[0])
    own_copy.start()
    def gather_tiles(dz):
        k = zs[dz]

        def gather_for(i, carry):
            r = i * nz + k
            filled = send_count[0, r]
            for s in range(2):
                obuf[k, i * 2 + s] = jnp.where(filled > s, src[send_ids[s, r]], 0.0)
            return carry

        lax.fori_loop(0, nx, gather_for, 0, unroll=min(nx, 8))

    pl.semaphore_wait(barrier, len(greeted))

    t_copy, m_copy = {}, {}
    for d in first:
        device = (xs[d], gy, gz)
        m_copy[d] = sent(mbuf, meta_of(meta_all, gx), m_send.at[d], m_recv.at[d], device)
        t_copy[d] = sent(tbuf, t_all.at[gx], t_send.at[d], t_recv.at[d], device)
    loads[-1].wait()

    def moments(g, carry):
        x, y, z, m = ([src[pl.ds(g * 8, 8), h * 4 + r, :] for h in range(2)] for r in range(4))
        cbuf[pl.ds(g, 1), :] = cell_row(x, y, z, m)
        return carry

    lax.fori_loop(0, own // 8, moments, 0, unroll=2)
    c_copies = [
        sent(cbuf, cells_all.at[gy, gz], c_send.at[d], c_recv.at[d], (gx, gy, zs[d]))
        for d in range(1, nz)
    ]
    c_copies += [
        sent(cnt_buf, cnt_all.at[gz], n_send.at[d], n_recv.at[d], (gx, gy, zs[d]))
        for d in range(1, nz)
    ]
    cells_all[gy, gz] = cbuf[...]
    o_copies = []
    gather_tiles(1)
    for d in range(1, nz):
        gather_tiles((d + 1) % nz)
        o_copies.append(
            sent(obuf.at[zs[d]], tiles_all.at[gz], o_send.at[d], o_recv.at[d], (gx, gy, zs[d]))
        )
    t_all[gx] = tbuf[...]
    meta_all[pl.ds(pl.multiple_of(gx * 1024, 1024), 1024)] = mbuf[...]
    cnt_all[gz] = cnt_buf[...]
    mine = pltpu.make_async_copy(obuf.at[gz], tiles_all.at[gz], own_sem)
    mine.start()

    for copy in c_copies:
        copy.wait_recv()
    x_copies = [
        sent(cells_all.at[gy], cells_all.at[gy], x_send.at[d], x_recv.at[d], (gx, ys[d], gz))
        for d in range(1, ny)
    ]

    half = nx // 2
    for e in range(1, half - jump + 1):
        up, down = jump + e, nx - jump - e
        for copies, ref, of, s_sems, r_sems in (
            (m_copy, meta_all, meta_of, m_send, m_recv),
            (t_copy, t_all, lambda ref, i: ref.at[i], t_send, t_recv),
        ):
            if e == 1:
                copies[jump].wait_recv()
                copies[nx - jump].wait_recv()
            if e < half - jump or copies is t_copy:
                behind = of(ref, xs[nx - jump])
                copies[up] = sent(behind, behind, s_sems.at[up], r_sems.at[up], (xs[e], gy, gz))
            if e < half - jump or copies is m_copy:
                ahead = of(ref, xs[jump])
                copies[down] = sent(ahead, ahead, s_sems.at[down], r_sems.at[down], (xs[nx - e], gy, gz))

    near_end = nx // 2
    mid_end = (near_end + nx) // 2
    stages = (range(0, near_end), range(near_end, mid_end), range(mid_end, nx))
    waited = {jump, nx - jump} if half > jump else set()

    def arrived(stage):
        copies = [own_copy] if stage == 0 else []
        for n in stages[stage]:
            d = nx - (n + 1) // 2 if n % 2 else n // 2
            if d == 0:
                continue
            if d not in waited:
                m_copy[d].wait_recv()
                t_copy[d].wait_recv()
            copy = pltpu.make_async_copy(
                meta_of(meta_all, xs[nx - d]), meta_of(metas[stage], xs[nx - d]), list_sems.at[d]
            )
            copy.start()
            copies.append(copy)
        return copies

    listed = arrived(0)
    for copy in x_copies:
        copy.wait_recv()
    blocks = own // 64

    def expand(n, carry):
        for b in range(blocks):
            cells = cells_all[n // nz, n % nz, b * 8 : b * 8 + 8, :]
            for j in range(8):
                moved = pltpu.roll(cells, 128 - PARAMS * j, 1) if j else cells
                table[pl.ds((n * blocks + b) * 64 + j * 8, 8), :] = moved
        return carry

    lax.fori_loop(0, ny * nz, expand, 0, unroll=4)

    k = iota((128, 128), 0)
    spread = jnp.concatenate(
        [jnp.where(((k & 15) == p) & (k < 48), 1.0, 0.0) for p in range(11)], axis=1
    ).astype(jnp.bfloat16)

    def far_domain(meta, n, carry):
        i = wrap(gx + nx + jnp.where((n & 1) == 1, (n + 1) >> 1, -(n >> 1)), nx)
        bounds = []
        slot = rows.at[n & 3]
        for t in range(8):
            at = i * 1024 + t * 128
            f0 = meta[at + LISTED + gx]
            bounds.append(meta[at + LISTED + gx + 1] - f0)
            for u in range(8):
                slot[t * 8 + u : t * 8 + u + 1, :] = table[pl.ds(meta[at + f0 + u], 1), :]
        high, mid, low = parts(slot[...])
        lane = iota((64, 128), 1)
        packed = jnp.where(
            lane < 16, high, jnp.where(lane < 32, pltpu.roll(mid, 16, 1), pltpu.roll(low, 32, 1))
        )
        wide = jnp.dot(packed.astype(jnp.bfloat16), spread, preferred_element_type=jnp.float32)
        values = []
        for t in range(8):
            tx, ty, tz = (t_all[i, c, t : t + 1, :] for c in range(3))
            p = lambda n: wide[t * 8 : t * 8 + 8, n * 128 : n * 128 + 128]
            values.append(far_value(p, bounds[t], tx, ty, tz))
        far_out[i] = -jnp.concatenate(values, axis=0)
        return carry

    for stage, span in enumerate(stages):
        for copy in listed:
            copy.wait()
        lax.fori_loop(
            span.start, span.stop, functools.partial(far_domain, metas[stage]), 0,
            unroll=min(4, max(1, len(span))),
        )
        if stage < 2:
            listed = arrived(stage + 1)
    for copy in o_copies:
        copy.wait()
    for copy in [*t_copy.values(), *m_copy.values(), *c_copies, *x_copies]:
        copy.wait_send()
    mine.wait()


def parts(v):
    high = v.astype(jnp.bfloat16).astype(jnp.float32)
    rest = v - high
    mid = rest.astype(jnp.bfloat16).astype(jnp.float32)
    return high, mid, rest - mid


def near_row(tile, x, y, z):
    sub = iota((8, 128), 0)
    left = jnp.concatenate([*parts(tile), jnp.where(sub < 3, 1.0, tile)], axis=0).T
    picks = []
    for c, row in enumerate((x, y, z)):
        high, mid, low = parts(jnp.broadcast_to(-row, (8, 128)))
        target = jnp.where(sub == 0, high, jnp.where(sub == 1, mid, jnp.where(sub == 2, low, 0.0)))
        for h in range(2):
            one = jnp.where(sub == h * 4 + c, 1.0, 0.0)
            picks.append(jnp.concatenate([one, one, one, target], axis=0))
    right = jnp.concatenate(picks, axis=1).astype(jnp.bfloat16)
    d = jnp.dot(left.astype(jnp.bfloat16), right, preferred_element_type=jnp.float32)
    total = jnp.zeros((8, 128), jnp.float32)
    for h in range(2):
        for s in range(0, 128, 8):
            dx, dy, dz = (
                d[s : s + 8, (2 * c + h) * 128 : (2 * c + h + 1) * 128] for c in range(3)
            )
            inv = lax.rsqrt(dx * dx + dy * dy + dz * dz + SOFT)
            total += inv * jnp.broadcast_to(left[s : s + 8, 27 + 4 * h : 28 + 4 * h], (8, 128))
    return jnp.sum(total, axis=0, keepdims=True)


def far_value(p, live, tx, ty, tz):
    dx, dy, dz = tx - p(1), ty - p(2), tz - p(3)
    r2 = dx * dx + dy * dy + dz * dz + SOFT
    inv = lax.rsqrt(r2)
    inv2 = inv * inv
    quad = dx * (p(4) * dx + p(7) * dy + p(8) * dz) + dy * (p(5) * dy + p(9) * dz) + p(6) * dz * dz
    value = inv * (p(0) + (quad - r2 * p(10)) * (inv2 * inv2))
    return jnp.sum(jnp.where(iota((8, 128), 0) < live, value, 0.0), axis=0, keepdims=True)


def walk_kernel(
    sizes, meta, cnt, t_all, tiles, table, src, out, todo, rows
):
    nx, ny, nz = sizes
    a = lax.axis_index("gx")
    gz = lax.axis_index("gz")
    out[...] = jnp.zeros_like(out)
    near_base = LISTED + nx + 1

    def domain(i, found):
        base = i * 1024
        n0 = meta[base + near_base + a]
        n1 = meta[base + near_base + a + 1]

        @pl.when(meta[base + LISTED + 2 * nx + 3 + a] > 8)
        def _():
            def bucket(t, carry):
                at = base + t * 128
                f0 = meta[at + LISTED + a]
                f1 = meta[at + LISTED + a + 1]
                tx, ty, tz = (t_all[i, c, pl.ds(t, 1), :] for c in range(3))

                def chunk(n, carry):
                    start = f0 + n * 8
                    for u in range(8):
                        rows[u : u + 1, :] = table[pl.ds(meta[at + start + u], 1), :]
                    v = rows[...]
                    p = lambda n: jnp.broadcast_to(v[:, n : n + 1], (8, 128))
                    out[i, pl.ds(t, 1), :] -= far_value(p, f1 - start, tx, ty, tz)
                    return carry

                return lax.fori_loop(1, (f1 - f0 + 7) >> 3, chunk, carry)

            lax.fori_loop(0, 8, bucket, 0)

        def entry(e, found):
            code = meta[base + ((e >> 3) << 7) + FAR + (e & 7)]
            peer, slot = (code & 127) >> 1, code & 1
            todo[found] = (i * 8 + (code >> 7)) * 1024 + peer * (nx * 2) + i * 2 + slot
            return found + jnp.where(cnt[peer * (nx * nz) + i * nz + gz] > slot, 1, 0)

        return lax.fori_loop(n0, n1, entry, found)

    found = lax.fori_loop(0, nx, domain, jnp.int32(0))
    todo[nx * 64 + 1] = found

    def away(n, carry):
        item = todo[n]
        i, t = item >> 13, (item >> 10) & 7
        row = near_row(tiles[item & 1023], *(t_all[i, c, pl.ds(t, 1), :] for c in range(3)))
        out[i, pl.ds(t, 1), :] -= row
        return carry

    lax.fori_loop(AWAY, found, away, 0)
    base = a * 1024

    def own_entry(e, carry):
        code = meta[base + ((e >> 3) << 7) + FAR + (e & 7)]
        t = code >> 7
        row = near_row(src[code & 127], *(t_all[a, c, pl.ds(t, 1), :] for c in range(3)))
        out[a, pl.ds(t, 1), :] -= row
        return carry

    lax.fori_loop(meta[base + near_base + nx] + OWN, meta[base + near_base + nx + 1], own_entry, 0)


def return_kernel(
    sizes, todo, lists, t_all, tiles, part, far_part, src,
    out, landed, near_rows, mine, send, recv,
):
    nx, ny, nz = sizes
    gx, gy, gz = (lax.axis_index(n) for n in ALL)
    barrier = pltpu.get_barrier_semaphore()
    xs = [wrap(gx + d, nx) for d in range(nx)]
    far_first = sorted(range(1, nx), key=lambda d: -min(d, nx - d))
    for d in far_first:
        pl.semaphore_signal(barrier, inc=1, device_id=(xs[d], gy, gz), device_id_type=MESH)
    lane = iota((8, 128), 1)
    found = todo[nx * 64 + 1]

    def near(j, ids):
        item = jnp.where(j < found, todo[j], 0)
        bucket = item >> 10
        i, t = bucket >> 3, bucket & 7
        row = near_row(tiles[item & 1023], *(t_all[i, c, pl.ds(t, 1), :] for c in range(3)))
        near_rows[pl.ds(j, 1), :] = row
        return jnp.where(lane == j, jnp.where(j < found, bucket, -1), ids)

    near_rows[...] = jnp.zeros_like(near_rows)
    ids = lax.fori_loop(0, AWAY, near, jnp.full((8, 128), -1, jnp.int32), unroll=4)
    pick = jnp.where(iota((nx * 8, 128), 0) == jnp.broadcast_to(ids[0:1], (nx * 8, 128)), 1.0, 0.0)
    placed = sum(
        jnp.dot(pick.astype(jnp.bfloat16), v.astype(jnp.bfloat16), preferred_element_type=jnp.float32)
        for v in parts(near_rows[...])
    )
    mine[...] = part[...] + far_part[...] - placed.reshape(nx, 8, 128)

    pl.semaphore_wait(barrier, nx - 1)
    copies = []
    for d in far_first:
        copy = pltpu.make_async_remote_copy(
            src_ref=mine.at[xs[d]], dst_ref=landed.at[d - 1],
            send_sem=send.at[d], recv_sem=recv.at[d],
            device_id=(xs[d], gy, gz), device_id_type=MESH,
        )
        copy.start()
        copies.append(copy)

    n0 = lists[LISTED + nx + 1 + nx]
    n1 = lists[LISTED + nx + 1 + nx + 1]
    sub = iota((8, 128), 0)

    def own_item(j, total):
        e = n0 + j
        p = jnp.minimum(e, 8 * NEAR - 1)
        code = lists[((p >> 3) << 7) + FAR + (p & 7)]
        t = code >> 7
        tile = src[code & 127]
        row = near_row(tile, *(t_all[gx, c, pl.ds(t, 1), :] for c in range(3)))
        return total - jnp.where((sub == t) & (e < n1), row, 0.0)

    summed = lax.fori_loop(0, OWN, own_item, mine[gx], unroll=4)
    for copy in copies:
        copy.wait()
    for d in range(nx - 1):
        summed += landed[d]
    out[...] = summed


def body(sizes, targets, sources, send_ids, send_count, far_ids, near_ids, near_count):
    nx, ny, nz = sizes
    f32, i32 = jnp.float32, jnp.int32
    own = sources.shape[0]
    shape = jax.ShapeDtypeStruct
    vmem = pl.BlockSpec(memory_space=VMEM)
    smem = pl.BlockSpec(memory_space=SMEM)
    hbm = pl.BlockSpec(memory_space=pltpu.HBM)
    dma = pltpu.SemaphoreType.DMA
    in_hbm = functools.partial(pltpu.with_memory_space_constraint, memory_space=pltpu.HBM)
    tgt = jnp.transpose(targets.reshape(3, 8, 128), (1, 0, 2))
    src = jnp.transpose(sources.reshape(own, 4, 2, 128), (0, 2, 1, 3)).reshape(own, 8, 128)
    t_all, meta, tiles_all, cnt, table, far_part, lists, held = pl.pallas_call(
        functools.partial(gather_kernel, sizes),
        out_shape=(
            shape((nx, 3, 8, 128), f32), shape((nx * 1024,), i32),
            shape((nz, nx * 2, 8, 128), f32), shape((nz, 1, nx * nz), i32),
            shape((ny * nz * own, 128), f32),
            shape((nx, 8, 128), f32), shape((1024,), i32), shape((own, 8, 128), f32),
        ),
        in_specs=[hbm] * 7,
        out_specs=(vmem,) * 8,
        scratch_shapes=[
            SMEM((2, nx * nz), i32), SMEM((1, nx * nz), i32), VMEM((1, nx * nz), i32),
            SMEM((8,), i32),
            VMEM((8, FAR), i32), VMEM((8, NEAR), i32), VMEM((8, 3, 128), f32),
            VMEM((8, 128), i32), VMEM((3, 8, 128), f32),
            VMEM((nz, nx * 2, 8, 128), f32), VMEM((own // 8, 128), f32),
            VMEM((ny, nz, own // 8, 128), f32), VMEM((4, 64, 128), f32),
            SMEM((nx * 1024,), i32), SMEM((nx * 1024,), i32), SMEM((nx * 1024,), i32),
            dma((nx,)), dma((nx,)), dma((nx,)), dma((nx,)), dma((nz,)), dma((nz,)),
            dma((nz,)), dma((nz,)), dma((ny,)), dma((ny,)), dma((nz,)), dma((nz,)),
            dma, dma((nx,)), dma((8,)),
        ],
        compiler_params=pltpu.CompilerParams(
            collective_id=0, has_side_effects=True, vmem_limit_bytes=LIMIT
        ),
        name="gather",
    )(*map(in_hbm, (send_ids[0].T, send_count, near_count, far_ids, near_ids, tgt, src)))

    tiles = tiles_all.reshape(nz * nx * 2, 8, 128)
    part, todo = pl.pallas_call(
        functools.partial(walk_kernel, sizes),
        out_shape=(shape((nx, 8, 128), f32), shape((nx * 64 + 2,), i32)),
        in_specs=[smem, smem, vmem, vmem, vmem, vmem],
        out_specs=(vmem, smem),
        scratch_shapes=[VMEM((8, 128), f32)],
        compiler_params=pltpu.CompilerParams(vmem_limit_bytes=LIMIT),
        name="walk",
    )(meta, cnt.reshape(-1), t_all, tiles, table, held)

    out = pl.pallas_call(
        functools.partial(return_kernel, sizes),
        out_shape=shape((8, 128), f32),
        in_specs=[smem, smem, vmem, vmem, vmem, vmem, vmem],
        out_specs=vmem,
        scratch_shapes=[
            VMEM((nx - 1, 8, 128), f32), VMEM((128, 128), f32),
            VMEM((nx, 8, 128), f32), dma((nx,)), dma((nx,)),
        ],
        compiler_params=pltpu.CompilerParams(
            collective_id=1, has_side_effects=True, vmem_limit_bytes=LIMIT
        ),
        name="bring_back",
    )(todo, lists, t_all, tiles, part, far_part, held)
    return out.reshape(-1)


def solution(mesh):
    sizes = tuple(mesh.shape[n] for n in ALL)
    in_specs = (
        P(None, ALL), P(ALL, None, None), P(ALL, None, None), P(ALL, None),
        P(ALL, None), P(ALL, None), P(ALL),
    )
    return jax.shard_map(
        functools.partial(body, sizes), mesh=mesh, in_specs=in_specs, out_specs=P(ALL),
        check_vma=False,
    )
```

```python
import functools

import jax
import jax.numpy as jnp
from jax import lax
from jax.experimental import pallas as pl
from jax.experimental.pallas import tpu as pltpu
from jax.sharding import PartitionSpec as P

ALL = ("gx", "gy", "gz")
MESH = pl.DeviceIdType.MESH
SOFT = 0.01
FAR = 64
NEAR = 8
LISTED = FAR + NEAR
PARAMS = 16
LIMIT = 16 * 1024 * 1024
OWN = 24
AWAY = 28
VMEM = pltpu.VMEM
SMEM = pltpu.SMEM


def iota(shape, dim):
    return lax.broadcasted_iota(jnp.int32, shape, dim)


def sorted_lists(nx, nz, cells_per_x, own, ids, counts):
    lane = iota((8, 128), 1)
    sub = iota((8, 128), 0)
    is_far = lane < FAR
    is_near = (lane >= FAR) & (lane < LISTED)
    remote = ids - own
    rank = remote >> 1
    live = lane - FAR < counts
    near_code = sub * 128 + jnp.where(remote >= 0, (rank % nz) * 2 + (remote & 1), ids)
    holder = jnp.where(remote >= 0, rank // nz, nx)
    cell = ids % cells_per_x
    cell = cell - (cell & 63) + ((cell & 7) << 3) + ((cell >> 3) & 7)
    order = jnp.where(is_far, lane, sub * NEAR + lane - FAR)
    key = jnp.where(is_far, ids // cells_per_x, jnp.where(live, holder, nx + 1)) * 64 + order
    far_base, near_base, most_base = LISTED, LISTED + nx + 1, LISTED + 2 * nx + 3
    far_limit = jnp.where((lane >= far_base) & (lane < near_base), (lane - far_base) * 64, 0)
    near_limit = jnp.where((lane >= near_base) & (lane < most_base), (lane - near_base) * 64, 0)
    zero = jnp.zeros((8, 128), jnp.int32)
    far_place, near_place, far_start, near_start = zero, zero, zero, zero
    for e in range(FAR):
        other = jnp.broadcast_to(key[:, e : e + 1], (8, 128))
        far_place += jnp.where(other < key, 1, 0)
        far_start += jnp.where(other < far_limit, 1, 0)
    for e in range(NEAR):
        other = jnp.broadcast_to(key[:, FAR + e : FAR + e + 1], (8, 128))
        near_start += jnp.where(other < near_limit, 1, 0)
        for r in range(8):
            moved = pltpu.roll(other, r, 0) if r else other
            near_place += jnp.where(moved < key, 1, 0)
    both = jnp.where(is_far, far_place * 8192 + cell, near_place * 8192 + near_code)
    far_list, near_list = zero, zero
    for e in range(LISTED):
        entry = jnp.broadcast_to(both[:, e : e + 1], (8, 128))
        term = jnp.where((entry >> 13) == lane, entry & 8191, 0)
        if e < FAR:
            far_list += term
        else:
            near_list += term
    near_list = jnp.broadcast_to(jnp.sum(near_list, axis=0, keepdims=True), (8, 128))
    near_start = jnp.broadcast_to(jnp.sum(near_start, axis=0, keepdims=True), (8, 128))
    near_rows = zero
    for t in range(8):
        near_rows = jnp.where(sub == t, pltpu.roll(near_list, (FAR - 8 * t) % 128, 1), near_rows)
    most = pltpu.roll(far_start, 127, 1) - far_start
    most = jnp.broadcast_to(jnp.max(most, axis=0, keepdims=True), (8, 128))
    most = pltpu.roll(most, most_base - far_base, 1)
    out = jnp.where(is_far, far_list, jnp.where(is_near, near_rows, far_start + near_start))
    return jnp.where(lane >= most_base, most, out)


def cell_row(x, y, z, m):
    lane = iota((8, 128), 1)
    sub = iota((8, 128), 0)

    def total(*v):
        return jnp.sum(sum(p * q for p, q in zip(*v)) if len(v) == 2 else sum(v[0]), axis=1, keepdims=True)

    mass = total(m)
    cx, cy, cz = (total(v, m) / mass for v in (x, y, z))
    dx, dy, dz = ([h - c for h in v] for v, c in ((x, cx), (y, cy), (z, cz)))
    wx, wy, wz = ([h * w for h, w in zip(v, m)] for v in (dx, dy, dz))
    sxx, syy, szz = total(wx, dx), total(wy, dy), total(wz, dz)
    sxy, sxz, syz = total(wx, dy), total(wx, dz), total(wy, dz)
    values = (
        mass, cx, cy, cz, 1.5 * sxx, 1.5 * syy, 1.5 * szz,
        3.0 * sxy, 3.0 * sxz, 3.0 * syz, 0.5 * (sxx + syy + szz),
    )
    spread = jnp.zeros((8, 128), jnp.float32)
    for p, value in enumerate(values):
        spread = jnp.where(lane == sub * PARAMS + p, value, spread)
    return jnp.sum(spread, axis=0, keepdims=True)


def wrap(value, size):
    return value & (size - 1) if size & (size - 1) == 0 else lax.rem(value, size)


def gather_kernel(
    sizes, send_ids_hbm, send_count_hbm, near_count_hbm, far_hbm, near_hbm, tgt_hbm, src_hbm,
    t_all, meta_all, tiles_all, cnt_all, table, far_out, mbuf, src,
    send_ids, send_count, cnt_buf, near_count, far, near, tgt,
    ids_buf, tbuf, obuf, cbuf, cells_all, rows, meta_a, meta_b, meta_c,
    t_send, t_recv, m_send, m_recv, o_send, o_recv, c_send, c_recv, x_send, x_recv, n_send, n_recv,
    own_sem, list_sems, in_sems,
):
    nx, ny, nz = sizes
    gx, gy, gz = (lax.axis_index(n) for n in ALL)
    own = src.shape[0]
    jump = max(1, nx // 4)
    metas = (meta_a, meta_b, meta_c)
    barrier = pltpu.get_barrier_semaphore()
    loads = [
        pltpu.make_async_copy(source, dest, in_sems.at[n])
        for n, (source, dest) in enumerate((
            (send_ids_hbm, send_ids), (send_count_hbm, send_count),
            (send_count_hbm, cnt_buf), (near_count_hbm, near_count),
            (far_hbm, far), (near_hbm, near), (tgt_hbm, tgt), (src_hbm, src),
        ))
    ]
    for load in loads:
        load.start()
    xs = [wrap(gx + d, nx) for d in range(nx)]
    ys = [wrap(gy + d, ny) for d in range(ny)]
    zs = [wrap(gz + d, nz) for d in range(nz)]
    first = sorted((d for d in range(1, nx) if min(d, nx - d) <= jump), key=lambda d: -min(d, nx - d))
    greeted = [(xs[d], gy, gz) for d in first]
    greeted += [(gx, gy, zs[d]) for d in range(1, nz)]
    greeted += [(gx, ys[d], gz) for d in range(1, ny)]
    for device in greeted:
        pl.semaphore_signal(barrier, inc=1, device_id=device, device_id_type=MESH)

    def sent(source, dest, s_sem, r_sem, device):
        copy = pltpu.make_async_remote_copy(
            src_ref=source, dst_ref=dest, send_sem=s_sem, recv_sem=r_sem,
            device_id=device, device_id_type=MESH,
        )
        copy.start()
        return copy

    def meta_of(ref, i):
        return ref.at[pl.ds(pl.multiple_of(i * 1024, 1024), 1024)]

    for load in loads[:-1]:
        load.wait()
    for t in range(8):
        for c in range(3):
            tbuf[c, t : t + 1, :] = tgt[t, c : c + 1, :]
    ids_buf[...] = jnp.zeros((8, 128), jnp.int32)
    ids_buf[:, 0:FAR] = far[...]
    ids_buf[:, FAR:LISTED] = near[...]
    sub = iota((8, 128), 0)
    counts = jnp.zeros((8, 128), jnp.int32)
    for t in range(8):
        counts = jnp.where(sub == t, near_count[t], counts)
    lists = sorted_lists(nx, nz, ny * nz * own, own, ids_buf[...], counts)
    for t in range(8):
        mbuf[pl.ds(t * 128, 128)] = lists[t]
    own_copy = pltpu.make_async_copy(mbuf, meta_of(metas[0], gx), list_sems.at[0])
    own_copy.start()
    loads[-1].wait()
    flat = src.reshape(own * 8, 128)

    def moments(g, carry):
        x, y, z, m = (
            [flat[pl.ds(g * 64 + h * 4 + r, 8, stride=8), :] for h in range(2)] for r in range(4)
        )
        cbuf[pl.ds(g, 1), :] = cell_row(x, y, z, m)
        return carry

    lax.fori_loop(0, own // 8, moments, 0, unroll=4)

    def gather_tiles(dz):
        k = zs[dz]

        def gather_for(i, carry):
            r = i * nz + k
            filled = send_count[0, r]
            for s in range(2):
                obuf[k, i * 2 + s] = jnp.where(filled > s, src[send_ids[s, r]], 0.0)
            return carry

        lax.fori_loop(0, nx, gather_for, 0, unroll=min(nx, 8))

    pl.semaphore_wait(barrier, len(greeted))

    t_copy, m_copy = {}, {}
    for d in first:
        device = (xs[d], gy, gz)
        m_copy[d] = sent(mbuf, meta_of(meta_all, gx), m_send.at[d], m_recv.at[d], device)
        t_copy[d] = sent(tbuf, t_all.at[gx], t_send.at[d], t_recv.at[d], device)
    c_copies = [
        sent(cbuf, cells_all.at[gy, gz], c_send.at[d], c_recv.at[d], (gx, gy, zs[d]))
        for d in range(1, nz)
    ]
    c_copies += [
        sent(cnt_buf, cnt_all.at[gz], n_send.at[d], n_recv.at[d], (gx, gy, zs[d]))
        for d in range(1, nz)
    ]
    cells_all[gy, gz] = cbuf[...]
    o_copies = []
    gather_tiles(1)
    for d in range(1, nz):
        gather_tiles((d + 1) % nz)
        o_copies.append(
            sent(obuf.at[zs[d]], tiles_all.at[gz], o_send.at[d], o_recv.at[d], (gx, gy, zs[d]))
        )
    t_all[gx] = tbuf[...]
    meta_all[pl.ds(pl.multiple_of(gx * 1024, 1024), 1024)] = mbuf[...]
    cnt_all[gz] = cnt_buf[...]
    mine = pltpu.make_async_copy(obuf.at[gz], tiles_all.at[gz], own_sem)
    mine.start()

    for copy in c_copies:
        copy.wait_recv()
    x_copies = [
        sent(cells_all.at[gy], cells_all.at[gy], x_send.at[d], x_recv.at[d], (gx, ys[d], gz))
        for d in range(1, ny)
    ]

    half = nx // 2
    for e in range(1, half - jump + 1):
        up, down = jump + e, nx - jump - e
        for copies, ref, of, s_sems, r_sems in (
            (m_copy, meta_all, meta_of, m_send, m_recv),
            (t_copy, t_all, lambda ref, i: ref.at[i], t_send, t_recv),
        ):
            if e == 1:
                copies[jump].wait_recv()
                copies[nx - jump].wait_recv()
            if e < half - jump or copies is t_copy:
                behind = of(ref, xs[nx - jump])
                copies[up] = sent(behind, behind, s_sems.at[up], r_sems.at[up], (xs[e], gy, gz))
            if e < half - jump or copies is m_copy:
                ahead = of(ref, xs[jump])
                copies[down] = sent(ahead, ahead, s_sems.at[down], r_sems.at[down], (xs[nx - e], gy, gz))

    near_end = nx // 2
    mid_end = (near_end + nx) // 2
    stages = (range(0, near_end), range(near_end, mid_end), range(mid_end, nx))
    waited = {jump, nx - jump} if half > jump else set()

    def arrived(stage):
        copies = [own_copy] if stage == 0 else []
        for n in stages[stage]:
            d = nx - (n + 1) // 2 if n % 2 else n // 2
            if d == 0:
                continue
            if d not in waited:
                m_copy[d].wait_recv()
                t_copy[d].wait_recv()
            copy = pltpu.make_async_copy(
                meta_of(meta_all, xs[nx - d]), meta_of(metas[stage], xs[nx - d]), list_sems.at[d]
            )
            copy.start()
            copies.append(copy)
        return copies

    listed = arrived(0)
    for copy in x_copies:
        copy.wait_recv()
    blocks = own // 64

    def expand(n, carry):
        for b in range(blocks):
            cells = cells_all[n // nz, n % nz, b * 8 : b * 8 + 8, :]
            for j in range(8):
                moved = pltpu.roll(cells, 128 - PARAMS * j, 1) if j else cells
                table[pl.ds((n * blocks + b) * 64 + j * 8, 8), :] = moved
        return carry

    lax.fori_loop(0, ny * nz, expand, 0, unroll=4)

    k = iota((128, 128), 0)
    spread = jnp.concatenate(
        [jnp.where(((k & 15) == p) & (k < 48), 1.0, 0.0) for p in range(11)], axis=1
    ).astype(jnp.bfloat16)

    def far_domain(meta, n, carry):
        i = wrap(gx + nx + jnp.where((n & 1) == 1, (n + 1) >> 1, -(n >> 1)), nx)
        bounds = []
        slot = rows.at[n & 3]
        for t in range(8):
            at = i * 1024 + t * 128
            f0 = meta[at + LISTED + gx]
            bounds.append(meta[at + LISTED + gx + 1] - f0)
            for u in range(8):
                slot[t * 8 + u : t * 8 + u + 1, :] = table[pl.ds(meta[at + f0 + u], 1), :]
        high, mid, low = parts(slot[...])
        lane = iota((64, 128), 1)
        packed = jnp.where(
            lane < 16, high, jnp.where(lane < 32, pltpu.roll(mid, 16, 1), pltpu.roll(low, 32, 1))
        )
        wide = jnp.dot(packed.astype(jnp.bfloat16), spread, preferred_element_type=jnp.float32)
        values = []
        for t in range(8):
            tx, ty, tz = (t_all[i, c, t : t + 1, :] for c in range(3))
            p = lambda n: wide[t * 8 : t * 8 + 8, n * 128 : n * 128 + 128]
            values.append(far_value(p, bounds[t], tx, ty, tz))
        far_out[i] = -jnp.concatenate(values, axis=0)
        return carry

    for stage, span in enumerate(stages):
        for copy in listed:
            copy.wait()
        lax.fori_loop(
            span.start, span.stop, functools.partial(far_domain, metas[stage]), 0,
            unroll=min(4, max(1, len(span))),
        )
        if stage < 2:
            listed = arrived(stage + 1)
    for copy in o_copies:
        copy.wait()
    for copy in [*t_copy.values(), *m_copy.values(), *c_copies, *x_copies]:
        copy.wait_send()
    mine.wait()


def parts(v):
    high = v.astype(jnp.bfloat16).astype(jnp.float32)
    rest = v - high
    mid = rest.astype(jnp.bfloat16).astype(jnp.float32)
    return high, mid, rest - mid


def near_row(tile, x, y, z):
    sub = iota((8, 128), 0)
    left = jnp.concatenate([*parts(tile), jnp.where(sub < 3, 1.0, tile)], axis=0).T
    picks = []
    for c, row in enumerate((x, y, z)):
        high, mid, low = parts(jnp.broadcast_to(-row, (8, 128)))
        target = jnp.where(sub == 0, high, jnp.where(sub == 1, mid, jnp.where(sub == 2, low, 0.0)))
        for h in range(2):
            one = jnp.where(sub == h * 4 + c, 1.0, 0.0)
            picks.append(jnp.concatenate([one, one, one, target], axis=0))
    right = jnp.concatenate(picks, axis=1).astype(jnp.bfloat16)
    d = jnp.dot(left.astype(jnp.bfloat16), right, preferred_element_type=jnp.float32)
    total = jnp.zeros((8, 128), jnp.float32)
    for h in range(2):
        for s in range(0, 128, 8):
            dx, dy, dz = (
                d[s : s + 8, (2 * c + h) * 128 : (2 * c + h + 1) * 128] for c in range(3)
            )
            inv = lax.rsqrt(dx * dx + dy * dy + dz * dz + SOFT)
            total += inv * jnp.broadcast_to(left[s : s + 8, 27 + 4 * h : 28 + 4 * h], (8, 128))
    return jnp.sum(total, axis=0, keepdims=True)


def far_value(p, live, tx, ty, tz):
    dx, dy, dz = tx - p(1), ty - p(2), tz - p(3)
    r2 = dx * dx + dy * dy + dz * dz + SOFT
    inv = lax.rsqrt(r2)
    inv2 = inv * inv
    quad = dx * (p(4) * dx + p(7) * dy + p(8) * dz) + dy * (p(5) * dy + p(9) * dz) + p(6) * dz * dz
    value = inv * (p(0) + (quad - r2 * p(10)) * (inv2 * inv2))
    return jnp.sum(jnp.where(iota((8, 128), 0) < live, value, 0.0), axis=0, keepdims=True)


def walk_kernel(
    sizes, meta_in, cnt_in, lists_in, t_all, tiles, table, src,
    out, todo, rows, meta_a, meta_b, meta_c, meta_d, cnt, lists, in_sems,
):
    nx, ny, nz = sizes
    a = lax.axis_index("gx")
    gz = lax.axis_index("gz")
    near_base = LISTED + nx + 1
    metas = (meta_a, meta_b, meta_c, meta_d)
    each = meta_a.shape[0] // 1024
    copies = [pltpu.make_async_copy(cnt_in, cnt, in_sems.at[4])]
    for q in range(nx // each):
        part = meta_in.at[pl.ds(q * each * 1024, each * 1024)]
        copies.append(pltpu.make_async_copy(part, metas[q], in_sems.at[q]))
    copies.append(pltpu.make_async_copy(lists_in, lists, in_sems.at[5]))
    for copy in copies:
        copy.start()
    out[...] = jnp.zeros_like(out)

    def domain(meta, q, i, found):
        base = (i - q * each) * 1024
        n0 = meta[base + near_base + a]
        n1 = meta[base + near_base + a + 1]

        @pl.when(meta[base + LISTED + 2 * nx + 3 + a] > 8)
        def _():
            def bucket(t, carry):
                at = base + t * 128
                f0 = meta[at + LISTED + a]
                f1 = meta[at + LISTED + a + 1]
                tx, ty, tz = (t_all[i, c, pl.ds(t, 1), :] for c in range(3))

                def chunk(n, carry):
                    start = f0 + n * 8
                    for u in range(8):
                        rows[u : u + 1, :] = table[pl.ds(meta[at + start + u], 1), :]
                    v = rows[...]
                    p = lambda n: jnp.broadcast_to(v[:, n : n + 1], (8, 128))
                    out[i, pl.ds(t, 1), :] -= far_value(p, f1 - start, tx, ty, tz)
                    return carry

                return lax.fori_loop(1, (f1 - f0 + 7) >> 3, chunk, carry)

            lax.fori_loop(0, 8, bucket, 0)

        def entry(e, found):
            code = meta[base + ((e >> 3) << 7) + FAR + (e & 7)]
            peer, slot = (code & 127) >> 1, code & 1
            todo[found] = (i * 8 + (code >> 7)) * 1024 + peer * (nx * 2) + i * 2 + slot
            return found + jnp.where(cnt[peer * (nx * nz) + i * nz + gz] > slot, 1, 0)

        return lax.fori_loop(n0, n1, entry, found)

    copies[0].wait()
    found = jnp.int32(0)
    for q in range(nx // each):
        copies[q + 1].wait()
        step = functools.partial(domain, metas[q], q)
        found = lax.fori_loop(q * each, (q + 1) * each, step, found)
    copies[-1].wait()
    todo[nx * 64 + 1] = found

    def away(n, carry):
        item = todo[n]
        i, t = item >> 13, (item >> 10) & 7
        row = near_row(tiles[item & 1023], *(t_all[i, c, pl.ds(t, 1), :] for c in range(3)))
        out[i, pl.ds(t, 1), :] -= row
        return carry

    lax.fori_loop(AWAY, found, away, 0)

    def own_entry(e, carry):
        code = lists[((e >> 3) << 7) + FAR + (e & 7)]
        t = code >> 7
        row = near_row(src[code & 127], *(t_all[a, c, pl.ds(t, 1), :] for c in range(3)))
        out[a, pl.ds(t, 1), :] -= row
        return carry

    lax.fori_loop(lists[near_base + nx] + OWN, lists[near_base + nx + 1], own_entry, 0)


def return_kernel(
    sizes, todo_in, lists_in, t_all, tiles, part, far_part, src,
    out, landed, near_rows, mine, todo, lists, send, recv, in_sems,
):
    nx, ny, nz = sizes
    gx, gy, gz = (lax.axis_index(n) for n in ALL)
    barrier = pltpu.get_barrier_semaphore()
    xs = [wrap(gx + d, nx) for d in range(nx)]
    far_first = sorted(range(1, nx), key=lambda d: -min(d, nx - d))
    for d in far_first:
        pl.semaphore_signal(barrier, inc=1, device_id=(xs[d], gy, gz), device_id_type=MESH)
    lane = iota((8, 128), 1)
    todo_copy = pltpu.make_async_copy(todo_in, todo, in_sems.at[0])
    lists_copy = pltpu.make_async_copy(lists_in, lists, in_sems.at[1])
    todo_copy.start()
    lists_copy.start()
    todo_copy.wait()
    lists_copy.wait()
    found = todo[nx * 64 + 1]

    def near(j, ids):
        item = jnp.where(j < found, todo[j], 0)
        bucket = item >> 10
        i, t = bucket >> 3, bucket & 7
        row = near_row(tiles[item & 1023], *(t_all[i, c, pl.ds(t, 1), :] for c in range(3)))
        near_rows[pl.ds(j, 1), :] = row
        return jnp.where(lane == j, jnp.where(j < found, bucket, -1), ids)

    near_rows[...] = jnp.zeros_like(near_rows)
    ids = lax.fori_loop(0, AWAY, near, jnp.full((8, 128), -1, jnp.int32), unroll=4)
    pick = jnp.where(iota((nx * 8, 128), 0) == jnp.broadcast_to(ids[0:1], (nx * 8, 128)), 1.0, 0.0)
    placed = sum(
        jnp.dot(pick.astype(jnp.bfloat16), v.astype(jnp.bfloat16), preferred_element_type=jnp.float32)
        for v in parts(near_rows[...])
    )
    mine[...] = part[...] + far_part[...] - placed.reshape(nx, 8, 128)

    pl.semaphore_wait(barrier, nx - 1)
    copies = []
    for d in far_first:
        copy = pltpu.make_async_remote_copy(
            src_ref=mine.at[xs[d]], dst_ref=landed.at[d - 1],
            send_sem=send.at[d], recv_sem=recv.at[d],
            device_id=(xs[d], gy, gz), device_id_type=MESH,
        )
        copy.start()
        copies.append(copy)

    n0 = lists[LISTED + nx + 1 + nx]
    n1 = lists[LISTED + nx + 1 + nx + 1]
    sub = iota((8, 128), 0)

    def own_item(j, total):
        e = n0 + j
        p = jnp.minimum(e, 8 * NEAR - 1)
        code = lists[((p >> 3) << 7) + FAR + (p & 7)]
        t = code >> 7
        tile = src[code & 127]
        row = near_row(tile, *(t_all[gx, c, pl.ds(t, 1), :] for c in range(3)))
        return total - jnp.where((sub == t) & (e < n1), row, 0.0)

    summed = lax.fori_loop(0, OWN, own_item, mine[gx], unroll=4)
    for copy in copies:
        copy.wait()
    for d in range(nx - 1):
        summed += landed[d]
    out[...] = summed


def body(sizes, targets, sources, send_ids, send_count, far_ids, near_ids, near_count):
    nx, ny, nz = sizes
    f32, i32 = jnp.float32, jnp.int32
    own = sources.shape[0]
    shape = jax.ShapeDtypeStruct
    vmem = pl.BlockSpec(memory_space=VMEM)
    smem = pl.BlockSpec(memory_space=SMEM)
    hbm = pl.BlockSpec(memory_space=pltpu.HBM)
    dma = pltpu.SemaphoreType.DMA
    in_hbm = functools.partial(pltpu.with_memory_space_constraint, memory_space=pltpu.HBM)
    tgt = jnp.transpose(targets.reshape(3, 8, 128), (1, 0, 2))
    src = jnp.transpose(sources.reshape(own, 4, 2, 128), (0, 2, 1, 3)).reshape(own, 8, 128)
    t_all, meta, tiles_all, cnt, table, far_part, lists, held = pl.pallas_call(
        functools.partial(gather_kernel, sizes),
        out_shape=(
            shape((nx, 3, 8, 128), f32), shape((nx * 1024,), i32),
            shape((nz, nx * 2, 8, 128), f32), shape((nz, 1, nx * nz), i32),
            shape((ny * nz * own, 128), f32),
            shape((nx, 8, 128), f32), shape((1024,), i32), shape((own, 8, 128), f32),
        ),
        in_specs=[hbm] * 7,
        out_specs=(vmem,) * 8,
        scratch_shapes=[
            SMEM((2, nx * nz), i32), SMEM((1, nx * nz), i32), VMEM((1, nx * nz), i32),
            SMEM((8,), i32),
            VMEM((8, FAR), i32), VMEM((8, NEAR), i32), VMEM((8, 3, 128), f32),
            VMEM((8, 128), i32), VMEM((3, 8, 128), f32),
            VMEM((nz, nx * 2, 8, 128), f32), VMEM((own // 8, 128), f32),
            VMEM((ny, nz, own // 8, 128), f32), VMEM((4, 64, 128), f32),
            SMEM((nx * 1024,), i32), SMEM((nx * 1024,), i32), SMEM((nx * 1024,), i32),
            dma((nx,)), dma((nx,)), dma((nx,)), dma((nx,)), dma((nz,)), dma((nz,)),
            dma((nz,)), dma((nz,)), dma((ny,)), dma((ny,)), dma((nz,)), dma((nz,)),
            dma, dma((nx,)), dma((8,)),
        ],
        compiler_params=pltpu.CompilerParams(
            collective_id=0, has_side_effects=True, vmem_limit_bytes=LIMIT
        ),
        name="gather",
    )(*map(in_hbm, (send_ids[0].T, send_count, near_count, far_ids, near_ids, tgt, src)))

    tiles = tiles_all.reshape(nz * nx * 2, 8, 128)
    part, todo = pl.pallas_call(
        functools.partial(walk_kernel, sizes),
        out_shape=(shape((nx, 8, 128), f32), shape((nx * 64 + 2,), i32)),
        in_specs=[vmem] * 7,
        out_specs=(vmem, smem),
        scratch_shapes=[
            VMEM((8, 128), f32), *[SMEM((max(1, nx // 4) * 1024,), i32)] * 4,
            SMEM((nz * nx * nz,), i32), SMEM((1024,), i32), dma((6,)),
        ],
        compiler_params=pltpu.CompilerParams(vmem_limit_bytes=LIMIT),
        name="walk",
    )(meta, cnt.reshape(-1), lists, t_all, tiles, table, held)

    out = pl.pallas_call(
        functools.partial(return_kernel, sizes),
        out_shape=shape((8, 128), f32),
        in_specs=[vmem] * 7,
        out_specs=vmem,
        scratch_shapes=[
            VMEM((nx - 1, 8, 128), f32), VMEM((128, 128), f32),
            VMEM((nx, 8, 128), f32), SMEM((nx * 64 + 2,), i32), SMEM((1024,), i32),
            dma((nx,)), dma((nx,)), dma((2,)),
        ],
        compiler_params=pltpu.CompilerParams(
            collective_id=1, has_side_effects=True, vmem_limit_bytes=LIMIT
        ),
        name="bring_back",
    )(todo, lists, t_all, tiles, part, far_part, held)
    return out.reshape(-1)


def solution(mesh):
    sizes = tuple(mesh.shape[n] for n in ALL)
    in_specs = (
        P(None, ALL), P(ALL, None, None), P(ALL, None, None), P(ALL, None),
        P(ALL, None), P(ALL, None), P(ALL),
    )
    return jax.shard_map(
        functools.partial(body, sizes), mesh=mesh, in_specs=in_specs, out_specs=P(ALL),
        check_vma=False,
    )
```

```python
import functools

import jax
import jax.numpy as jnp
from jax import lax
from jax.experimental import pallas as pl
from jax.experimental.pallas import tpu as pltpu
from jax.sharding import PartitionSpec as P

ALL = ("gx", "gy", "gz")
MESH = pl.DeviceIdType.MESH
SOFT = 0.01
FAR = 64
NEAR = 8
LISTED = FAR + NEAR
PARAMS = 16
LIMIT = 16 * 1024 * 1024
OWN = 24
AWAY = 28
VMEM = pltpu.VMEM
SMEM = pltpu.SMEM


def iota(shape, dim):
    return lax.broadcasted_iota(jnp.int32, shape, dim)


def sorted_lists(nx, nz, cells_per_x, own, ids, counts):
    lane = iota((8, 128), 1)
    sub = iota((8, 128), 0)
    is_far = lane < FAR
    is_near = (lane >= FAR) & (lane < LISTED)
    remote = ids - own
    rank = remote >> 1
    live = lane - FAR < counts
    near_code = sub * 128 + jnp.where(remote >= 0, (rank % nz) * 2 + (remote & 1), ids)
    holder = jnp.where(remote >= 0, rank // nz, nx)
    cell = ids % cells_per_x
    cell = cell - (cell & 63) + ((cell & 7) << 3) + ((cell >> 3) & 7)
    order = jnp.where(is_far, lane, sub * NEAR + lane - FAR)
    key = jnp.where(is_far, ids // cells_per_x, jnp.where(live, holder, nx + 1)) * 64 + order
    far_base, near_base, most_base = LISTED, LISTED + nx + 1, LISTED + 2 * nx + 3
    far_limit = jnp.where((lane >= far_base) & (lane < near_base), (lane - far_base) * 64, 0)
    near_limit = jnp.where((lane >= near_base) & (lane < most_base), (lane - near_base) * 64, 0)
    zero = jnp.zeros((8, 128), jnp.int32)
    far_place, near_place, far_start, near_start = zero, zero, zero, zero
    for e in range(FAR):
        other = jnp.broadcast_to(key[:, e : e + 1], (8, 128))
        far_place += jnp.where(other < key, 1, 0)
        far_start += jnp.where(other < far_limit, 1, 0)
    for e in range(NEAR):
        other = jnp.broadcast_to(key[:, FAR + e : FAR + e + 1], (8, 128))
        near_start += jnp.where(other < near_limit, 1, 0)
        for r in range(8):
            moved = pltpu.roll(other, r, 0) if r else other
            near_place += jnp.where(moved < key, 1, 0)
    both = jnp.where(is_far, far_place * 8192 + cell, near_place * 8192 + near_code)
    far_list, near_list = zero, zero
    for e in range(LISTED):
        entry = jnp.broadcast_to(both[:, e : e + 1], (8, 128))
        term = jnp.where((entry >> 13) == lane, entry & 8191, 0)
        if e < FAR:
            far_list += term
        else:
            near_list += term
    near_list = jnp.broadcast_to(jnp.sum(near_list, axis=0, keepdims=True), (8, 128))
    near_start = jnp.broadcast_to(jnp.sum(near_start, axis=0, keepdims=True), (8, 128))
    near_rows = zero
    for t in range(8):
        near_rows = jnp.where(sub == t, pltpu.roll(near_list, (FAR - 8 * t) % 128, 1), near_rows)
    length = pltpu.roll(far_start, 127, 1) - far_start
    top = jnp.max(length * 8 + sub, axis=0, keepdims=True) & 7
    most = jnp.sum(jnp.where(length > 8, 1, 0), axis=0, keepdims=True) * 8 + top
    most = jnp.broadcast_to(most, (8, 128))
    most = pltpu.roll(most, most_base - far_base, 1)
    out = jnp.where(is_far, far_list, jnp.where(is_near, near_rows, far_start + near_start))
    return jnp.where(lane >= most_base, most, out)


def cell_row(x, y, z, m):
    lane = iota((8, 128), 1)
    sub = iota((8, 128), 0)

    def total(*v):
        return jnp.sum(sum(p * q for p, q in zip(*v)) if len(v) == 2 else sum(v[0]), axis=1, keepdims=True)

    mass = total(m)
    cx, cy, cz = (total(v, m) / mass for v in (x, y, z))
    dx, dy, dz = ([h - c for h in v] for v, c in ((x, cx), (y, cy), (z, cz)))
    wx, wy, wz = ([h * w for h, w in zip(v, m)] for v in (dx, dy, dz))
    sxx, syy, szz = total(wx, dx), total(wy, dy), total(wz, dz)
    sxy, sxz, syz = total(wx, dy), total(wx, dz), total(wy, dz)
    values = (
        mass, cx, cy, cz, 1.5 * sxx, 1.5 * syy, 1.5 * szz,
        3.0 * sxy, 3.0 * sxz, 3.0 * syz, 0.5 * (sxx + syy + szz),
    )
    spread = jnp.zeros((8, 128), jnp.float32)
    for p, value in enumerate(values):
        spread = jnp.where(lane == sub * PARAMS + p, value, spread)
    return jnp.sum(spread, axis=0, keepdims=True)


def wrap(value, size):
    return value & (size - 1) if size & (size - 1) == 0 else lax.rem(value, size)


def gather_kernel(
    sizes, send_ids_hbm, send_count_hbm, near_count_hbm, far_hbm, near_hbm, tgt_hbm, src_hbm,
    t_all, meta_all, tiles_all, cnt_all, table, far_out, mbuf, src,
    send_ids, send_count, cnt_buf, near_count, far, near, tgt,
    ids_buf, tbuf, obuf, cbuf, cells_all, rows, meta_a, meta_b, meta_c,
    t_send, t_recv, m_send, m_recv, o_send, o_recv, c_send, c_recv, x_send, x_recv, n_send, n_recv,
    own_sem, list_sems, in_sems,
):
    nx, ny, nz = sizes
    gx, gy, gz = (lax.axis_index(n) for n in ALL)
    own = src.shape[0]
    jump = max(1, nx // 4)
    metas = (meta_a, meta_b, meta_c)
    barrier = pltpu.get_barrier_semaphore()
    loads = [
        pltpu.make_async_copy(source, dest, in_sems.at[n])
        for n, (source, dest) in enumerate((
            (send_ids_hbm, send_ids), (send_count_hbm, send_count),
            (send_count_hbm, cnt_buf), (near_count_hbm, near_count),
            (far_hbm, far), (near_hbm, near), (tgt_hbm, tgt), (src_hbm, src),
        ))
    ]
    for load in loads:
        load.start()
    xs = [wrap(gx + d, nx) for d in range(nx)]
    ys = [wrap(gy + d, ny) for d in range(ny)]
    zs = [wrap(gz + d, nz) for d in range(nz)]
    first = sorted((d for d in range(1, nx) if min(d, nx - d) <= jump), key=lambda d: -min(d, nx - d))
    greeted = [(xs[d], gy, gz) for d in first]
    greeted += [(gx, gy, zs[d]) for d in range(1, nz)]
    greeted += [(gx, ys[d], gz) for d in range(1, ny)]
    for device in greeted:
        pl.semaphore_signal(barrier, inc=1, device_id=device, device_id_type=MESH)

    def sent(source, dest, s_sem, r_sem, device):
        copy = pltpu.make_async_remote_copy(
            src_ref=source, dst_ref=dest, send_sem=s_sem, recv_sem=r_sem,
            device_id=device, device_id_type=MESH,
        )
        copy.start()
        return copy

    def meta_of(ref, i):
        return ref.at[pl.ds(pl.multiple_of(i * 1024, 1024), 1024)]

    for load in loads[:-1]:
        load.wait()
    for t in range(8):
        for c in range(3):
            tbuf[c, t : t + 1, :] = tgt[t, c : c + 1, :]
    ids_buf[...] = jnp.zeros((8, 128), jnp.int32)
    ids_buf[:, 0:FAR] = far[...]
    ids_buf[:, FAR:LISTED] = near[...]
    sub = iota((8, 128), 0)
    counts = jnp.zeros((8, 128), jnp.int32)
    for t in range(8):
        counts = jnp.where(sub == t, near_count[t], counts)
    lists = sorted_lists(nx, nz, ny * nz * own, own, ids_buf[...], counts)
    for t in range(8):
        mbuf[pl.ds(t * 128, 128)] = lists[t]
    own_copy = pltpu.make_async_copy(mbuf, meta_of(metas[0], gx), list_sems.at[0])
    own_copy.start()
    loads[-1].wait()
    flat = src.reshape(own * 8, 128)

    def moments(g, carry):
        x, y, z, m = (
            [flat[pl.ds(g * 64 + h * 4 + r, 8, stride=8), :] for h in range(2)] for r in range(4)
        )
        cbuf[pl.ds(g, 1), :] = cell_row(x, y, z, m)
        return carry

    lax.fori_loop(0, own // 8, moments, 0, unroll=4)

    def gather_tiles(dz):
        k = zs[dz]

        def gather_for(i, carry):
            r = i * nz + k
            filled = send_count[0, r]
            for s in range(2):
                obuf[k, i * 2 + s] = jnp.where(filled > s, src[send_ids[s, r]], 0.0)
            return carry

        lax.fori_loop(0, nx, gather_for, 0, unroll=min(nx, 8))

    pl.semaphore_wait(barrier, len(greeted))

    t_copy, m_copy = {}, {}
    for d in first:
        device = (xs[d], gy, gz)
        m_copy[d] = sent(mbuf, meta_of(meta_all, gx), m_send.at[d], m_recv.at[d], device)
        t_copy[d] = sent(tbuf, t_all.at[gx], t_send.at[d], t_recv.at[d], device)
    c_copies = [
        sent(cbuf, cells_all.at[gy, gz], c_send.at[d], c_recv.at[d], (gx, gy, zs[d]))
        for d in range(1, nz)
    ]
    c_copies += [
        sent(cnt_buf, cnt_all.at[gz], n_send.at[d], n_recv.at[d], (gx, gy, zs[d]))
        for d in range(1, nz)
    ]
    cells_all[gy, gz] = cbuf[...]
    o_copies = []
    gather_tiles(1)
    for d in range(1, nz):
        gather_tiles((d + 1) % nz)
        o_copies.append(
            sent(obuf.at[zs[d]], tiles_all.at[gz], o_send.at[d], o_recv.at[d], (gx, gy, zs[d]))
        )
    t_all[gx] = tbuf[...]
    meta_all[pl.ds(pl.multiple_of(gx * 1024, 1024), 1024)] = mbuf[...]
    cnt_all[gz] = cnt_buf[...]
    mine = pltpu.make_async_copy(obuf.at[gz], tiles_all.at[gz], own_sem)
    mine.start()

    for copy in c_copies:
        copy.wait_recv()
    x_copies = [
        sent(cells_all.at[gy], cells_all.at[gy], x_send.at[d], x_recv.at[d], (gx, ys[d], gz))
        for d in range(1, ny)
    ]

    half = nx // 2
    for e in range(1, half - jump + 1):
        up, down = jump + e, nx - jump - e
        for copies, ref, of, s_sems, r_sems in (
            (m_copy, meta_all, meta_of, m_send, m_recv),
            (t_copy, t_all, lambda ref, i: ref.at[i], t_send, t_recv),
        ):
            if e == 1:
                copies[jump].wait_recv()
                copies[nx - jump].wait_recv()
            if e < half - jump or copies is t_copy:
                behind = of(ref, xs[nx - jump])
                copies[up] = sent(behind, behind, s_sems.at[up], r_sems.at[up], (xs[e], gy, gz))
            if e < half - jump or copies is m_copy:
                ahead = of(ref, xs[jump])
                copies[down] = sent(ahead, ahead, s_sems.at[down], r_sems.at[down], (xs[nx - e], gy, gz))

    near_end = nx // 2
    mid_end = (near_end + nx) // 2
    stages = (range(0, near_end), range(near_end, mid_end), range(mid_end, nx))
    waited = {jump, nx - jump} if half > jump else set()

    def arrived(stage):
        copies = [own_copy] if stage == 0 else []
        for n in stages[stage]:
            d = nx - (n + 1) // 2 if n % 2 else n // 2
            if d == 0:
                continue
            if d not in waited:
                m_copy[d].wait_recv()
                t_copy[d].wait_recv()
            copy = pltpu.make_async_copy(
                meta_of(meta_all, xs[nx - d]), meta_of(metas[stage], xs[nx - d]), list_sems.at[d]
            )
            copy.start()
            copies.append(copy)
        return copies

    listed = arrived(0)
    for copy in x_copies:
        copy.wait_recv()
    blocks = own // 64

    def expand(n, carry):
        for b in range(blocks):
            cells = cells_all[n // nz, n % nz, b * 8 : b * 8 + 8, :]
            for j in range(8):
                moved = pltpu.roll(cells, 128 - PARAMS * j, 1) if j else cells
                table[pl.ds((n * blocks + b) * 64 + j * 8, 8), :] = moved
        return carry

    lax.fori_loop(0, ny * nz, expand, 0, unroll=4)

    k = iota((128, 128), 0)
    spread = jnp.concatenate(
        [jnp.where(((k & 15) == p) & (k < 48), 1.0, 0.0) for p in range(11)], axis=1
    ).astype(jnp.bfloat16)

    def far_domain(meta, n, carry):
        i = wrap(gx + nx + jnp.where((n & 1) == 1, (n + 1) >> 1, -(n >> 1)), nx)
        bounds = []
        slot = rows.at[n & 3]
        for t in range(8):
            at = i * 1024 + t * 128
            f0 = meta[at + LISTED + gx]
            bounds.append(meta[at + LISTED + gx + 1] - f0)
            for u in range(8):
                slot[t * 8 + u : t * 8 + u + 1, :] = table[pl.ds(meta[at + f0 + u], 1), :]
        high, mid, low = parts(slot[...])
        lane = iota((64, 128), 1)
        packed = jnp.where(
            lane < 16, high, jnp.where(lane < 32, pltpu.roll(mid, 16, 1), pltpu.roll(low, 32, 1))
        )
        wide = jnp.dot(packed.astype(jnp.bfloat16), spread, preferred_element_type=jnp.float32)
        values = []
        for t in range(8):
            tx, ty, tz = (t_all[i, c, t : t + 1, :] for c in range(3))
            p = lambda n: wide[t * 8 : t * 8 + 8, n * 128 : n * 128 + 128]
            values.append(far_value(p, bounds[t], tx, ty, tz))
        far_out[i] = -jnp.concatenate(values, axis=0)
        return carry

    for stage, span in enumerate(stages):
        for copy in listed:
            copy.wait()
        lax.fori_loop(
            span.start, span.stop, functools.partial(far_domain, metas[stage]), 0,
            unroll=min(4, max(1, len(span))),
        )
        if stage < 2:
            listed = arrived(stage + 1)
    for copy in o_copies:
        copy.wait()
    for copy in [*t_copy.values(), *m_copy.values(), *c_copies, *x_copies]:
        copy.wait_send()
    mine.wait()


def parts(v):
    high = v.astype(jnp.bfloat16).astype(jnp.float32)
    rest = v - high
    mid = rest.astype(jnp.bfloat16).astype(jnp.float32)
    return high, mid, rest - mid


def near_row(tile, x, y, z):
    sub = iota((8, 128), 0)
    left = jnp.concatenate([*parts(tile), jnp.where(sub < 3, 1.0, tile)], axis=0).T
    picks = []
    for c, row in enumerate((x, y, z)):
        high, mid, low = parts(jnp.broadcast_to(-row, (8, 128)))
        target = jnp.where(sub == 0, high, jnp.where(sub == 1, mid, jnp.where(sub == 2, low, 0.0)))
        for h in range(2):
            one = jnp.where(sub == h * 4 + c, 1.0, 0.0)
            picks.append(jnp.concatenate([one, one, one, target], axis=0))
    right = jnp.concatenate(picks, axis=1).astype(jnp.bfloat16)
    d = jnp.dot(left.astype(jnp.bfloat16), right, preferred_element_type=jnp.float32)
    total = jnp.zeros((8, 128), jnp.float32)
    for h in range(2):
        for s in range(0, 128, 8):
            dx, dy, dz = (
                d[s : s + 8, (2 * c + h) * 128 : (2 * c + h + 1) * 128] for c in range(3)
            )
            inv = lax.rsqrt(dx * dx + dy * dy + dz * dz + SOFT)
            total += inv * jnp.broadcast_to(left[s : s + 8, 27 + 4 * h : 28 + 4 * h], (8, 128))
    return jnp.sum(total, axis=0, keepdims=True)


def far_value(p, live, tx, ty, tz):
    dx, dy, dz = tx - p(1), ty - p(2), tz - p(3)
    r2 = dx * dx + dy * dy + dz * dz + SOFT
    inv = lax.rsqrt(r2)
    inv2 = inv * inv
    quad = dx * (p(4) * dx + p(7) * dy + p(8) * dz) + dy * (p(5) * dy + p(9) * dz) + p(6) * dz * dz
    value = inv * (p(0) + (quad - r2 * p(10)) * (inv2 * inv2))
    return jnp.sum(jnp.where(iota((8, 128), 0) < live, value, 0.0), axis=0, keepdims=True)


def walk_kernel(
    sizes, meta_in, cnt_in, lists_in, t_all, tiles, table, src,
    out, todo, rows, meta_a, meta_b, meta_c, meta_d, cnt, lists, in_sems,
):
    nx, ny, nz = sizes
    a = lax.axis_index("gx")
    gz = lax.axis_index("gz")
    near_base = LISTED + nx + 1
    metas = (meta_a, meta_b, meta_c, meta_d)
    each = meta_a.shape[0] // 1024
    copies = [pltpu.make_async_copy(cnt_in, cnt, in_sems.at[4])]
    for q in range(nx // each):
        part = meta_in.at[pl.ds(q * each * 1024, each * 1024)]
        copies.append(pltpu.make_async_copy(part, metas[q], in_sems.at[q]))
    copies.append(pltpu.make_async_copy(lists_in, lists, in_sems.at[5]))
    for copy in copies:
        copy.start()
    out[...] = jnp.zeros_like(out)

    def domain(meta, q, i, found):
        base = (i - q * each) * 1024
        n0 = meta[base + near_base + a]
        n1 = meta[base + near_base + a + 1]

        def bucket(t, carry):
            at = base + t * 128
            f0 = meta[at + LISTED + a]
            f1 = meta[at + LISTED + a + 1]
            tx, ty, tz = (t_all[i, c, pl.ds(t, 1), :] for c in range(3))

            def chunk(n, carry):
                start = f0 + n * 8
                for u in range(8):
                    rows[u : u + 1, :] = table[pl.ds(meta[at + start + u], 1), :]
                v = rows[...]
                p = lambda n: jnp.broadcast_to(v[:, n : n + 1], (8, 128))
                out[i, pl.ds(t, 1), :] -= far_value(p, f1 - start, tx, ty, tz)
                return carry

            return lax.fori_loop(1, (f1 - f0 + 7) >> 3, chunk, carry)

        longer = meta[base + LISTED + 2 * nx + 3 + a]

        @pl.when(longer >= 8)
        def _():
            alone = longer < 16
            begin = jnp.where(alone, longer & 7, 0)
            lax.fori_loop(begin, jnp.where(alone, begin + 1, 8), bucket, 0)

        def entry(e, found):
            code = meta[base + ((e >> 3) << 7) + FAR + (e & 7)]
            peer, slot = (code & 127) >> 1, code & 1
            todo[found] = (i * 8 + (code >> 7)) * 1024 + peer * (nx * 2) + i * 2 + slot
            return found + jnp.where(cnt[peer * (nx * nz) + i * nz + gz] > slot, 1, 0)

        return lax.fori_loop(n0, n1, entry, found)

    copies[0].wait()
    found = jnp.int32(0)
    for q in range(nx // each):
        copies[q + 1].wait()
        step = functools.partial(domain, metas[q], q)
        found = lax.fori_loop(q * each, (q + 1) * each, step, found)
    copies[-1].wait()
    todo[nx * 64 + 1] = found

    def away(n, carry):
        item = todo[n]
        i, t = item >> 13, (item >> 10) & 7
        row = near_row(tiles[item & 1023], *(t_all[i, c, pl.ds(t, 1), :] for c in range(3)))
        out[i, pl.ds(t, 1), :] -= row
        return carry

    lax.fori_loop(AWAY, found, away, 0)

    def own_entry(e, carry):
        code = lists[((e >> 3) << 7) + FAR + (e & 7)]
        t = code >> 7
        row = near_row(src[code & 127], *(t_all[a, c, pl.ds(t, 1), :] for c in range(3)))
        out[a, pl.ds(t, 1), :] -= row
        return carry

    lax.fori_loop(lists[near_base + nx] + OWN, lists[near_base + nx + 1], own_entry, 0)


def return_kernel(
    sizes, todo_in, lists_in, t_all, tiles, part, far_part, src,
    out, landed, near_rows, mine, todo, lists, send, recv, in_sems,
):
    nx, ny, nz = sizes
    gx, gy, gz = (lax.axis_index(n) for n in ALL)
    barrier = pltpu.get_barrier_semaphore()
    xs = [wrap(gx + d, nx) for d in range(nx)]
    far_first = sorted(range(1, nx), key=lambda d: -min(d, nx - d))
    for d in far_first:
        pl.semaphore_signal(barrier, inc=1, device_id=(xs[d], gy, gz), device_id_type=MESH)
    lane = iota((8, 128), 1)
    todo_copy = pltpu.make_async_copy(todo_in, todo, in_sems.at[0])
    lists_copy = pltpu.make_async_copy(lists_in, lists, in_sems.at[1])
    todo_copy.start()
    lists_copy.start()
    todo_copy.wait()
    lists_copy.wait()
    found = todo[nx * 64 + 1]

    def near(j, ids):
        item = jnp.where(j < found, todo[j], 0)
        bucket = item >> 10
        i, t = bucket >> 3, bucket & 7
        row = near_row(tiles[item & 1023], *(t_all[i, c, pl.ds(t, 1), :] for c in range(3)))
        near_rows[pl.ds(j, 1), :] = row
        return jnp.where(lane == j, jnp.where(j < found, bucket, -1), ids)

    near_rows[...] = jnp.zeros_like(near_rows)
    ids = lax.fori_loop(0, AWAY, near, jnp.full((8, 128), -1, jnp.int32), unroll=4)
    pick = jnp.where(iota((nx * 8, 128), 0) == jnp.broadcast_to(ids[0:1], (nx * 8, 128)), 1.0, 0.0)
    placed = sum(
        jnp.dot(pick.astype(jnp.bfloat16), v.astype(jnp.bfloat16), preferred_element_type=jnp.float32)
        for v in parts(near_rows[...])
    )
    mine[...] = part[...] + far_part[...] - placed.reshape(nx, 8, 128)

    pl.semaphore_wait(barrier, nx - 1)
    copies = []
    for d in far_first:
        copy = pltpu.make_async_remote_copy(
            src_ref=mine.at[xs[d]], dst_ref=landed.at[d - 1],
            send_sem=send.at[d], recv_sem=recv.at[d],
            device_id=(xs[d], gy, gz), device_id_type=MESH,
        )
        copy.start()
        copies.append(copy)

    n0 = lists[LISTED + nx + 1 + nx]
    n1 = lists[LISTED + nx + 1 + nx + 1]
    sub = iota((8, 128), 0)

    def own_item(j, total):
        e = n0 + j
        p = jnp.minimum(e, 8 * NEAR - 1)
        code = lists[((p >> 3) << 7) + FAR + (p & 7)]
        t = code >> 7
        tile = src[code & 127]
        row = near_row(tile, *(t_all[gx, c, pl.ds(t, 1), :] for c in range(3)))
        return total - jnp.where((sub == t) & (e < n1), row, 0.0)

    summed = lax.fori_loop(0, OWN, own_item, mine[gx], unroll=4)
    for copy in copies:
        copy.wait()
    for d in range(nx - 1):
        summed += landed[d]
    out[...] = summed


def body(sizes, targets, sources, send_ids, send_count, far_ids, near_ids, near_count):
    nx, ny, nz = sizes
    f32, i32 = jnp.float32, jnp.int32
    own = sources.shape[0]
    shape = jax.ShapeDtypeStruct
    vmem = pl.BlockSpec(memory_space=VMEM)
    smem = pl.BlockSpec(memory_space=SMEM)
    hbm = pl.BlockSpec(memory_space=pltpu.HBM)
    dma = pltpu.SemaphoreType.DMA
    in_hbm = functools.partial(pltpu.with_memory_space_constraint, memory_space=pltpu.HBM)
    tgt = jnp.transpose(targets.reshape(3, 8, 128), (1, 0, 2))
    src = jnp.transpose(sources.reshape(own, 4, 2, 128), (0, 2, 1, 3)).reshape(own, 8, 128)
    t_all, meta, tiles_all, cnt, table, far_part, lists, held = pl.pallas_call(
        functools.partial(gather_kernel, sizes),
        out_shape=(
            shape((nx, 3, 8, 128), f32), shape((nx * 1024,), i32),
            shape((nz, nx * 2, 8, 128), f32), shape((nz, 1, nx * nz), i32),
            shape((ny * nz * own, 128), f32),
            shape((nx, 8, 128), f32), shape((1024,), i32), shape((own, 8, 128), f32),
        ),
        in_specs=[hbm] * 7,
        out_specs=(vmem,) * 8,
        scratch_shapes=[
            SMEM((2, nx * nz), i32), SMEM((1, nx * nz), i32), VMEM((1, nx * nz), i32),
            SMEM((8,), i32),
            VMEM((8, FAR), i32), VMEM((8, NEAR), i32), VMEM((8, 3, 128), f32),
            VMEM((8, 128), i32), VMEM((3, 8, 128), f32),
            VMEM((nz, nx * 2, 8, 128), f32), VMEM((own // 8, 128), f32),
            VMEM((ny, nz, own // 8, 128), f32), VMEM((4, 64, 128), f32),
            SMEM((nx * 1024,), i32), SMEM((nx * 1024,), i32), SMEM((nx * 1024,), i32),
            dma((nx,)), dma((nx,)), dma((nx,)), dma((nx,)), dma((nz,)), dma((nz,)),
            dma((nz,)), dma((nz,)), dma((ny,)), dma((ny,)), dma((nz,)), dma((nz,)),
            dma, dma((nx,)), dma((8,)),
        ],
        compiler_params=pltpu.CompilerParams(
            collective_id=0, has_side_effects=True, vmem_limit_bytes=LIMIT
        ),
        name="gather",
    )(*map(in_hbm, (send_ids[0].T, send_count, near_count, far_ids, near_ids, tgt, src)))

    tiles = tiles_all.reshape(nz * nx * 2, 8, 128)
    part, todo = pl.pallas_call(
        functools.partial(walk_kernel, sizes),
        out_shape=(shape((nx, 8, 128), f32), shape((nx * 64 + 2,), i32)),
        in_specs=[vmem] * 7,
        out_specs=(vmem, smem),
        scratch_shapes=[
            VMEM((8, 128), f32), *[SMEM((max(1, nx // 4) * 1024,), i32)] * 4,
            SMEM((nz * nx * nz,), i32), SMEM((1024,), i32), dma((6,)),
        ],
        compiler_params=pltpu.CompilerParams(vmem_limit_bytes=LIMIT),
        name="walk",
    )(meta, cnt.reshape(-1), lists, t_all, tiles, table, held)

    out = pl.pallas_call(
        functools.partial(return_kernel, sizes),
        out_shape=shape((8, 128), f32),
        in_specs=[vmem] * 7,
        out_specs=vmem,
        scratch_shapes=[
            VMEM((nx - 1, 8, 128), f32), VMEM((128, 128), f32),
            VMEM((nx, 8, 128), f32), SMEM((nx * 64 + 2,), i32), SMEM((1024,), i32),
            dma((nx,)), dma((nx,)), dma((2,)),
        ],
        compiler_params=pltpu.CompilerParams(
            collective_id=1, has_side_effects=True, vmem_limit_bytes=LIMIT
        ),
        name="bring_back",
    )(todo, lists, t_all, tiles, part, far_part, held)
    return out.reshape(-1)


def solution(mesh):
    sizes = tuple(mesh.shape[n] for n in ALL)
    in_specs = (
        P(None, ALL), P(ALL, None, None), P(ALL, None, None), P(ALL, None),
        P(ALL, None), P(ALL, None), P(ALL),
    )
    return jax.shard_map(
        functools.partial(body, sizes), mesh=mesh, in_specs=in_specs, out_specs=P(ALL),
        check_vma=False,
    )
```

```python
import functools

import jax
import jax.numpy as jnp
from jax import lax
from jax.experimental import pallas as pl
from jax.experimental.pallas import tpu as pltpu
from jax.sharding import PartitionSpec as P

ALL = ("gx", "gy", "gz")
MESH = pl.DeviceIdType.MESH
SOFT = 0.01
FAR = 64
NEAR = 8
LISTED = FAR + NEAR
PARAMS = 16
LIMIT = 16 * 1024 * 1024
OWN = 24
AWAY = 28
VMEM = pltpu.VMEM
SMEM = pltpu.SMEM


def iota(shape, dim):
    return lax.broadcasted_iota(jnp.int32, shape, dim)


def sorted_lists(nx, nz, cells_per_x, own, ids, counts):
    lane = iota((8, 128), 1)
    sub = iota((8, 128), 0)
    is_far = lane < FAR
    is_near = (lane >= FAR) & (lane < LISTED)
    remote = ids - own
    rank = remote >> 1
    live = lane - FAR < counts
    near_code = sub * 128 + jnp.where(remote >= 0, (rank % nz) * 2 + (remote & 1), ids)
    holder = jnp.where(remote >= 0, rank // nz, nx)
    cell = ids % cells_per_x
    cell = cell - (cell & 63) + ((cell & 7) << 3) + ((cell >> 3) & 7)
    order = jnp.where(is_far, lane, sub * NEAR + lane - FAR)
    key = jnp.where(is_far, ids // cells_per_x, jnp.where(live, holder, nx + 1)) * 64 + order
    far_base, near_base, most_base = LISTED, LISTED + nx + 1, LISTED + 2 * nx + 3
    far_limit = jnp.where((lane >= far_base) & (lane < near_base), (lane - far_base) * 64, 0)
    near_limit = jnp.where((lane >= near_base) & (lane < most_base), (lane - near_base) * 64, 0)
    zero = jnp.zeros((8, 128), jnp.int32)
    far_place, near_place, far_start, near_start = zero, zero, zero, zero
    for e in range(FAR):
        other = jnp.broadcast_to(key[:, e : e + 1], (8, 128))
        far_place += jnp.where(other < key, 1, 0)
        far_start += jnp.where(other < far_limit, 1, 0)
    for e in range(NEAR):
        other = jnp.broadcast_to(key[:, FAR + e : FAR + e + 1], (8, 128))
        near_start += jnp.where(other < near_limit, 1, 0)
        for r in range(8):
            moved = pltpu.roll(other, r, 0) if r else other
            near_place += jnp.where(moved < key, 1, 0)
    both = jnp.where(is_far, far_place * 8192 + cell, near_place * 8192 + near_code)
    far_list, near_list = zero, zero
    for e in range(LISTED):
        entry = jnp.broadcast_to(both[:, e : e + 1], (8, 128))
        term = jnp.where((entry >> 13) == lane, entry & 8191, 0)
        if e < FAR:
            far_list += term
        else:
            near_list += term
    near_list = jnp.broadcast_to(jnp.sum(near_list, axis=0, keepdims=True), (8, 128))
    near_start = jnp.broadcast_to(jnp.sum(near_start, axis=0, keepdims=True), (8, 128))
    near_rows = zero
    for t in range(8):
        near_rows = jnp.where(sub == t, pltpu.roll(near_list, (FAR - 8 * t) % 128, 1), near_rows)
    length = pltpu.roll(far_start, 127, 1) - far_start
    top = jnp.max(length * 8 + sub, axis=0, keepdims=True) & 7
    most = jnp.sum(jnp.where(length > 8, 1, 0), axis=0, keepdims=True) * 8 + top
    most = jnp.broadcast_to(most, (8, 128))
    most = pltpu.roll(most, most_base - far_base, 1)
    out = jnp.where(is_far, far_list, jnp.where(is_near, near_rows, far_start + near_start))
    return jnp.where(lane >= most_base, most, out)


def cell_row(x, y, z, m):
    lane = iota((8, 128), 1)
    sub = iota((8, 128), 0)

    def total(*v):
        return jnp.sum(sum(p * q for p, q in zip(*v)) if len(v) == 2 else sum(v[0]), axis=1, keepdims=True)

    mass = total(m)
    cx, cy, cz = (total(v, m) / mass for v in (x, y, z))
    dx, dy, dz = ([h - c for h in v] for v, c in ((x, cx), (y, cy), (z, cz)))
    wx, wy, wz = ([h * w for h, w in zip(v, m)] for v in (dx, dy, dz))
    sxx, syy, szz = total(wx, dx), total(wy, dy), total(wz, dz)
    sxy, sxz, syz = total(wx, dy), total(wx, dz), total(wy, dz)
    values = (
        mass, cx, cy, cz, 1.5 * sxx, 1.5 * syy, 1.5 * szz,
        3.0 * sxy, 3.0 * sxz, 3.0 * syz, 0.5 * (sxx + syy + szz),
    )
    spread = jnp.zeros((8, 128), jnp.float32)
    for p, value in enumerate(values):
        spread = jnp.where(lane == sub * PARAMS + p, value, spread)
    return jnp.sum(spread, axis=0, keepdims=True)


def wrap(value, size):
    return value & (size - 1) if size & (size - 1) == 0 else lax.rem(value, size)


def gather_kernel(
    sizes, send_ids_hbm, send_count_hbm, near_count_hbm, far_hbm, near_hbm, tgt_hbm, src_hbm,
    t_all, meta_all, tiles_all, cnt_all, table, far_out, mbuf, src,
    send_ids, send_count, cnt_buf, near_count, far, near, tgt,
    ids_buf, tbuf, obuf, cbuf, cells_all, rows, meta_a, meta_b, meta_c,
    t_send, t_recv, m_send, m_recv, o_send, o_recv, c_send, c_recv, x_send, x_recv, n_send, n_recv,
    own_sem, list_sems, in_sems,
):
    nx, ny, nz = sizes
    gx, gy, gz = (lax.axis_index(n) for n in ALL)
    own = src.shape[0]
    jump = max(1, nx // 4)
    metas = (meta_a, meta_b, meta_c)
    barrier = pltpu.get_barrier_semaphore()
    loads = [
        pltpu.make_async_copy(source, dest, in_sems.at[n])
        for n, (source, dest) in enumerate((
            (send_ids_hbm, send_ids), (send_count_hbm, send_count),
            (send_count_hbm, cnt_buf), (near_count_hbm, near_count),
            (far_hbm, far), (near_hbm, near), (tgt_hbm, tgt), (src_hbm, src),
        ))
    ]
    for load in loads:
        load.start()
    xs = [wrap(gx + d, nx) for d in range(nx)]
    ys = [wrap(gy + d, ny) for d in range(ny)]
    zs = [wrap(gz + d, nz) for d in range(nz)]
    first = sorted((d for d in range(1, nx) if min(d, nx - d) <= jump), key=lambda d: -min(d, nx - d))
    greeted = [(xs[d], gy, gz) for d in first]
    greeted += [(gx, gy, zs[d]) for d in range(1, nz)]
    greeted += [(gx, ys[d], gz) for d in range(1, ny)]
    for device in greeted:
        pl.semaphore_signal(barrier, inc=1, device_id=device, device_id_type=MESH)

    def sent(source, dest, s_sem, r_sem, device):
        copy = pltpu.make_async_remote_copy(
            src_ref=source, dst_ref=dest, send_sem=s_sem, recv_sem=r_sem,
            device_id=device, device_id_type=MESH,
        )
        copy.start()
        return copy

    def meta_of(ref, i):
        return ref.at[pl.ds(pl.multiple_of(i * 1024, 1024), 1024)]

    for load in loads[:-1]:
        load.wait()
    for t in range(8):
        for c in range(3):
            tbuf[c, t : t + 1, :] = tgt[t, c : c + 1, :]
    ids_buf[...] = jnp.zeros((8, 128), jnp.int32)
    ids_buf[:, 0:FAR] = far[...]
    ids_buf[:, FAR:LISTED] = near[...]
    sub = iota((8, 128), 0)
    counts = jnp.zeros((8, 128), jnp.int32)
    for t in range(8):
        counts = jnp.where(sub == t, near_count[t], counts)
    lists = sorted_lists(nx, nz, ny * nz * own, own, ids_buf[...], counts)
    for t in range(8):
        mbuf[pl.ds(t * 128, 128)] = lists[t]
    own_copy = pltpu.make_async_copy(mbuf, meta_of(metas[0], gx), list_sems.at[0])
    own_copy.start()
    loads[-1].wait()
    flat = src.reshape(own * 8, 128)

    def moments(g, carry):
        x, y, z, m = (
            [flat[pl.ds(g * 64 + h * 4 + r, 8, stride=8), :] for h in range(2)] for r in range(4)
        )
        cbuf[pl.ds(g, 1), :] = cell_row(x, y, z, m)
        return carry

    lax.fori_loop(0, own // 8, moments, 0, unroll=4)

    def gather_tiles(dz):
        k = zs[dz]

        def gather_for(i, carry):
            r = i * nz + k
            filled = send_count[0, r]
            for s in range(2):
                obuf[k, i * 2 + s] = jnp.where(filled > s, src[send_ids[s, r]], 0.0)
            return carry

        lax.fori_loop(0, nx, gather_for, 0, unroll=min(nx, 8))

    pl.semaphore_wait(barrier, len(greeted))

    t_copy, m_copy = {}, {}
    for d in first:
        device = (xs[d], gy, gz)
        m_copy[d] = sent(mbuf, meta_of(meta_all, gx), m_send.at[d], m_recv.at[d], device)
        t_copy[d] = sent(tbuf, t_all.at[gx], t_send.at[d], t_recv.at[d], device)
    c_copies = [
        sent(cbuf, cells_all.at[gy, gz], c_send.at[d], c_recv.at[d], (gx, gy, zs[d]))
        for d in range(1, nz)
    ]
    c_copies += [
        sent(cnt_buf, cnt_all.at[gz], n_send.at[d], n_recv.at[d], (gx, gy, zs[d]))
        for d in range(1, nz)
    ]
    cells_all[gy, gz] = cbuf[...]
    o_copies = []
    middle = nz // 2
    order = [middle, *(d for d in (2, nz - 2, 3) if d != middle and 0 < d < nz)]
    order = list(dict.fromkeys(order))
    later = [d for d in range(1, nz) if d not in order]

    def send_tiles(d):
        o_copies.append(
            sent(obuf.at[zs[d]], tiles_all.at[gz], o_send.at[d], o_recv.at[d], (gx, gy, zs[d]))
        )

    gather_tiles(order[0])
    for d, following in zip(order, [*order[1:], None]):
        if following:
            gather_tiles(following)
        send_tiles(d)
    for d in [*later, 0]:
        gather_tiles(d)
    t_all[gx] = tbuf[...]
    meta_all[pl.ds(pl.multiple_of(gx * 1024, 1024), 1024)] = mbuf[...]
    cnt_all[gz] = cnt_buf[...]
    mine = pltpu.make_async_copy(obuf.at[gz], tiles_all.at[gz], own_sem)
    mine.start()

    for copy in c_copies:
        copy.wait_recv()
    x_copies = [
        sent(cells_all.at[gy], cells_all.at[gy], x_send.at[d], x_recv.at[d], (gx, ys[d], gz))
        for d in range(1, ny)
    ]

    half = nx // 2
    for e in range(1, half - jump + 1):
        up, down = jump + e, nx - jump - e
        for copies, ref, of, s_sems, r_sems in (
            (m_copy, meta_all, meta_of, m_send, m_recv),
            (t_copy, t_all, lambda ref, i: ref.at[i], t_send, t_recv),
        ):
            if e == 1:
                copies[jump].wait_recv()
                copies[nx - jump].wait_recv()
            if e < half - jump or copies is t_copy:
                behind = of(ref, xs[nx - jump])
                copies[up] = sent(behind, behind, s_sems.at[up], r_sems.at[up], (xs[e], gy, gz))
            if e < half - jump or copies is m_copy:
                ahead = of(ref, xs[jump])
                copies[down] = sent(ahead, ahead, s_sems.at[down], r_sems.at[down], (xs[nx - e], gy, gz))

    for d in later:
        send_tiles(d)

    near_end = nx // 2
    mid_end = (near_end + nx) // 2
    stages = (range(0, near_end), range(near_end, mid_end), range(mid_end, nx))
    waited = {jump, nx - jump} if half > jump else set()

    def arrived(stage):
        copies = [own_copy] if stage == 0 else []
        for n in stages[stage]:
            d = nx - (n + 1) // 2 if n % 2 else n // 2
            if d == 0:
                continue
            if d not in waited:
                m_copy[d].wait_recv()
                t_copy[d].wait_recv()
            copy = pltpu.make_async_copy(
                meta_of(meta_all, xs[nx - d]), meta_of(metas[stage], xs[nx - d]), list_sems.at[d]
            )
            copy.start()
            copies.append(copy)
        return copies

    listed = arrived(0)
    for copy in x_copies:
        copy.wait_recv()
    blocks = own // 64

    def expand(n, carry):
        for b in range(blocks):
            cells = cells_all[n // nz, n % nz, b * 8 : b * 8 + 8, :]
            for j in range(8):
                moved = pltpu.roll(cells, 128 - PARAMS * j, 1) if j else cells
                table[pl.ds((n * blocks + b) * 64 + j * 8, 8), :] = moved
        return carry

    lax.fori_loop(0, ny * nz, expand, 0, unroll=4)

    k = iota((128, 128), 0)
    spread = jnp.concatenate(
        [jnp.where(((k & 15) == p) & (k < 48), 1.0, 0.0) for p in range(11)], axis=1
    ).astype(jnp.bfloat16)

    def far_domain(meta, n, carry):
        i = wrap(gx + nx + jnp.where((n & 1) == 1, (n + 1) >> 1, -(n >> 1)), nx)
        bounds = []
        slot = rows.at[n & 3]
        for t in range(8):
            at = i * 1024 + t * 128
            f0 = meta[at + LISTED + gx]
            bounds.append(meta[at + LISTED + gx + 1] - f0)
            for u in range(8):
                slot[t * 8 + u : t * 8 + u + 1, :] = table[pl.ds(meta[at + f0 + u], 1), :]
        high, mid, low = parts(slot[...])
        lane = iota((64, 128), 1)
        packed = jnp.where(
            lane < 16, high, jnp.where(lane < 32, pltpu.roll(mid, 16, 1), pltpu.roll(low, 32, 1))
        )
        wide = jnp.dot(packed.astype(jnp.bfloat16), spread, preferred_element_type=jnp.float32)
        values = []
        for t in range(8):
            tx, ty, tz = (t_all[i, c, t : t + 1, :] for c in range(3))
            p = lambda n: wide[t * 8 : t * 8 + 8, n * 128 : n * 128 + 128]
            values.append(far_value(p, bounds[t], tx, ty, tz))
        far_out[i] = -jnp.concatenate(values, axis=0)
        return carry

    for stage, span in enumerate(stages):
        for copy in listed:
            copy.wait()
        lax.fori_loop(
            span.start, span.stop, functools.partial(far_domain, metas[stage]), 0,
            unroll=min(4, max(1, len(span))),
        )
        if stage < 2:
            listed = arrived(stage + 1)
    for copy in o_copies:
        copy.wait()
    for copy in [*t_copy.values(), *m_copy.values(), *c_copies, *x_copies]:
        copy.wait_send()
    mine.wait()


def parts(v):
    high = v.astype(jnp.bfloat16).astype(jnp.float32)
    rest = v - high
    mid = rest.astype(jnp.bfloat16).astype(jnp.float32)
    return high, mid, rest - mid


def near_row(tile, x, y, z):
    sub = iota((8, 128), 0)
    left = jnp.concatenate([*parts(tile), jnp.where(sub < 3, 1.0, tile)], axis=0).T
    picks = []
    for c, row in enumerate((x, y, z)):
        high, mid, low = parts(jnp.broadcast_to(-row, (8, 128)))
        target = jnp.where(sub == 0, high, jnp.where(sub == 1, mid, jnp.where(sub == 2, low, 0.0)))
        for h in range(2):
            one = jnp.where(sub == h * 4 + c, 1.0, 0.0)
            picks.append(jnp.concatenate([one, one, one, target], axis=0))
    right = jnp.concatenate(picks, axis=1).astype(jnp.bfloat16)
    d = jnp.dot(left.astype(jnp.bfloat16), right, preferred_element_type=jnp.float32)
    total = jnp.zeros((8, 128), jnp.float32)
    for h in range(2):
        for s in range(0, 128, 8):
            dx, dy, dz = (
                d[s : s + 8, (2 * c + h) * 128 : (2 * c + h + 1) * 128] for c in range(3)
            )
            inv = lax.rsqrt(dx * dx + dy * dy + dz * dz + SOFT)
            total += inv * jnp.broadcast_to(left[s : s + 8, 27 + 4 * h : 28 + 4 * h], (8, 128))
    return jnp.sum(total, axis=0, keepdims=True)


def far_value(p, live, tx, ty, tz):
    dx, dy, dz = tx - p(1), ty - p(2), tz - p(3)
    r2 = dx * dx + dy * dy + dz * dz + SOFT
    inv = lax.rsqrt(r2)
    inv2 = inv * inv
    quad = dx * (p(4) * dx + p(7) * dy + p(8) * dz) + dy * (p(5) * dy + p(9) * dz) + p(6) * dz * dz
    value = inv * (p(0) + (quad - r2 * p(10)) * (inv2 * inv2))
    return jnp.sum(jnp.where(iota((8, 128), 0) < live, value, 0.0), axis=0, keepdims=True)


def walk_kernel(
    sizes, meta_in, cnt_in, lists_in, t_all, tiles, table, src,
    out, todo, rows, meta_a, meta_b, meta_c, meta_d, cnt, lists, in_sems,
):
    nx, ny, nz = sizes
    a = lax.axis_index("gx")
    gz = lax.axis_index("gz")
    near_base = LISTED + nx + 1
    metas = (meta_a, meta_b, meta_c, meta_d)
    each = meta_a.shape[0] // 1024
    copies = [pltpu.make_async_copy(cnt_in, cnt, in_sems.at[4])]
    for q in range(nx // each):
        part = meta_in.at[pl.ds(q * each * 1024, each * 1024)]
        copies.append(pltpu.make_async_copy(part, metas[q], in_sems.at[q]))
    copies.append(pltpu.make_async_copy(lists_in, lists, in_sems.at[5]))
    for copy in copies:
        copy.start()
    out[...] = jnp.zeros_like(out)

    def domain(meta, q, i, found):
        base = (i - q * each) * 1024
        n0 = meta[base + near_base + a]
        n1 = meta[base + near_base + a + 1]

        def bucket(t, carry):
            at = base + t * 128
            f0 = meta[at + LISTED + a]
            f1 = meta[at + LISTED + a + 1]
            tx, ty, tz = (t_all[i, c, pl.ds(t, 1), :] for c in range(3))

            def chunk(n, carry):
                start = f0 + n * 8
                for u in range(8):
                    rows[u : u + 1, :] = table[pl.ds(meta[at + start + u], 1), :]
                v = rows[...]
                p = lambda n: jnp.broadcast_to(v[:, n : n + 1], (8, 128))
                out[i, pl.ds(t, 1), :] -= far_value(p, f1 - start, tx, ty, tz)
                return carry

            return lax.fori_loop(1, (f1 - f0 + 7) >> 3, chunk, carry)

        longer = meta[base + LISTED + 2 * nx + 3 + a]

        @pl.when(longer >= 8)
        def _():
            alone = longer < 16
            begin = jnp.where(alone, longer & 7, 0)
            lax.fori_loop(begin, jnp.where(alone, begin + 1, 8), bucket, 0)

        def entry(e, found):
            code = meta[base + ((e >> 3) << 7) + FAR + (e & 7)]
            peer, slot = (code & 127) >> 1, code & 1
            todo[found] = (i * 8 + (code >> 7)) * 1024 + peer * (nx * 2) + i * 2 + slot
            return found + jnp.where(cnt[peer * (nx * nz) + i * nz + gz] > slot, 1, 0)

        return lax.fori_loop(n0, n1, entry, found)

    copies[0].wait()
    found = jnp.int32(0)
    for q in range(nx // each):
        copies[q + 1].wait()
        step = functools.partial(domain, metas[q], q)
        found = lax.fori_loop(q * each, (q + 1) * each, step, found)
    copies[-1].wait()
    todo[nx * 64 + 1] = found

    def away(n, carry):
        item = todo[n]
        i, t = item >> 13, (item >> 10) & 7
        row = near_row(tiles[item & 1023], *(t_all[i, c, pl.ds(t, 1), :] for c in range(3)))
        out[i, pl.ds(t, 1), :] -= row
        return carry

    lax.fori_loop(AWAY, found, away, 0)

    def own_entry(e, carry):
        code = lists[((e >> 3) << 7) + FAR + (e & 7)]
        t = code >> 7
        row = near_row(src[code & 127], *(t_all[a, c, pl.ds(t, 1), :] for c in range(3)))
        out[a, pl.ds(t, 1), :] -= row
        return carry

    lax.fori_loop(lists[near_base + nx] + OWN, lists[near_base + nx + 1], own_entry, 0)


def return_kernel(
    sizes, todo_in, lists_in, t_all, tiles, part, far_part, src,
    out, landed, near_rows, mine, todo, lists, send, recv, in_sems,
):
    nx, ny, nz = sizes
    gx, gy, gz = (lax.axis_index(n) for n in ALL)
    barrier = pltpu.get_barrier_semaphore()
    xs = [wrap(gx + d, nx) for d in range(nx)]
    far_first = sorted(range(1, nx), key=lambda d: -min(d, nx - d))
    for d in far_first:
        pl.semaphore_signal(barrier, inc=1, device_id=(xs[d], gy, gz), device_id_type=MESH)
    lane = iota((8, 128), 1)
    todo_copy = pltpu.make_async_copy(todo_in, todo, in_sems.at[0])
    lists_copy = pltpu.make_async_copy(lists_in, lists, in_sems.at[1])
    todo_copy.start()
    lists_copy.start()
    todo_copy.wait()
    lists_copy.wait()
    found = todo[nx * 64 + 1]

    def near(j, ids):
        item = jnp.where(j < found, todo[j], 0)
        bucket = item >> 10
        i, t = bucket >> 3, bucket & 7
        row = near_row(tiles[item & 1023], *(t_all[i, c, pl.ds(t, 1), :] for c in range(3)))
        near_rows[pl.ds(j, 1), :] = row
        return jnp.where(lane == j, jnp.where(j < found, bucket, -1), ids)

    near_rows[...] = jnp.zeros_like(near_rows)
    ids = lax.fori_loop(0, AWAY, near, jnp.full((8, 128), -1, jnp.int32), unroll=4)
    pick = jnp.where(iota((nx * 8, 128), 0) == jnp.broadcast_to(ids[0:1], (nx * 8, 128)), 1.0, 0.0)
    placed = sum(
        jnp.dot(pick.astype(jnp.bfloat16), v.astype(jnp.bfloat16), preferred_element_type=jnp.float32)
        for v in parts(near_rows[...])
    )
    mine[...] = part[...] + far_part[...] - placed.reshape(nx, 8, 128)

    pl.semaphore_wait(barrier, nx - 1)
    copies = []
    for d in far_first:
        copy = pltpu.make_async_remote_copy(
            src_ref=mine.at[xs[d]], dst_ref=landed.at[d - 1],
            send_sem=send.at[d], recv_sem=recv.at[d],
            device_id=(xs[d], gy, gz), device_id_type=MESH,
        )
        copy.start()
        copies.append(copy)

    n0 = lists[LISTED + nx + 1 + nx]
    n1 = lists[LISTED + nx + 1 + nx + 1]
    sub = iota((8, 128), 0)

    def own_item(j, total):
        e = n0 + j
        p = jnp.minimum(e, 8 * NEAR - 1)
        code = lists[((p >> 3) << 7) + FAR + (p & 7)]
        t = code >> 7
        tile = src[code & 127]
        row = near_row(tile, *(t_all[gx, c, pl.ds(t, 1), :] for c in range(3)))
        return total - jnp.where((sub == t) & (e < n1), row, 0.0)

    summed = lax.fori_loop(0, OWN, own_item, mine[gx], unroll=4)
    for copy in copies:
        copy.wait()
    for d in range(nx - 1):
        summed += landed[d]
    out[...] = summed


def body(sizes, targets, sources, send_ids, send_count, far_ids, near_ids, near_count):
    nx, ny, nz = sizes
    f32, i32 = jnp.float32, jnp.int32
    own = sources.shape[0]
    shape = jax.ShapeDtypeStruct
    vmem = pl.BlockSpec(memory_space=VMEM)
    smem = pl.BlockSpec(memory_space=SMEM)
    hbm = pl.BlockSpec(memory_space=pltpu.HBM)
    dma = pltpu.SemaphoreType.DMA
    in_hbm = functools.partial(pltpu.with_memory_space_constraint, memory_space=pltpu.HBM)
    tgt = jnp.transpose(targets.reshape(3, 8, 128), (1, 0, 2))
    src = jnp.transpose(sources.reshape(own, 4, 2, 128), (0, 2, 1, 3)).reshape(own, 8, 128)
    t_all, meta, tiles_all, cnt, table, far_part, lists, held = pl.pallas_call(
        functools.partial(gather_kernel, sizes),
        out_shape=(
            shape((nx, 3, 8, 128), f32), shape((nx * 1024,), i32),
            shape((nz, nx * 2, 8, 128), f32), shape((nz, 1, nx * nz), i32),
            shape((ny * nz * own, 128), f32),
            shape((nx, 8, 128), f32), shape((1024,), i32), shape((own, 8, 128), f32),
        ),
        in_specs=[hbm] * 7,
        out_specs=(vmem,) * 8,
        scratch_shapes=[
            SMEM((2, nx * nz), i32), SMEM((1, nx * nz), i32), VMEM((1, nx * nz), i32),
            SMEM((8,), i32),
            VMEM((8, FAR), i32), VMEM((8, NEAR), i32), VMEM((8, 3, 128), f32),
            VMEM((8, 128), i32), VMEM((3, 8, 128), f32),
            VMEM((nz, nx * 2, 8, 128), f32), VMEM((own // 8, 128), f32),
            VMEM((ny, nz, own // 8, 128), f32), VMEM((4, 64, 128), f32),
            SMEM((nx * 1024,), i32), SMEM((nx * 1024,), i32), SMEM((nx * 1024,), i32),
            dma((nx,)), dma((nx,)), dma((nx,)), dma((nx,)), dma((nz,)), dma((nz,)),
            dma((nz,)), dma((nz,)), dma((ny,)), dma((ny,)), dma((nz,)), dma((nz,)),
            dma, dma((nx,)), dma((8,)),
        ],
        compiler_params=pltpu.CompilerParams(
            collective_id=0, has_side_effects=True, vmem_limit_bytes=LIMIT
        ),
        name="gather",
    )(*map(in_hbm, (send_ids[0].T, send_count, near_count, far_ids, near_ids, tgt, src)))

    tiles = tiles_all.reshape(nz * nx * 2, 8, 128)
    part, todo = pl.pallas_call(
        functools.partial(walk_kernel, sizes),
        out_shape=(shape((nx, 8, 128), f32), shape((nx * 64 + 2,), i32)),
        in_specs=[vmem] * 7,
        out_specs=(vmem, smem),
        scratch_shapes=[
            VMEM((8, 128), f32), *[SMEM((max(1, nx // 4) * 1024,), i32)] * 4,
            SMEM((nz * nx * nz,), i32), SMEM((1024,), i32), dma((6,)),
        ],
        compiler_params=pltpu.CompilerParams(vmem_limit_bytes=LIMIT),
        name="walk",
    )(meta, cnt.reshape(-1), lists, t_all, tiles, table, held)

    out = pl.pallas_call(
        functools.partial(return_kernel, sizes),
        out_shape=shape((8, 128), f32),
        in_specs=[vmem] * 7,
        out_specs=vmem,
        scratch_shapes=[
            VMEM((nx - 1, 8, 128), f32), VMEM((128, 128), f32),
            VMEM((nx, 8, 128), f32), SMEM((nx * 64 + 2,), i32), SMEM((1024,), i32),
            dma((nx,)), dma((nx,)), dma((2,)),
        ],
        compiler_params=pltpu.CompilerParams(
            collective_id=1, has_side_effects=True, vmem_limit_bytes=LIMIT
        ),
        name="bring_back",
    )(todo, lists, t_all, tiles, part, far_part, held)
    return out.reshape(-1)


def solution(mesh):
    sizes = tuple(mesh.shape[n] for n in ALL)
    in_specs = (
        P(None, ALL), P(ALL, None, None), P(ALL, None, None), P(ALL, None),
        P(ALL, None), P(ALL, None), P(ALL),
    )
    return jax.shard_map(
        functools.partial(body, sizes), mesh=mesh, in_specs=in_specs, out_specs=P(ALL),
        check_vma=False,
    )
```

```python
import functools

import jax
import jax.numpy as jnp
from jax import lax
from jax.experimental import pallas as pl
from jax.experimental.pallas import tpu as pltpu
from jax.sharding import PartitionSpec as P

ALL = ("gx", "gy", "gz")
MESH = pl.DeviceIdType.MESH
SOFT = 0.01
FAR = 64
NEAR = 8
LISTED = FAR + NEAR
PARAMS = 16
LIMIT = 16 * 1024 * 1024
OWN = 24
AWAY = 28
VMEM = pltpu.VMEM
SMEM = pltpu.SMEM


def iota(shape, dim):
    return lax.broadcasted_iota(jnp.int32, shape, dim)


def sorted_lists(nx, nz, cells_per_x, own, ids, counts):
    lane = iota((8, 128), 1)
    sub = iota((8, 128), 0)
    is_far = lane < FAR
    is_near = (lane >= FAR) & (lane < LISTED)
    remote = ids - own
    rank = remote >> 1
    live = lane - FAR < counts
    near_code = sub * 128 + jnp.where(remote >= 0, (rank % nz) * 2 + (remote & 1), ids)
    holder = jnp.where(remote >= 0, rank // nz, nx)
    cell = ids % cells_per_x
    cell = cell - (cell & 63) + ((cell & 7) << 3) + ((cell >> 3) & 7)
    order = jnp.where(is_far, lane, sub * NEAR + lane - FAR)
    key = jnp.where(is_far, ids // cells_per_x, jnp.where(live, holder, nx + 1)) * 64 + order
    far_base, near_base, most_base = LISTED, LISTED + nx + 1, LISTED + 2 * nx + 3
    far_limit = jnp.where((lane >= far_base) & (lane < near_base), (lane - far_base) * 64, 0)
    near_limit = jnp.where((lane >= near_base) & (lane < most_base), (lane - near_base) * 64, 0)
    zero = jnp.zeros((8, 128), jnp.int32)
    far_place, near_place, far_start, near_start = zero, zero, zero, zero
    for e in range(FAR):
        other = jnp.broadcast_to(key[:, e : e + 1], (8, 128))
        far_place += jnp.where(other < key, 1, 0)
        far_start += jnp.where(other < far_limit, 1, 0)
    for e in range(NEAR):
        other = jnp.broadcast_to(key[:, FAR + e : FAR + e + 1], (8, 128))
        near_start += jnp.where(other < near_limit, 1, 0)
        for r in range(8):
            moved = pltpu.roll(other, r, 0) if r else other
            near_place += jnp.where(moved < key, 1, 0)
    both = jnp.where(is_far, far_place * 8192 + cell, near_place * 8192 + near_code)
    far_list, near_list = zero, zero
    for e in range(LISTED):
        entry = jnp.broadcast_to(both[:, e : e + 1], (8, 128))
        term = jnp.where((entry >> 13) == lane, entry & 8191, 0)
        if e < FAR:
            far_list += term
        else:
            near_list += term
    near_list = jnp.broadcast_to(jnp.sum(near_list, axis=0, keepdims=True), (8, 128))
    near_start = jnp.broadcast_to(jnp.sum(near_start, axis=0, keepdims=True), (8, 128))
    near_rows = zero
    for t in range(8):
        near_rows = jnp.where(sub == t, pltpu.roll(near_list, (FAR - 8 * t) % 128, 1), near_rows)
    length = pltpu.roll(far_start, 127, 1) - far_start
    top = jnp.max(length * 8 + sub, axis=0, keepdims=True) & 7
    most = jnp.sum(jnp.where(length > 8, 1, 0), axis=0, keepdims=True) * 8 + top
    most = jnp.broadcast_to(most, (8, 128))
    most = pltpu.roll(most, most_base - far_base, 1)
    out = jnp.where(is_far, far_list, jnp.where(is_near, near_rows, far_start + near_start))
    return jnp.where(lane >= most_base, most, out)


def cell_row(x, y, z, m):
    lane = iota((8, 128), 1)
    sub = iota((8, 128), 0)

    def total(*v):
        return jnp.sum(sum(p * q for p, q in zip(*v)) if len(v) == 2 else sum(v[0]), axis=1, keepdims=True)

    mass = total(m)
    cx, cy, cz = (total(v, m) / mass for v in (x, y, z))
    dx, dy, dz = ([h - c for h in v] for v, c in ((x, cx), (y, cy), (z, cz)))
    wx, wy, wz = ([h * w for h, w in zip(v, m)] for v in (dx, dy, dz))
    sxx, syy, szz = total(wx, dx), total(wy, dy), total(wz, dz)
    sxy, sxz, syz = total(wx, dy), total(wx, dz), total(wy, dz)
    values = (
        mass, cx, cy, cz, 1.5 * sxx, 1.5 * syy, 1.5 * szz,
        3.0 * sxy, 3.0 * sxz, 3.0 * syz, 0.5 * (sxx + syy + szz),
    )
    spread = jnp.zeros((8, 128), jnp.float32)
    for p, value in enumerate(values):
        spread = jnp.where(lane == sub * PARAMS + p, value, spread)
    return jnp.sum(spread, axis=0, keepdims=True)


def wrap(value, size):
    return value & (size - 1) if size & (size - 1) == 0 else lax.rem(value, size)


def gather_kernel(
    sizes, send_ids_hbm, send_count_hbm, near_count_hbm, far_hbm, near_hbm, tgt_hbm, src_hbm,
    t_all, meta_all, tiles_all, cnt_all, table, far_out, mbuf, src,
    send_ids, send_count, cnt_buf, near_count, far, near, tgt,
    ids_buf, tbuf, obuf, cbuf, cells_all, rows, meta_a, meta_b, meta_c,
    t_send, t_recv, m_send, m_recv, o_send, o_recv, c_send, c_recv, x_send, x_recv, n_send, n_recv,
    own_sem, list_sems, in_sems,
):
    nx, ny, nz = sizes
    gx, gy, gz = (lax.axis_index(n) for n in ALL)
    own = src.shape[0]
    jump = max(1, nx // 4)
    metas = (meta_a, meta_b, meta_c)
    barrier = pltpu.get_barrier_semaphore()
    loads = [
        pltpu.make_async_copy(source, dest, in_sems.at[n])
        for n, (source, dest) in enumerate((
            (send_ids_hbm, send_ids), (send_count_hbm, send_count),
            (send_count_hbm, cnt_buf), (near_count_hbm, near_count),
            (far_hbm, far), (near_hbm, near), (tgt_hbm, tgt), (src_hbm, src),
        ))
    ]
    for load in loads:
        load.start()
    xs = [wrap(gx + d, nx) for d in range(nx)]
    ys = [wrap(gy + d, ny) for d in range(ny)]
    zs = [wrap(gz + d, nz) for d in range(nz)]
    first = sorted((d for d in range(1, nx) if min(d, nx - d) <= jump), key=lambda d: -min(d, nx - d))
    greeted = [(xs[d], gy, gz) for d in first]
    greeted += [(gx, gy, zs[d]) for d in range(1, nz)]
    greeted += [(gx, ys[d], gz) for d in range(1, ny)]
    for device in greeted:
        pl.semaphore_signal(barrier, inc=1, device_id=device, device_id_type=MESH)

    def sent(source, dest, s_sem, r_sem, device):
        copy = pltpu.make_async_remote_copy(
            src_ref=source, dst_ref=dest, send_sem=s_sem, recv_sem=r_sem,
            device_id=device, device_id_type=MESH,
        )
        copy.start()
        return copy

    def meta_of(ref, i):
        return ref.at[pl.ds(pl.multiple_of(i * 1024, 1024), 1024)]

    for load in loads[:-1]:
        load.wait()
    for t in range(8):
        for c in range(3):
            tbuf[c, t : t + 1, :] = tgt[t, c : c + 1, :]
    ids_buf[...] = jnp.zeros((8, 128), jnp.int32)
    ids_buf[:, 0:FAR] = far[...]
    ids_buf[:, FAR:LISTED] = near[...]
    sub = iota((8, 128), 0)
    counts = jnp.zeros((8, 128), jnp.int32)
    for t in range(8):
        counts = jnp.where(sub == t, near_count[t], counts)
    lists = sorted_lists(nx, nz, ny * nz * own, own, ids_buf[...], counts)
    for t in range(8):
        mbuf[pl.ds(t * 128, 128)] = lists[t]
    own_copy = pltpu.make_async_copy(mbuf, meta_of(metas[0], gx), list_sems.at[0])
    own_copy.start()
    loads[-1].wait()
    flat = src.reshape(own * 8, 128)

    def moments(g, carry):
        x, y, z, m = (
            [flat[pl.ds(g * 64 + h * 4 + r, 8, stride=8), :] for h in range(2)] for r in range(4)
        )
        cbuf[pl.ds(g, 1), :] = cell_row(x, y, z, m)
        return carry

    lax.fori_loop(0, own // 8, moments, 0, unroll=4)

    def gather_tiles(dz):
        k = zs[dz]

        def gather_for(i, carry):
            r = i * nz + k
            filled = send_count[0, r]
            for s in range(2):
                obuf[k, i * 2 + s] = jnp.where(filled > s, src[send_ids[s, r]], 0.0)
            return carry

        lax.fori_loop(0, nx, gather_for, 0, unroll=min(nx, 8))

    pl.semaphore_wait(barrier, len(greeted))

    t_copy, m_copy = {}, {}

    def send_own(d):
        device = (xs[d], gy, gz)
        m_copy[d] = sent(mbuf, meta_of(meta_all, gx), m_send.at[d], m_recv.at[d], device)
        t_copy[d] = sent(tbuf, t_all.at[gx], t_send.at[d], t_recv.at[d], device)

    to_forward = [d for d in first if min(d, nx - d) == jump]
    for d in to_forward:
        send_own(d)
    c_copies = [
        sent(cbuf, cells_all.at[gy, gz], c_send.at[d], c_recv.at[d], (gx, gy, zs[d]))
        for d in range(1, nz)
    ]
    c_copies += [
        sent(cnt_buf, cnt_all.at[gz], n_send.at[d], n_recv.at[d], (gx, gy, zs[d]))
        for d in range(1, nz)
    ]
    cells_all[gy, gz] = cbuf[...]
    o_copies = []
    middle = nz // 2
    order = [middle, *(d for d in (2, nz - 2, 3) if d != middle and 0 < d < nz)]
    order = list(dict.fromkeys(order))
    later = [d for d in range(1, nz) if d not in order]

    def send_tiles(d):
        o_copies.append(
            sent(obuf.at[zs[d]], tiles_all.at[gz], o_send.at[d], o_recv.at[d], (gx, gy, zs[d]))
        )

    gather_tiles(order[0])
    for d, following in zip(order, [*order[1:], None]):
        if following:
            gather_tiles(following)
        send_tiles(d)
    for d in first:
        if d not in to_forward:
            send_own(d)
    for d in [*later, 0]:
        gather_tiles(d)
    t_all[gx] = tbuf[...]
    meta_all[pl.ds(pl.multiple_of(gx * 1024, 1024), 1024)] = mbuf[...]
    cnt_all[gz] = cnt_buf[...]
    mine = pltpu.make_async_copy(obuf.at[gz], tiles_all.at[gz], own_sem)
    mine.start()

    for copy in c_copies:
        copy.wait_recv()
    x_copies = [
        sent(cells_all.at[gy], cells_all.at[gy], x_send.at[d], x_recv.at[d], (gx, ys[d], gz))
        for d in range(1, ny)
    ]

    half = nx // 2
    for e in range(1, half - jump + 1):
        up, down = jump + e, nx - jump - e
        for copies, ref, of, s_sems, r_sems in (
            (m_copy, meta_all, meta_of, m_send, m_recv),
            (t_copy, t_all, lambda ref, i: ref.at[i], t_send, t_recv),
        ):
            if e == 1:
                copies[jump].wait_recv()
                copies[nx - jump].wait_recv()
            if e < half - jump or copies is t_copy:
                behind = of(ref, xs[nx - jump])
                copies[up] = sent(behind, behind, s_sems.at[up], r_sems.at[up], (xs[e], gy, gz))
            if e < half - jump or copies is m_copy:
                ahead = of(ref, xs[jump])
                copies[down] = sent(ahead, ahead, s_sems.at[down], r_sems.at[down], (xs[nx - e], gy, gz))

    for d in later:
        send_tiles(d)

    near_end = nx // 2
    mid_end = (near_end + nx) // 2
    stages = (range(0, near_end), range(near_end, mid_end), range(mid_end, nx))
    waited = {jump, nx - jump} if half > jump else set()

    def arrived(stage):
        copies = [own_copy] if stage == 0 else []
        for n in stages[stage]:
            d = nx - (n + 1) // 2 if n % 2 else n // 2
            if d == 0:
                continue
            if d not in waited:
                m_copy[d].wait_recv()
                t_copy[d].wait_recv()
            copy = pltpu.make_async_copy(
                meta_of(meta_all, xs[nx - d]), meta_of(metas[stage], xs[nx - d]), list_sems.at[d]
            )
            copy.start()
            copies.append(copy)
        return copies

    listed = arrived(0)
    for copy in x_copies:
        copy.wait_recv()
    blocks = own // 64

    def expand(n, carry):
        for b in range(blocks):
            cells = cells_all[n // nz, n % nz, b * 8 : b * 8 + 8, :]
            for j in range(8):
                moved = pltpu.roll(cells, 128 - PARAMS * j, 1) if j else cells
                table[pl.ds((n * blocks + b) * 64 + j * 8, 8), :] = moved
        return carry

    lax.fori_loop(0, ny * nz, expand, 0, unroll=4)

    k = iota((128, 128), 0)
    spread = jnp.concatenate(
        [jnp.where(((k & 15) == p) & (k < 48), 1.0, 0.0) for p in range(11)], axis=1
    ).astype(jnp.bfloat16)

    def far_domain(meta, n, carry):
        i = wrap(gx + nx + jnp.where((n & 1) == 1, (n + 1) >> 1, -(n >> 1)), nx)
        bounds = []
        slot = rows.at[n & 3]
        for t in range(8):
            at = i * 1024 + t * 128
            f0 = meta[at + LISTED + gx]
            bounds.append(meta[at + LISTED + gx + 1] - f0)
            for u in range(8):
                slot[t * 8 + u : t * 8 + u + 1, :] = table[pl.ds(meta[at + f0 + u], 1), :]
        high, mid, low = parts(slot[...])
        lane = iota((64, 128), 1)
        packed = jnp.where(
            lane < 16, high, jnp.where(lane < 32, pltpu.roll(mid, 16, 1), pltpu.roll(low, 32, 1))
        )
        wide = jnp.dot(packed.astype(jnp.bfloat16), spread, preferred_element_type=jnp.float32)
        values = []
        for t in range(8):
            tx, ty, tz = (t_all[i, c, t : t + 1, :] for c in range(3))
            p = lambda n: wide[t * 8 : t * 8 + 8, n * 128 : n * 128 + 128]
            values.append(far_value(p, bounds[t], tx, ty, tz))
        far_out[i] = -jnp.concatenate(values, axis=0)
        return carry

    for stage, span in enumerate(stages):
        for copy in listed:
            copy.wait()
        lax.fori_loop(
            span.start, span.stop, functools.partial(far_domain, metas[stage]), 0,
            unroll=min(4, max(1, len(span))),
        )
        if stage < 2:
            listed = arrived(stage + 1)
    for copy in o_copies:
        copy.wait()
    for copy in [*t_copy.values(), *m_copy.values(), *c_copies, *x_copies]:
        copy.wait_send()
    mine.wait()


def parts(v):
    high = v.astype(jnp.bfloat16).astype(jnp.float32)
    rest = v - high
    mid = rest.astype(jnp.bfloat16).astype(jnp.float32)
    return high, mid, rest - mid


def near_row(tile, x, y, z):
    sub = iota((8, 128), 0)
    left = jnp.concatenate([*parts(tile), jnp.where(sub < 3, 1.0, tile)], axis=0).T
    picks = []
    for c, row in enumerate((x, y, z)):
        high, mid, low = parts(jnp.broadcast_to(-row, (8, 128)))
        target = jnp.where(sub == 0, high, jnp.where(sub == 1, mid, jnp.where(sub == 2, low, 0.0)))
        for h in range(2):
            one = jnp.where(sub == h * 4 + c, 1.0, 0.0)
            picks.append(jnp.concatenate([one, one, one, target], axis=0))
    right = jnp.concatenate(picks, axis=1).astype(jnp.bfloat16)
    d = jnp.dot(left.astype(jnp.bfloat16), right, preferred_element_type=jnp.float32)
    total = jnp.zeros((8, 128), jnp.float32)
    for h in range(2):
        for s in range(0, 128, 8):
            dx, dy, dz = (
                d[s : s + 8, (2 * c + h) * 128 : (2 * c + h + 1) * 128] for c in range(3)
            )
            inv = lax.rsqrt(dx * dx + dy * dy + dz * dz + SOFT)
            total += inv * jnp.broadcast_to(left[s : s + 8, 27 + 4 * h : 28 + 4 * h], (8, 128))
    return jnp.sum(total, axis=0, keepdims=True)


def far_value(p, live, tx, ty, tz):
    dx, dy, dz = tx - p(1), ty - p(2), tz - p(3)
    r2 = dx * dx + dy * dy + dz * dz + SOFT
    inv = lax.rsqrt(r2)
    inv2 = inv * inv
    quad = dx * (p(4) * dx + p(7) * dy + p(8) * dz) + dy * (p(5) * dy + p(9) * dz) + p(6) * dz * dz
    value = inv * (p(0) + (quad - r2 * p(10)) * (inv2 * inv2))
    return jnp.sum(jnp.where(iota((8, 128), 0) < live, value, 0.0), axis=0, keepdims=True)


def walk_kernel(
    sizes, meta_in, cnt_in, lists_in, t_all, tiles, table, src,
    out, todo, rows, meta_a, meta_b, meta_c, meta_d, cnt, lists, in_sems,
):
    nx, ny, nz = sizes
    a = lax.axis_index("gx")
    gz = lax.axis_index("gz")
    near_base = LISTED + nx + 1
    metas = (meta_a, meta_b, meta_c, meta_d)
    each = meta_a.shape[0] // 1024
    copies = [pltpu.make_async_copy(cnt_in, cnt, in_sems.at[4])]
    for q in range(nx // each):
        part = meta_in.at[pl.ds(q * each * 1024, each * 1024)]
        copies.append(pltpu.make_async_copy(part, metas[q], in_sems.at[q]))
    copies.append(pltpu.make_async_copy(lists_in, lists, in_sems.at[5]))
    for copy in copies:
        copy.start()
    out[...] = jnp.zeros_like(out)

    def domain(meta, q, i, found):
        base = (i - q * each) * 1024
        n0 = meta[base + near_base + a]
        n1 = meta[base + near_base + a + 1]

        def bucket(t, carry):
            at = base + t * 128
            f0 = meta[at + LISTED + a]
            f1 = meta[at + LISTED + a + 1]
            tx, ty, tz = (t_all[i, c, pl.ds(t, 1), :] for c in range(3))

            def chunk(n, carry):
                start = f0 + n * 8
                for u in range(8):
                    rows[u : u + 1, :] = table[pl.ds(meta[at + start + u], 1), :]
                v = rows[...]
                p = lambda n: jnp.broadcast_to(v[:, n : n + 1], (8, 128))
                out[i, pl.ds(t, 1), :] -= far_value(p, f1 - start, tx, ty, tz)
                return carry

            return lax.fori_loop(1, (f1 - f0 + 7) >> 3, chunk, carry)

        longer = meta[base + LISTED + 2 * nx + 3 + a]

        @pl.when(longer >= 8)
        def _():
            alone = longer < 16
            begin = jnp.where(alone, longer & 7, 0)
            lax.fori_loop(begin, jnp.where(alone, begin + 1, 8), bucket, 0)

        def entry(e, found):
            code = meta[base + ((e >> 3) << 7) + FAR + (e & 7)]
            peer, slot = (code & 127) >> 1, code & 1
            todo[found] = (i * 8 + (code >> 7)) * 1024 + peer * (nx * 2) + i * 2 + slot
            return found + jnp.where(cnt[peer * (nx * nz) + i * nz + gz] > slot, 1, 0)

        return lax.fori_loop(n0, n1, entry, found)

    copies[0].wait()
    found = jnp.int32(0)
    for q in range(nx // each):
        copies[q + 1].wait()
        step = functools.partial(domain, metas[q], q)
        found = lax.fori_loop(q * each, (q + 1) * each, step, found)
    copies[-1].wait()
    todo[nx * 64 + 1] = found

    def away(n, carry):
        item = todo[n]
        i, t = item >> 13, (item >> 10) & 7
        row = near_row(tiles[item & 1023], *(t_all[i, c, pl.ds(t, 1), :] for c in range(3)))
        out[i, pl.ds(t, 1), :] -= row
        return carry

    lax.fori_loop(AWAY, found, away, 0)

    def own_entry(e, carry):
        code = lists[((e >> 3) << 7) + FAR + (e & 7)]
        t = code >> 7
        row = near_row(src[code & 127], *(t_all[a, c, pl.ds(t, 1), :] for c in range(3)))
        out[a, pl.ds(t, 1), :] -= row
        return carry

    lax.fori_loop(lists[near_base + nx] + OWN, lists[near_base + nx + 1], own_entry, 0)


def return_kernel(
    sizes, todo_in, lists_in, t_all, tiles, part, far_part, src,
    out, landed, near_rows, mine, todo, lists, send, recv, in_sems,
):
    nx, ny, nz = sizes
    gx, gy, gz = (lax.axis_index(n) for n in ALL)
    barrier = pltpu.get_barrier_semaphore()
    xs = [wrap(gx + d, nx) for d in range(nx)]
    far_first = sorted(range(1, nx), key=lambda d: -min(d, nx - d))
    for d in far_first:
        pl.semaphore_signal(barrier, inc=1, device_id=(xs[d], gy, gz), device_id_type=MESH)
    lane = iota((8, 128), 1)
    todo_copy = pltpu.make_async_copy(todo_in, todo, in_sems.at[0])
    lists_copy = pltpu.make_async_copy(lists_in, lists, in_sems.at[1])
    todo_copy.start()
    lists_copy.start()
    todo_copy.wait()
    lists_copy.wait()
    found = todo[nx * 64 + 1]

    def near(j, ids):
        item = jnp.where(j < found, todo[j], 0)
        bucket = item >> 10
        i, t = bucket >> 3, bucket & 7
        row = near_row(tiles[item & 1023], *(t_all[i, c, pl.ds(t, 1), :] for c in range(3)))
        near_rows[pl.ds(j, 1), :] = row
        return jnp.where(lane == j, jnp.where(j < found, bucket, -1), ids)

    near_rows[...] = jnp.zeros_like(near_rows)
    ids = lax.fori_loop(0, AWAY, near, jnp.full((8, 128), -1, jnp.int32), unroll=4)
    pick = jnp.where(iota((nx * 8, 128), 0) == jnp.broadcast_to(ids[0:1], (nx * 8, 128)), 1.0, 0.0)
    placed = sum(
        jnp.dot(pick.astype(jnp.bfloat16), v.astype(jnp.bfloat16), preferred_element_type=jnp.float32)
        for v in parts(near_rows[...])
    )
    mine[...] = part[...] + far_part[...] - placed.reshape(nx, 8, 128)

    pl.semaphore_wait(barrier, nx - 1)
    copies = []
    for d in far_first:
        copy = pltpu.make_async_remote_copy(
            src_ref=mine.at[xs[d]], dst_ref=landed.at[d - 1],
            send_sem=send.at[d], recv_sem=recv.at[d],
            device_id=(xs[d], gy, gz), device_id_type=MESH,
        )
        copy.start()
        copies.append(copy)

    n0 = lists[LISTED + nx + 1 + nx]
    n1 = lists[LISTED + nx + 1 + nx + 1]
    sub = iota((8, 128), 0)

    def own_item(j, total):
        e = n0 + j
        p = jnp.minimum(e, 8 * NEAR - 1)
        code = lists[((p >> 3) << 7) + FAR + (p & 7)]
        t = code >> 7
        tile = src[code & 127]
        row = near_row(tile, *(t_all[gx, c, pl.ds(t, 1), :] for c in range(3)))
        return total - jnp.where((sub == t) & (e < n1), row, 0.0)

    summed = lax.fori_loop(0, OWN, own_item, mine[gx], unroll=4)
    for copy in copies:
        copy.wait()
    for d in range(nx - 1):
        summed += landed[d]
    out[...] = summed


def body(sizes, targets, sources, send_ids, send_count, far_ids, near_ids, near_count):
    nx, ny, nz = sizes
    f32, i32 = jnp.float32, jnp.int32
    own = sources.shape[0]
    shape = jax.ShapeDtypeStruct
    vmem = pl.BlockSpec(memory_space=VMEM)
    smem = pl.BlockSpec(memory_space=SMEM)
    hbm = pl.BlockSpec(memory_space=pltpu.HBM)
    dma = pltpu.SemaphoreType.DMA
    in_hbm = functools.partial(pltpu.with_memory_space_constraint, memory_space=pltpu.HBM)
    tgt = jnp.transpose(targets.reshape(3, 8, 128), (1, 0, 2))
    src = jnp.transpose(sources.reshape(own, 4, 2, 128), (0, 2, 1, 3)).reshape(own, 8, 128)
    t_all, meta, tiles_all, cnt, table, far_part, lists, held = pl.pallas_call(
        functools.partial(gather_kernel, sizes),
        out_shape=(
            shape((nx, 3, 8, 128), f32), shape((nx * 1024,), i32),
            shape((nz, nx * 2, 8, 128), f32), shape((nz, 1, nx * nz), i32),
            shape((ny * nz * own, 128), f32),
            shape((nx, 8, 128), f32), shape((1024,), i32), shape((own, 8, 128), f32),
        ),
        in_specs=[hbm] * 7,
        out_specs=(vmem,) * 8,
        scratch_shapes=[
            SMEM((2, nx * nz), i32), SMEM((1, nx * nz), i32), VMEM((1, nx * nz), i32),
            SMEM((8,), i32),
            VMEM((8, FAR), i32), VMEM((8, NEAR), i32), VMEM((8, 3, 128), f32),
            VMEM((8, 128), i32), VMEM((3, 8, 128), f32),
            VMEM((nz, nx * 2, 8, 128), f32), VMEM((own // 8, 128), f32),
            VMEM((ny, nz, own // 8, 128), f32), VMEM((4, 64, 128), f32),
            SMEM((nx * 1024,), i32), SMEM((nx * 1024,), i32), SMEM((nx * 1024,), i32),
            dma((nx,)), dma((nx,)), dma((nx,)), dma((nx,)), dma((nz,)), dma((nz,)),
            dma((nz,)), dma((nz,)), dma((ny,)), dma((ny,)), dma((nz,)), dma((nz,)),
            dma, dma((nx,)), dma((8,)),
        ],
        compiler_params=pltpu.CompilerParams(
            collective_id=0, has_side_effects=True, vmem_limit_bytes=LIMIT
        ),
        name="gather",
    )(*map(in_hbm, (send_ids[0].T, send_count, near_count, far_ids, near_ids, tgt, src)))

    tiles = tiles_all.reshape(nz * nx * 2, 8, 128)
    part, todo = pl.pallas_call(
        functools.partial(walk_kernel, sizes),
        out_shape=(shape((nx, 8, 128), f32), shape((nx * 64 + 2,), i32)),
        in_specs=[vmem] * 7,
        out_specs=(vmem, smem),
        scratch_shapes=[
            VMEM((8, 128), f32), *[SMEM((max(1, nx // 4) * 1024,), i32)] * 4,
            SMEM((nz * nx * nz,), i32), SMEM((1024,), i32), dma((6,)),
        ],
        compiler_params=pltpu.CompilerParams(vmem_limit_bytes=LIMIT),
        name="walk",
    )(meta, cnt.reshape(-1), lists, t_all, tiles, table, held)

    out = pl.pallas_call(
        functools.partial(return_kernel, sizes),
        out_shape=shape((8, 128), f32),
        in_specs=[vmem] * 7,
        out_specs=vmem,
        scratch_shapes=[
            VMEM((nx - 1, 8, 128), f32), VMEM((128, 128), f32),
            VMEM((nx, 8, 128), f32), SMEM((nx * 64 + 2,), i32), SMEM((1024,), i32),
            dma((nx,)), dma((nx,)), dma((2,)),
        ],
        compiler_params=pltpu.CompilerParams(
            collective_id=1, has_side_effects=True, vmem_limit_bytes=LIMIT
        ),
        name="bring_back",
    )(todo, lists, t_all, tiles, part, far_part, held)
    return out.reshape(-1)


def solution(mesh):
    sizes = tuple(mesh.shape[n] for n in ALL)
    in_specs = (
        P(None, ALL), P(ALL, None, None), P(ALL, None, None), P(ALL, None),
        P(ALL, None), P(ALL, None), P(ALL),
    )
    return jax.shard_map(
        functools.partial(body, sizes), mesh=mesh, in_specs=in_specs, out_specs=P(ALL),
        check_vma=False,
    )
```
